32 devices in a mesh: groups: 1, tok: 32 (over z, y, x, core).
Axes of the slice: x: 2, y: 2, z: 4, core: 2. Of those that a mesh axis runs over, the one named last changes fastest.
Arguments:
- queries: bfloat16 [4096, 2560], P(('groups', 'tok')), may hold values from -5 to 5
- key_rows: bfloat16 [4096, 2560], P(('groups', 'tok')), may hold values from -5 to 5
- value_rows: bfloat16 [4096, 2560], P(('groups', 'tok')), may hold values from -6 to 6
- learn_rates: float32 [4096, 8], P(('groups', 'tok')), may hold values from 0.0002 to 0.002
- frame_order: int32 [4096], P('groups'), may hold values from 0 to 4095, as said below
- window_ids: int32 [4096], P('groups'), may hold values from 0 to 7, never falling along the last dimension, each value on 1 to 2048 neighbouring positions
- fast_init: bfloat16 [640, 3, 2560], replicated, may hold values from -0.3125 to 0.3125
- norm_gain: float32 [2560], replicated, may hold values from 0.5 to 1.5
Outputs:
- layer_out: bfloat16 [4096, 2560], P(('groups', 'tok'))
The draws below stay inside these ranges and needn't reach their ends.
Inputs may be any that keep to these rules, and one draw needn't show every extreme that they name: frame_order[i] is the sequence position of the token stored at row i; every position appears once, and every aligned block of 128 stored rows holds exactly 4 positions of every aligned block of 128 positions.
All inputs are finite; a program needn't handle non-finite values.
Results may differ from the reference program's by a relative error of at most 0.025.
Values may be sent and summed in bfloat16 or wider, within the bound.
No kernel may reach another device: no remote copies, remote signals or barrier semaphores. Data moves between devices by JAX's collectives and lax.ppermute only.
A program may use at most 192 MiB of HBM per device.

```python
import math
import jax
import jax.numpy as jnp
import numpy as np
from jax import lax

HEADS = 8
HEAD_DIM = 320
FAST_HID = 640
ATT_DIM = 128
WINDOW = 1024
TOK_DEV = 128
WIDTH = 2560
ATT_HEADS = 20
TOKENS = 4096
SLOTS = 4


def shuffled(sub_key):
    return jax.random.permutation(sub_key, TOK_DEV)


def make_order(key):
    base = jax.random.fold_in(key, 101)
    sources = TOKENS // TOK_DEV
    send_slots = jax.vmap(shuffled)(jax.random.split(jax.random.fold_in(base, 1), sources))
    recv_slots = jax.vmap(shuffled)(jax.random.split(jax.random.fold_in(base, 2), sources))
    source = jnp.arange(sources, dtype=jnp.int32)[:, None]
    target = send_slots // SLOTS
    within = send_slots % SLOTS
    landing = recv_slots[target, source * SLOTS + within]
    return (target * TOK_DEV + landing).reshape(-1).astype(jnp.int32)


def sequence_rows(key, salt):
    noise_key = jax.random.fold_in(key, salt)
    return jnp.clip(jax.random.normal(noise_key, (TOKENS, WIDTH), jnp.float32), -5.0, 5.0)


def draw_frame_order(key, part):
    return make_order(key)


def draw_queries(key, part):
    rows = sequence_rows(key, 202)
    return rows[make_order(key)].astype(jnp.bfloat16)


def draw_key_rows(key, part):
    rows = sequence_rows(key, 404)
    return rows[make_order(key)].astype(jnp.bfloat16)


def steps_of(own_key, dims, cuts, least, largest):
    level, own = 1.0, jax.random.fold_in(own_key, 6)
    for position, blocks in cuts:
        steps = jnp.exp(jax.random.uniform(jax.random.fold_in(own, position), (blocks,), jnp.float32, least / len(cuts), largest / len(cuts)))
        level = level * jnp.repeat(steps, dims[position] // blocks).reshape([-1 if axis == position else 1 for axis in range(len(dims))])
    return level


def split_up(count, total, bound, slope):
    loads = [(1 << 20) // math.isqrt(rank ** slope) + 1 for rank in range(2, count + 1)]
    surplus, given = total - bound - (count - 1), [1] * (count - 1)
    while surplus > 0:
        movable = [i for i in range(count - 1) if given[i] < bound]
        pool, left = sum([loads[i] for i in movable]), surplus
        for i in movable:
            more = min(bound - given[i], max(1, left * loads[i] // pool), surplus)
            given[i] = given[i] + more
            surplus = surplus - more
    return np.array([bound] + given)


def ragged_sizes(stream_key, count, total, most, slope):
    if count == 2:
        one = jax.random.randint(stream_key, (), max(1, total - most), min(most, total - 1) + 1)
        return jnp.stack([one, total - one])
    sizes = jnp.asarray(split_up(count, total, most, slope), jnp.int32)
    twos = (count - 1) // 2
    giver, receiver = sizes[1:1 + 2 * twos:2], sizes[2:2 + 2 * twos:2]
    slack = jnp.minimum(giver - 1, most - receiver)
    passed = jax.random.randint(jax.random.fold_in(stream_key, 1), (twos,), 0, 1 << 20) % (slack + 1)
    sizes = sizes.at[1:1 + 2 * twos:2].set(giver - passed).at[2:2 + 2 * twos:2].set(receiver + passed)
    return sizes[jax.random.permutation(jax.random.fold_in(stream_key, 2), count)]


def normal_values(stream_key, dims, width, bound, pieces=(), kind=jnp.bfloat16):
    values = width * jax.random.normal(stream_key, dims, jnp.float32)
    if pieces:
        values = values * steps_of(stream_key, dims, pieces, -0.22, 0.18)
    return jnp.clip(values, -bound, bound).astype(kind)


def setup_inputs(seed: int = 0, part: int = 0) -> dict:
    splits = jax.random.split(jax.random.key(seed), 9)
    part_keys = jax.random.split(jax.random.fold_in(splits[8], part), 9)
    queries = draw_queries(jax.random.fold_in(jax.random.fold_in(splits[8], part), 71), part)
    key_rows = draw_key_rows(jax.random.fold_in(jax.random.fold_in(splits[8], part), 71), part)
    value_rows = normal_values(part_keys[2], (TOKENS, WIDTH), 1.0, 6.0, ((0, 32),))
    learn_rates = jnp.clip(jnp.exp(math.log(0.002) - 2.3025852 * jax.random.uniform(part_keys[3], (TOKENS, HEADS), jnp.float32) ** steps_of(part_keys[3], (TOKENS, HEADS), ((0, 32),), -0.2, 0.2)), 0.0002, 0.002)
    frame_order = draw_frame_order(jax.random.fold_in(jax.random.fold_in(splits[8], part), 71), part)
    window_ids = jnp.searchsorted(jnp.cumsum(ragged_sizes(part_keys[5], TOKENS // (WINDOW // 2), TOKENS, 2 * WINDOW, 1)), jnp.arange(TOKENS), side="right").astype(jnp.int32)
    fast_init = normal_values(splits[6], (FAST_HID, 3, WIDTH), HEAD_DIM ** -0.5, 0.3125)
    norm_gain = jnp.clip(1.0 + 0.1 * jax.random.normal(splits[7], (WIDTH,), jnp.float32), 0.5, 1.5)
    return {"queries": queries, "key_rows": key_rows, "value_rows": value_rows, "learn_rates": learn_rates, "frame_order": frame_order, "window_ids": window_ids, "fast_init": fast_init, "norm_gain": norm_gain}


epsilon = 1e-06

def rounded(values):
    return lax.optimization_barrier(values.astype(jnp.bfloat16)).astype(jnp.float32)

def head_view(rows):
    return rows.astype(jnp.float32).reshape(rows.shape[0], HEADS, HEAD_DIM)

def matrix_view(weight_rows, which):
    return weight_rows[:, which].astype(jnp.float32).reshape(weight_rows.shape[0], HEADS, HEAD_DIM)

def fast_grads(key_block, value_block, rate_block, weight_rows):
    row_count = weight_rows.shape[0]
    key_heads = head_view(key_block)
    target = rounded(head_view(value_block) * rate_block.astype(jnp.float32)[:, :, None])
    gate = jnp.einsum('thd,jhd->thj', key_heads, matrix_view(weight_rows, 0))
    upward = jnp.einsum('thd,jhd->thj', key_heads, matrix_view(weight_rows, 1))
    backward = jnp.einsum('thd,jhd->thj', target, matrix_view(weight_rows, 2))
    sigmoid = jax.nn.sigmoid(gate)
    active = gate * sigmoid
    product = rounded(active * upward)
    delta_gate = rounded(backward * upward * sigmoid * (1.0 + gate * (1.0 - sigmoid)))
    delta_upper = rounded(backward * active)
    grad_gate = jnp.einsum('thj,thd->jhd', delta_gate, key_heads)
    grad_upper = jnp.einsum('thj,thd->jhd', delta_upper, key_heads)
    grad_down = jnp.einsum('thj,thd->jhd', product, target)
    return jnp.stack([grad_gate.reshape(row_count, WIDTH), grad_upper.reshape(row_count, WIDTH), grad_down.reshape(row_count, WIDTH)], axis=1)

def renormed(base_rows, grads):
    start_rows = base_rows.astype(jnp.float32)
    update = start_rows + grads
    shaped = update.reshape(update.shape[0], 3, HEADS, HEAD_DIM)
    anchor = start_rows.reshape(update.shape[0], 3, HEADS, HEAD_DIM)
    scaling = jnp.sqrt(lax.optimization_barrier(jnp.sum(anchor * anchor, axis=-1, keepdims=True)) + epsilon) / jnp.sqrt(lax.optimization_barrier(jnp.sum(shaped * shaped, axis=-1, keepdims=True)) + epsilon)
    return (shaped * scaling).reshape(update.shape).astype(jnp.bfloat16)

def fast_apply(query_block, weight_rows):
    query_heads = head_view(query_block)
    gate = jnp.einsum('thd,jhd->thj', query_heads, matrix_view(weight_rows, 0))
    upward = jnp.einsum('thd,jhd->thj', query_heads, matrix_view(weight_rows, 1))
    product = rounded(jax.nn.silu(gate) * upward)
    result = jnp.einsum('thj,jhd->thd', product, matrix_view(weight_rows, 2))
    return result.reshape(query_block.shape[0], WIDTH)

def reference(queries, key_rows, value_rows, learn_rates, frame_order, window_ids, fast_init, norm_gain):
    block_count = TOKENS // TOK_DEV
    indices = jnp.arange(block_count, dtype=jnp.int32)

    def accumulate(total, index):
        begin = index * TOK_DEV
        partial_value = fast_grads(lax.dynamic_slice_in_dim(key_rows, begin, TOK_DEV, 0), lax.dynamic_slice_in_dim(value_rows, begin, TOK_DEV, 0), lax.dynamic_slice_in_dim(learn_rates, begin, TOK_DEV, 0), fast_init)
        return (total + rounded(partial_value), jnp.zeros((), jnp.float32))
    grads = lax.scan(accumulate, jnp.zeros((FAST_HID, 3, WIDTH), jnp.float32), indices)[0]
    fresh = renormed(fast_init, grads)
    query_seq = jnp.zeros_like(queries).at[frame_order].set(queries)
    key_seq = jnp.zeros_like(key_rows).at[frame_order].set(key_rows)
    value_seq = jnp.zeros_like(value_rows).at[frame_order].set(value_rows)

    def apply_block(index):
        return fast_apply(lax.dynamic_slice_in_dim(query_seq, index * TOK_DEV, TOK_DEV, 0), fresh)
    fast_out = lax.map(apply_block, indices).reshape(TOKENS, WIDTH)
    half_span = WINDOW // 2
    span = TOK_DEV + 2 * half_span
    key_pad = jnp.pad(key_seq, ((half_span, half_span), (0, 0)))
    value_pad = jnp.pad(value_seq, ((half_span, half_span), (0, 0)))
    ids_pad = jnp.pad(window_ids, (half_span, half_span), constant_values=-1)

    def attend(index):
        begin = index * TOK_DEV
        query_block = lax.dynamic_slice_in_dim(query_seq, begin, TOK_DEV, 0).astype(jnp.float32).reshape(TOK_DEV, ATT_HEADS, ATT_DIM)
        key_block = lax.dynamic_slice_in_dim(key_pad, begin, span, 0).astype(jnp.float32).reshape(span, ATT_HEADS, ATT_DIM)
        value_block = lax.dynamic_slice_in_dim(value_pad, begin, span, 0).astype(jnp.float32).reshape(span, ATT_HEADS, ATT_DIM)
        query_ids = lax.dynamic_slice_in_dim(window_ids, begin, TOK_DEV, 0)
        key_ids = lax.dynamic_slice_in_dim(ids_pad, begin, span, 0)
        query_pos = begin + jnp.arange(TOK_DEV, dtype=jnp.int32)
        key_pos = begin - half_span + jnp.arange(span, dtype=jnp.int32)
        allowed = (key_pos[None, :] >= 0) & (key_pos[None, :] < TOKENS) & (jnp.abs(query_pos[:, None] - key_pos[None, :]) < half_span) & (query_ids[:, None] == key_ids[None, :])
        scores = jnp.einsum('tad,sad->ats', query_block, key_block) * ATT_DIM ** (-0.5)
        scores = jnp.where(allowed[None], scores, -1e+30)
        peak = lax.optimization_barrier(jnp.max(scores, axis=2, keepdims=True))
        weights = jnp.exp(scores - peak)
        total = lax.optimization_barrier(jnp.sum(weights, axis=2, keepdims=True))
        mixed = jnp.einsum('ats,sad->tad', rounded(weights), value_block)
        return (mixed / jnp.transpose(total, (1, 0, 2))).reshape(TOK_DEV, WIDTH)
    attended = lax.map(attend, indices).reshape(TOKENS, WIDTH)
    combined = fast_out + attended
    mean_square = lax.optimization_barrier(jnp.mean(combined * combined, axis=1, keepdims=True))
    return (combined * lax.rsqrt(mean_square + epsilon) * norm_gain).astype(jnp.bfloat16)
```

```python
import functools
import math

import jax
import jax.numpy as jnp
from jax import lax
from jax.experimental import pallas as pl
from jax.experimental.pallas import tpu as pltpu
from jax.sharding import PartitionSpec as P

HEADS = 8
HEAD_DIM = 320
ATT_DIM = 128
WINDOW = 1024
WIDTH = 2560
ATT_HEADS = 20
LANES = 128
EPS = 1e-06

PARTS = math.gcd(HEADS, ATT_HEADS)
PART_WIDTH = WIDTH // PARTS
PART_FAST = HEADS // PARTS
PART_ATT = ATT_HEADS // PARTS
SPAN = -(-HEAD_DIM // LANES) * LANES


F32 = jnp.float32
BF16 = jnp.bfloat16
VMEM = pltpu.VMEM


def iota(shape, dim):
    return lax.broadcasted_iota(jnp.int32, shape, dim)


def dot(a, b, dims=((1,), (0,))):
    return lax.dot_general(a, b, (dims, ((), ())), preferred_element_type=F32)


def column_of(row):
    n = row.shape[1]
    square = jnp.broadcast_to(row.astype(F32), (n, n))
    diagonal = iota((n, n), 0) == iota((n, n), 1)
    return jnp.sum(jnp.where(diagonal, square, 0.0), axis=1, keepdims=True)


def call(kernel, outs, ins, scratch=(), smem=0, flops=0, name=None, grid=None, in_specs=None, out_specs=None):
    specs = [pl.BlockSpec(memory_space=pltpu.SMEM)] * smem
    specs += in_specs or [pl.BlockSpec(memory_space=VMEM)] * (len(ins) - smem)
    moved = sum(x.size * x.dtype.itemsize for x in list(ins) + list(outs))
    extra = {} if grid is None else {"grid": grid}
    return pl.pallas_call(
        kernel,
        out_shape=list(outs),
        in_specs=specs,
        out_specs=out_specs or [pl.BlockSpec(memory_space=VMEM)] * len(outs),
        scratch_shapes=list(scratch),
        compiler_params=pltpu.CompilerParams(vmem_limit_bytes=48 << 20),
        cost_estimate=pl.CostEstimate(flops=flops, bytes_accessed=moved, transcendentals=0),
        name=name,
        **extra,
    )(*ins)


def pack_kernel(group_shift, low_shift, slots, place_ref, order_ref, query_ref, key_ref, value_ref, rate_ref, kv_ref, q_ref):
    n = query_ref.shape[0]
    planes, _, cores = kv_ref.shape[:3]
    pos = order_ref[pl.ds(place_ref[0], 1), :]
    pos_col = column_of(pos).astype(jnp.int32)
    group = lax.shift_right_logical(pos, group_shift)
    group_col = lax.shift_right_logical(pos_col, group_shift)
    earlier = (group_col == group) & (iota((n, n), 0) < iota((n, n), 1))
    rank = jnp.sum(jnp.where(earlier, 1.0, 0.0), axis=0, keepdims=True)
    slot = group * slots + rank.astype(jnp.int32)
    choose = jnp.where(iota((n, n), 0) == slot, 1.0, 0.0).astype(BF16)
    rates = rate_ref[...]
    heads = rates.shape[1]
    extra = jnp.zeros((n, LANES), F32)
    for part in range(3):
        piece = rates.astype(BF16)
        rates = rates - piece.astype(F32)
        put = iota((heads, LANES), 1) == iota((heads, LANES), 0) + part * heads
        extra += dot(piece, jnp.where(put, 1.0, 0.0).astype(BF16))
    within = pos_col & ((1 << group_shift) - 1)
    high = lax.shift_right_logical(within, low_shift).astype(F32)
    low = (within & ((1 << low_shift) - 1)).astype(F32)
    lane = iota((n, LANES), 1)
    extra += jnp.where(lane == 3 * heads, high, 0.0) + jnp.where(lane == 3 * heads + 1, low, 0.0)
    extra = dot(choose, extra.astype(BF16)).astype(BF16)

    def put_rows(ref, rows, part, begin):
        width = rows.shape[1]
        for plane in range(planes):
            for core in range(cores):
                at = (plane * cores + core) * slots
                ref[plane, part, core, :, begin : begin + width] = rows[at : at + slots]

    for part in range(PARTS):
        lanes = slice(part * PART_WIDTH, (part + 1) * PART_WIDTH)
        put_rows(kv_ref, dot(choose, key_ref[:, lanes]).astype(BF16), part, 0)
        put_rows(kv_ref, dot(choose, value_ref[:, lanes]).astype(BF16), part, PART_WIDTH)
        put_rows(kv_ref, extra, part, 2 * PART_WIDTH)
        put_rows(q_ref, dot(choose, query_ref[:, lanes]).astype(BF16), part, 0)


def arrival_choice(extra, low_shift):
    n = extra.shape[0]
    pick = iota((8, LANES), 1) == iota((8, LANES), 0) + 3 * HEADS
    rows = dot(jnp.where(pick, 1.0, 0.0).astype(BF16), extra, ((1,), (1,)))
    pos = rows[0:1] * float(1 << low_shift) + rows[1:2]
    return jnp.where(iota((n, n), 0) == pos.astype(jnp.int32), 1.0, 0.0).astype(BF16)


def place_kernel(low_shift, kv_in_ref, kv_ref, choose_ref):
    choose = arrival_choice(kv_in_ref[:, 2 * PART_WIDTH :], low_shift)
    choose_ref[...] = choose
    for part in range(2):
        lanes = slice(part * PART_WIDTH, (part + 1) * PART_WIDTH)
        kv_ref[:, lanes] = dot(choose, kv_in_ref[:, lanes]).astype(BF16)


def window_of(head):
    begin = head * HEAD_DIM // LANES * LANES
    begin = min(begin, PART_WIDTH - SPAN)
    return begin, head * HEAD_DIM - begin


def head_mask(head):
    _, offset = window_of(head)
    lane = iota((1, SPAN), 1)
    return (lane >= offset) & (lane < offset + HEAD_DIM)


def grads_kernel(chunk, place_ref, kv_ref, weight_ref, mine_ref, other_ref, key_buf, target_buf, dg_buf, du_buf, pr_buf, sums):
    n = kv_ref.shape[0]
    hidden = weight_ref.shape[2]
    part, core = place_ref[1], place_ref[2]
    for head in range(PART_FAST):
        begin, offset = window_of(head)
        valid = head_mask(head)
        rows = pl.ds(begin, SPAN)
        for at in range(0, n, chunk):
            here = pl.ds(at, chunk)
            extra = kv_ref[here, 2 * PART_WIDTH :].astype(F32)
            lane = iota((1, LANES), 1)
            own = part * PART_FAST + head
            wanted = (lane == own) | (lane == HEADS + own) | (lane == 2 * HEADS + own)
            rate = jnp.sum(jnp.where(wanted, extra, 0.0), axis=1, keepdims=True)
            key = jnp.where(valid, kv_ref[here, begin : begin + SPAN], jnp.zeros((), BF16))
            value = kv_ref[here, PART_WIDTH + begin : PART_WIDTH + begin + SPAN].astype(F32)
            target = jnp.where(valid, value * rate, 0.0).astype(BF16)
            key_buf[here, :] = key
            target_buf[here, :] = target
            gate = dot(key, weight_ref[0, rows, :])
            upward = dot(key, weight_ref[1, rows, :])
            backward = dot(target, weight_ref[2, rows, :])
            sigmoid = jax.nn.sigmoid(gate)
            active = gate * sigmoid
            pr_buf[here, :] = (active * upward).astype(BF16)
            du_buf[here, :] = (backward * active).astype(BF16)
            dg_buf[here, :] = (backward * upward * sigmoid * (1.0 + gate * (1.0 - sigmoid))).astype(BF16)
        for index, (left, right) in enumerate(((key_buf, dg_buf), (key_buf, du_buf), (target_buf, pr_buf))):
            total = dot(left[...], right[...], ((0,), (0,)))
            sums[head, :, index * hidden : (index + 1) * hidden] = total[offset : offset + HEAD_DIM].astype(BF16)
    mine_ref[...] = sums[core]
    other_ref[...] = sums[1 - core]


def attention_kernel(block, place_ref, choose_ref, query_in_ref, ids_ref, key_ref, key_low_ref, key_high_ref, value_ref, value_low_ref, value_high_ref, out_ref, query_ref, bias):
    n = choose_ref.shape[0]
    half = WINDOW // 2
    group = place_ref[3]
    last = ids_ref.shape[0] - 1

    @pl.when(pl.program_id(0) == 0)
    def _():
        mid = ids_ref[pl.ds(group, 1), :]
        low = ids_ref[pl.ds(jnp.maximum(group - 1, 0), 1), :]
        high = ids_ref[pl.ds(jnp.minimum(group + 1, last), 1), :]
        low = jnp.where(group > 0, low, -1)
        high = jnp.where(group < last, high, -1)
        for at in range(0, n, block):
            own = column_of(mid[:, at : at + block]).astype(jnp.int32)
            ids = jnp.concatenate([low[:, at:], mid, high[:, : at + block]], axis=1)
            span = ids.shape[1]
            gap = iota((block, span), 1) - iota((block, span), 0) - half
            allowed = (gap < half) & (gap > -half) & (own == ids)
            bias[at // block, :, :] = jnp.where(allowed, 0.0, -1e30)

    query = dot(choose_ref[...], query_in_ref[...]).astype(BF16)
    query_ref[...] = query
    factor = ATT_DIM ** (-0.5) * math.log2(math.e)
    for at in range(0, n, block):
        part = query[at : at + block]
        stops = (0, half - at, half - at + n, half + n + block - half)
        keys = (key_low_ref[at:, :], key_ref[...], key_high_ref[: at + block, :])
        values = (value_low_ref[at:, :], value_ref[...], value_high_ref[: at + block, :])
        scores = []
        for index in range(3):
            lanes = slice(stops[index], stops[index] + keys[index].shape[0])
            scores.append(dot(part, keys[index], ((1,), (1,))) + bias[at // block, :, lanes])
        peak = functools.reduce(jnp.maximum, [jnp.max(s, axis=1, keepdims=True) for s in scores])
        total = jnp.zeros_like(peak)
        mixed = jnp.zeros((block, ATT_DIM), F32)
        for score, value in zip(scores, values):
            weight = jnp.exp2((score - peak) * factor)
            total += jnp.sum(weight, axis=1, keepdims=True)
            mixed += dot(weight.astype(BF16), value)
        out_ref[pl.ds(at, block), :] = mixed / total


def apply_kernel(chunk, place_ref, weight_ref, mine_ref, other_ref, query_ref, attended_ref, out_ref, fresh):
    n = query_ref.shape[0]
    hidden = weight_ref.shape[2]
    core = place_ref[2]
    for head in range(PART_FAST):
        begin, offset = window_of(head)
        start = head * HEAD_DIM
        for index in range(3):
            lanes = slice(index * hidden, (index + 1) * hidden)
            base = weight_ref[index, start : start + HEAD_DIM, :].astype(F32)
            grad = jnp.where(core == head, mine_ref[:, lanes], other_ref[:, lanes]).astype(F32)
            update = base + grad
            anchor = jnp.sum(base * base, axis=0, keepdims=True) + EPS
            length = jnp.sum(update * update, axis=0, keepdims=True) + EPS
            scale = jnp.sqrt(anchor) / jnp.sqrt(length)
            if offset:
                fresh[head, index, :offset, :] = jnp.zeros((offset, hidden), BF16)
            if offset + HEAD_DIM < SPAN:
                fresh[head, index, offset + HEAD_DIM :, :] = jnp.zeros((SPAN - offset - HEAD_DIM, hidden), BF16)
            fresh[head, index, offset : offset + HEAD_DIM, :] = (update * scale).astype(BF16)
    for at in range(0, n, chunk):
        here = pl.ds(at, chunk)
        parts = []
        for head in range(PART_FAST):
            begin, offset = window_of(head)
            query = query_ref[here, begin : begin + SPAN]
            gate = dot(query, fresh[head, 0])
            upward = dot(query, fresh[head, 1])
            product = (gate * jax.nn.sigmoid(gate) * upward).astype(BF16)
            parts.append((begin, dot(product, fresh[head, 2], ((1,), (1,)))))
        for lane in range(0, PART_WIDTH, LANES):
            total = attended_ref[here, lane : lane + LANES]
            for begin, value in parts:
                if begin <= lane < begin + SPAN:
                    total += value[:, lane - begin : lane - begin + LANES]
            out_ref[here, lane : lane + LANES] = total.astype(BF16)


def norm_kernel(place_ref, *refs):
    part_refs, gain_ref, out_ref, buf = refs[:PARTS], refs[PARTS], refs[PARTS + 1], refs[PARTS + 2]
    square = jnp.zeros((out_ref.shape[0], 1), F32)
    for index, ref in enumerate(part_refs):
        rows = ref[...]
        buf[place_ref[4 + index]] = rows
        wide = rows.astype(F32)
        square += jnp.sum(wide * wide, axis=1, keepdims=True)
    factor = lax.rsqrt(square / WIDTH + EPS)
    for part in range(PARTS):
        lanes = slice(part * PART_WIDTH, (part + 1) * PART_WIDTH)
        out_ref[:, lanes] = (buf[part].astype(F32) * factor * gain_ref[:, lanes]).astype(BF16)


def shards(queries, key_rows, value_rows, learn_rates, frame_order, window_ids, fast_init, norm_gain):
    tok_dev = queries.shape[0]
    hidden = fast_init.shape[0]
    sections = lax.axis_size("tok")
    plane_size = PARTS * PART_FAST
    planes = sections // plane_size
    group_rows = tok_dev * PARTS
    groups = planes * PART_FAST
    slots = tok_dev // groups
    half = WINDOW // 2
    assert PART_FAST == 2 and half == group_rows and group_rows & (group_rows - 1) == 0
    group_shift = group_rows.bit_length() - 1
    low_shift = group_shift // 2

    rank = lax.axis_index("tok")
    plane = rank // plane_size
    part = rank // PART_FAST % PARTS
    core = rank % PART_FAST
    row, column = part // 2, part % 2
    group = plane * PART_FAST + core

    def at(plane, row, column, core):
        return plane * plane_size + (row * 2 + column) * PART_FAST + core

    everyone = [(z, y, x, c) for z in range(planes) for y in range(2) for x in range(2) for c in range(2)]

    def permute(array, target):
        route = []
        for source in everyone:
            goal = target(*source)
            if goal is not None:
                route.append((at(*source), at(*goal)))
        return lax.ppermute(array, "tok", route)

    sources = [2 * (core ^ j // 2) + (column ^ j % 2) for j in range(PARTS)]
    place = jnp.stack([rank, part, core, group] + sources).astype(jnp.int32)

    def weight_part():
        own = lax.dynamic_slice_in_dim(fast_init, part * PART_WIDTH, PART_WIDTH, 2)
        return jnp.transpose(own, (1, 2, 0))

    weights = weight_part()

    kv_width = 2 * PART_WIDTH + LANES
    shape = (planes, PARTS, PART_FAST, slots)
    kv_out, q_out = call(
        functools.partial(pack_kernel, group_shift, low_shift, slots),
        [jax.ShapeDtypeStruct(shape + (kv_width,), BF16), jax.ShapeDtypeStruct(shape + (PART_WIDTH,), BF16)],
        [place, frame_order.reshape(sections, tok_dev), queries, key_rows, value_rows, learn_rates],
        smem=1, flops=2 * tok_dev * tok_dev * 3 * WIDTH, name="pack",
    )

    def exchange(array):
        flat = array.reshape(sections, slots, array.shape[-1])
        return lax.all_to_all(flat, "tok", split_axis=0, concat_axis=0, tiled=True).reshape(group_rows, array.shape[-1])

    kv_in = exchange(kv_out)
    q_in = exchange(q_out)

    kv_seq, choose = call(
        functools.partial(place_kernel, low_shift),
        [jax.ShapeDtypeStruct((group_rows, 2 * PART_WIDTH), BF16), jax.ShapeDtypeStruct((group_rows, group_rows), BF16)],
        [kv_in], flops=2 * group_rows * group_rows * 2 * PART_WIDTH, name="place",
    )

    def neighbour(step):
        def target(z, y, x, c):
            goal = z * PART_FAST + c + step
            return (goal // PART_FAST, y, x, goal % PART_FAST) if 0 <= goal < groups else None
        return target

    kv_low = permute(kv_seq, neighbour(1))
    kv_high = permute(kv_seq, neighbour(-1))

    grad_shape = jax.ShapeDtypeStruct((HEAD_DIM, 3 * hidden), BF16)
    mine, other = call(
        functools.partial(grads_kernel, tok_dev),
        [grad_shape, grad_shape], [place, kv_in, weights],
        scratch=[VMEM((group_rows, SPAN), BF16)] * 2 + [VMEM((group_rows, hidden), BF16)] * 3
        + [VMEM((PART_FAST, HEAD_DIM, 3 * hidden), BF16)],
        smem=1, flops=12 * group_rows * PART_WIDTH * hidden, name="grads",
    )
    swap = lambda z, y, x, c: (z, y, x, 1 - c)
    pair = (mine.astype(F32) + permute(other, swap).astype(F32)).astype(BF16)

    piece = HEAD_DIM // planes if HEAD_DIM % planes == 0 else HEAD_DIM

    def turned(step):
        return lambda z, y, x, c: ((z + step) % planes, y, x, c)

    def piece_of(which):
        return lax.dynamic_slice_in_dim(pair, which * piece, piece, 0)

    total = piece_of(plane).astype(F32)
    for step in range(1, planes):
        total += permute(piece_of((plane + step) % planes), turned(step)).astype(F32)
    total = total.astype(BF16)
    whole = jnp.zeros((HEAD_DIM, 3 * hidden), BF16)
    whole = lax.dynamic_update_slice_in_dim(whole, total, plane * piece, 0)
    for step in range(1, planes):
        came = permute(total, turned(step))
        whole = lax.dynamic_update_slice_in_dim(whole, came, (plane + planes - step) % planes * piece, 0)
    whole_other = permute(whole, swap)

    block = min(LANES, group_rows)
    lane_block = lambda rows, shift: pl.BlockSpec((rows, ATT_DIM), lambda h: (0, h + shift))
    full = lambda a: pl.BlockSpec(a.shape, lambda h: (0,) * a.ndim)
    ids = window_ids.reshape(groups, group_rows)
    attended, query_seq = call(
        functools.partial(attention_kernel, block),
        [jax.ShapeDtypeStruct((group_rows, PART_WIDTH), F32), jax.ShapeDtypeStruct((group_rows, PART_WIDTH), BF16)],
        [place, choose, q_in, ids, kv_seq, kv_low, kv_high, kv_seq, kv_low, kv_high],
        in_specs=[full(choose), lane_block(group_rows, 0), full(ids)]
        + [lane_block(group_rows, 0)] * 3 + [lane_block(group_rows, PART_ATT)] * 3,
        out_specs=[lane_block(group_rows, 0)] * 2,
        grid=(PART_ATT,),
        scratch=[VMEM((group_rows // block, block, WINDOW + block), F32)],
        smem=1, flops=4 * group_rows * (WINDOW + block) * PART_WIDTH, name="attention",
    )

    (combined,) = call(
        functools.partial(apply_kernel, tok_dev),
        [jax.ShapeDtypeStruct((group_rows, PART_WIDTH), BF16)],
        [place, weights, whole, whole_other, query_seq, attended],
        scratch=[VMEM((PART_FAST, 3, SPAN, hidden), BF16)],
        smem=1, flops=6 * group_rows * PART_WIDTH * hidden, name="apply",
    )

    blocks = combined.reshape(PARTS, tok_dev, PART_WIDTH)
    parts = []
    for j in range(PARTS):
        goal = 2 * (column ^ j % 2) + (row ^ j // 2)
        send = lax.dynamic_index_in_dim(blocks, goal, 0, keepdims=False)
        parts.append(permute(send, lambda z, y, x, c, j=j: (z, c, x ^ j % 2, y ^ j // 2)))

    (out,) = call(
        norm_kernel,
        [jax.ShapeDtypeStruct((tok_dev, WIDTH), BF16)],
        [place] + parts + [norm_gain.reshape(1, WIDTH)],
        scratch=[VMEM((PARTS, tok_dev, PART_WIDTH), BF16)],
        smem=1, flops=6 * tok_dev * WIDTH, name="norm",
    )
    return out


def solution(mesh):
    rows = P(("groups", "tok"), None)
    return jax.shard_map(
        shards,
        mesh=mesh,
        in_specs=(rows, rows, rows, rows, P("groups"), P("groups"), P(), P()),
        out_specs=rows,
        check_vma=False,
    )
```

```python
import functools
import math

import jax
import jax.numpy as jnp
from jax import lax
from jax.experimental import pallas as pl
from jax.experimental.pallas import tpu as pltpu
from jax.sharding import PartitionSpec as P


HEADS = 8
HEAD_DIM = 320
ATT_DIM = 128
WINDOW = 1024
WIDTH = 2560
ATT_HEADS = 20
LANES = 128
EPS = 1e-06

PARTS = math.gcd(HEADS, ATT_HEADS)
PART_WIDTH = WIDTH // PARTS
PART_FAST = HEADS // PARTS
PART_ATT = ATT_HEADS // PARTS
SPAN = -(-HEAD_DIM // LANES) * LANES


F32 = jnp.float32
BF16 = jnp.bfloat16
VMEM = pltpu.VMEM


def iota(shape, dim):
    return lax.broadcasted_iota(jnp.int32, shape, dim)


def dot(a, b, dims=((1,), (0,))):
    return lax.dot_general(a, b, (dims, ((), ())), preferred_element_type=F32)


def column_of(row):
    n = row.shape[1]
    square = jnp.broadcast_to(row.astype(F32), (n, n))
    diagonal = iota((n, n), 0) == iota((n, n), 1)
    return jnp.sum(jnp.where(diagonal, square, 0.0), axis=1, keepdims=True)


def call(kernel, outs, ins, scratch=(), smem=0, flops=0, grid=None, in_specs=None, out_specs=None):
    specs = [pl.BlockSpec(memory_space=pltpu.SMEM)] * smem
    specs += in_specs or [pl.BlockSpec(memory_space=VMEM)] * (len(ins) - smem)
    moved = sum(x.size * x.dtype.itemsize for x in list(ins) + list(outs))
    extra = {} if grid is None else {"grid": grid}
    return pl.pallas_call(
        kernel,
        out_shape=list(outs),
        in_specs=specs,
        out_specs=out_specs or [pl.BlockSpec(memory_space=VMEM)] * len(outs),
        scratch_shapes=list(scratch),
        compiler_params=pltpu.CompilerParams(vmem_limit_bytes=48 << 20),
        cost_estimate=pl.CostEstimate(flops=flops, bytes_accessed=moved, transcendentals=0),
        **extra,
    )(*ins)


def pack_kernel(group_shift, low_shift, slots, place_ref, order_ref, rate_ref, query_ref, key_ref, value_ref, kv_ref, q_ref, choose_buf, extra_buf):
    n = query_ref.shape[0]
    planes, _, cores = kv_ref.shape[:3]

    @pl.when(pl.program_id(0) == 0)
    def _():
        pos = order_ref[pl.ds(place_ref[0], 1), :]
        pos_col = column_of(pos).astype(jnp.int32)
        group = lax.shift_right_logical(pos, group_shift)
        group_col = lax.shift_right_logical(pos_col, group_shift)
        earlier = (group_col == group) & (iota((n, n), 0) < iota((n, n), 1))
        rank = jnp.sum(jnp.where(earlier, 1.0, 0.0), axis=0, keepdims=True)
        slot = group * slots + rank.astype(jnp.int32)
        choose = jnp.where(iota((n, n), 0) == slot, 1.0, 0.0).astype(BF16)
        choose_buf[...] = choose
        rates = rate_ref[...]
        heads = rates.shape[1]
        extra = jnp.zeros((n, LANES), F32)
        for part in range(3):
            piece = rates.astype(BF16)
            rates = rates - piece.astype(F32)
            put = iota((heads, LANES), 1) == iota((heads, LANES), 0) + part * heads
            extra += dot(piece, jnp.where(put, 1.0, 0.0).astype(BF16))
        within = pos_col & ((1 << group_shift) - 1)
        high = lax.shift_right_logical(within, low_shift).astype(F32)
        low = (within & ((1 << low_shift) - 1)).astype(F32)
        lane = iota((n, LANES), 1)
        extra += jnp.where(lane == 3 * heads, high, 0.0) + jnp.where(lane == 3 * heads + 1, low, 0.0)
        extra_buf[...] = dot(choose, extra.astype(BF16)).astype(BF16)

    def put_rows(ref, rows, begin):
        width = rows.shape[1]
        for plane in range(planes):
            for core in range(cores):
                at = (plane * cores + core) * slots
                ref[plane, 0, core, :, begin : begin + width] = rows[at : at + slots]

    choose = choose_buf[...]
    put_rows(kv_ref, dot(choose, key_ref[...]).astype(BF16), 0)
    put_rows(kv_ref, dot(choose, value_ref[...]).astype(BF16), PART_WIDTH)
    put_rows(kv_ref, extra_buf[...], 2 * PART_WIDTH)
    put_rows(q_ref, dot(choose, query_ref[...]).astype(BF16), 0)


def arrival_choice(extra, low_shift):
    n = extra.shape[0]
    pick = iota((8, LANES), 1) == iota((8, LANES), 0) + 3 * HEADS
    rows = dot(jnp.where(pick, 1.0, 0.0).astype(BF16), extra, ((1,), (1,)))
    pos = rows[0:1] * float(1 << low_shift) + rows[1:2]
    return jnp.where(iota((n, n), 0) == pos.astype(jnp.int32), 1.0, 0.0).astype(BF16)


def place_kernel(low_shift, kv_in_ref, kv_ref, choose_ref):
    choose = arrival_choice(kv_in_ref[:, 2 * PART_WIDTH :], low_shift)
    choose_ref[...] = choose
    for part in range(2):
        lanes = slice(part * PART_WIDTH, (part + 1) * PART_WIDTH)
        kv_ref[:, lanes] = dot(choose, kv_in_ref[:, lanes]).astype(BF16)


def window_of(head):
    begin = head * HEAD_DIM // LANES * LANES
    begin = min(begin, PART_WIDTH - SPAN)
    return begin, head * HEAD_DIM - begin


def head_mask(head):
    _, offset = window_of(head)
    lane = iota((1, SPAN), 1)
    return (lane >= offset) & (lane < offset + HEAD_DIM)


def grads_kernel(chunk, place_ref, kv_ref, weight_ref, mine_ref, other_ref, key_buf, target_buf, dg_buf, du_buf, pr_buf, sums):
    n = kv_ref.shape[0]
    hidden = weight_ref.shape[2]
    part, core = place_ref[1], place_ref[2]
    for head in range(PART_FAST):
        begin, offset = window_of(head)
        valid = head_mask(head)
        rows = pl.ds(begin, SPAN)
        for at in range(0, n, chunk):
            here = pl.ds(at, chunk)
            extra = kv_ref[here, 2 * PART_WIDTH :].astype(F32)
            lane = iota((1, LANES), 1)
            own = part * PART_FAST + head
            wanted = (lane == own) | (lane == HEADS + own) | (lane == 2 * HEADS + own)
            rate = jnp.sum(jnp.where(wanted, extra, 0.0), axis=1, keepdims=True)
            key = jnp.where(valid, kv_ref[here, begin : begin + SPAN], jnp.zeros((), BF16))
            value = kv_ref[here, PART_WIDTH + begin : PART_WIDTH + begin + SPAN].astype(F32)
            target = jnp.where(valid, value * rate, 0.0).astype(BF16)
            key_buf[here, :] = key
            target_buf[here, :] = target
            gate = dot(key, weight_ref[0, rows, :])
            upward = dot(key, weight_ref[1, rows, :])
            backward = dot(target, weight_ref[2, rows, :])
            sigmoid = jax.nn.sigmoid(gate)
            active = gate * sigmoid
            pr_buf[here, :] = (active * upward).astype(BF16)
            du_buf[here, :] = (backward * active).astype(BF16)
            dg_buf[here, :] = (backward * upward * sigmoid * (1.0 + gate * (1.0 - sigmoid))).astype(BF16)
        for index, (left, right) in enumerate(((key_buf, dg_buf), (key_buf, du_buf), (target_buf, pr_buf))):
            total = dot(left[...], right[...], ((0,), (0,)))
            sums[head, :, index * hidden : (index + 1) * hidden] = total[offset : offset + HEAD_DIM].astype(BF16)
    mine_ref[...] = sums[core]
    other_ref[...] = sums[1 - core]


def attention_kernel(block, place_ref, choose_ref, query_in_ref, ids_ref, key_ref, key_low_ref, key_high_ref, value_ref, value_low_ref, value_high_ref, out_ref, query_ref, bias):
    n = choose_ref.shape[0]
    half = WINDOW // 2
    group = place_ref[3]
    last = ids_ref.shape[0] - 1

    @pl.when(pl.program_id(0) == 0)
    def _():
        mid = ids_ref[pl.ds(group, 1), :]
        low = ids_ref[pl.ds(jnp.maximum(group - 1, 0), 1), :]
        high = ids_ref[pl.ds(jnp.minimum(group + 1, last), 1), :]
        low = jnp.where(group > 0, low, -1)
        high = jnp.where(group < last, high, -1)
        for at in range(0, n, block):
            own = column_of(mid[:, at : at + block]).astype(jnp.int32)
            ids = jnp.concatenate([low[:, at:], mid, high[:, : at + block]], axis=1)
            span = ids.shape[1]
            gap = iota((block, span), 1) - iota((block, span), 0) - half
            allowed = (gap < half) & (gap > -half) & (own == ids)
            bias[at // block, :, :] = jnp.where(allowed, 0.0, -1e30)

    query = dot(choose_ref[...], query_in_ref[...]).astype(BF16)
    query_ref[...] = query
    factor = ATT_DIM ** (-0.5) * math.log2(math.e)
    for at in range(0, n, block):
        part = query[at : at + block]
        stops = (0, half - at, half - at + n, half + n + block - half)
        keys = (key_low_ref[at:, :], key_ref[...], key_high_ref[: at + block, :])
        values = (value_low_ref[at:, :], value_ref[...], value_high_ref[: at + block, :])
        scores = []
        for index in range(3):
            lanes = slice(stops[index], stops[index] + keys[index].shape[0])
            scores.append(dot(part, keys[index], ((1,), (1,))) + bias[at // block, :, lanes])
        peak = functools.reduce(jnp.maximum, [jnp.max(s, axis=1, keepdims=True) for s in scores])
        total = jnp.zeros_like(peak)
        mixed = jnp.zeros((block, ATT_DIM), F32)
        for score, value in zip(scores, values):
            weight = jnp.exp2((score - peak) * factor)
            total += jnp.sum(weight, axis=1, keepdims=True)
            mixed += dot(weight.astype(BF16), value)
        out_ref[pl.ds(at, block), :] = mixed / total


def apply_kernel(chunk, place_ref, weight_ref, query_ref, attended_ref, *refs):
    n = query_ref.shape[0]
    hidden = weight_ref.shape[2]
    planes = (len(refs) - 2) // 2
    mine_refs, other_refs, (out_ref, fresh) = refs[:planes], refs[planes : 2 * planes], refs[2 * planes :]
    piece = mine_refs[0].shape[0]
    core, plane = place_ref[2], place_ref[4 + PARTS]
    for head in range(PART_FAST):
        _, offset = window_of(head)
        for index in range(3):
            lanes = slice(index * hidden, (index + 1) * hidden)
            anchor = jnp.full((1, hidden), EPS, F32)
            length = jnp.full((1, hidden), EPS, F32)
            for step in range(planes):
                at = pl.multiple_of((plane + (planes - step)) % planes * piece, 16)
                base = weight_ref[index, pl.ds(at + head * HEAD_DIM, piece), :].astype(F32)
                grad = jnp.where(core == head, mine_refs[step][:, lanes], other_refs[step][:, lanes]).astype(F32)
                update = base + grad
                anchor += jnp.sum(base * base, axis=0, keepdims=True)
                length += jnp.sum(update * update, axis=0, keepdims=True)
            scale = jnp.sqrt(anchor) / jnp.sqrt(length)
            if offset:
                fresh[head, index, :offset, :] = jnp.zeros((offset, hidden), BF16)
            if offset + HEAD_DIM < SPAN:
                fresh[head, index, offset + HEAD_DIM :, :] = jnp.zeros((SPAN - offset - HEAD_DIM, hidden), BF16)
            for step in range(planes):
                at = pl.multiple_of((plane + (planes - step)) % planes * piece, 16)
                base = weight_ref[index, pl.ds(at + head * HEAD_DIM, piece), :].astype(F32)
                grad = jnp.where(core == head, mine_refs[step][:, lanes], other_refs[step][:, lanes]).astype(F32)
                fresh[head, index, pl.ds(at + offset, piece), :] = ((base + grad) * scale).astype(BF16)
    for at in range(0, n, chunk):
        here = pl.ds(at, chunk)
        parts = []
        for head in range(PART_FAST):
            begin, offset = window_of(head)
            query = query_ref[here, begin : begin + SPAN]
            gate = dot(query, fresh[head, 0])
            upward = dot(query, fresh[head, 1])
            product = (gate * jax.nn.sigmoid(gate) * upward).astype(BF16)
            parts.append((begin, dot(product, fresh[head, 2], ((1,), (1,)))))
        for lane in range(0, PART_WIDTH, LANES):
            total = attended_ref[here, lane : lane + LANES]
            for begin, value in parts:
                if begin <= lane < begin + SPAN:
                    total += value[:, lane - begin : lane - begin + LANES]
            out_ref[here, lane : lane + LANES] = total.astype(BF16)


def norm_kernel(place_ref, *refs):
    part_refs, gain_ref, out_ref, buf = refs[:PARTS], refs[PARTS], refs[PARTS + 1], refs[PARTS + 2]
    square = jnp.zeros((out_ref.shape[0], 1), F32)
    for index, ref in enumerate(part_refs):
        rows = ref[...]
        buf[place_ref[4 + index]] = rows
        wide = rows.astype(F32)
        square += jnp.sum(wide * wide, axis=1, keepdims=True)
    factor = lax.rsqrt(square / WIDTH + EPS)
    for part in range(PARTS):
        lanes = slice(part * PART_WIDTH, (part + 1) * PART_WIDTH)
        out_ref[:, lanes] = (buf[part].astype(F32) * factor * gain_ref[:, lanes]).astype(BF16)


def shards(queries, key_rows, value_rows, learn_rates, frame_order, window_ids, fast_init, norm_gain):
    tok_dev = queries.shape[0]
    hidden = fast_init.shape[0]
    sections = lax.axis_size("tok")
    plane_size = PARTS * PART_FAST
    planes = sections // plane_size
    group_rows = tok_dev * PARTS
    groups = planes * PART_FAST
    slots = tok_dev // groups
    half = WINDOW // 2
    assert PART_FAST == 2 and half == group_rows and group_rows & (group_rows - 1) == 0
    group_shift = group_rows.bit_length() - 1
    low_shift = group_shift // 2

    rank = lax.axis_index("tok")
    plane = rank // plane_size
    part = rank // PART_FAST % PARTS
    core = rank % PART_FAST
    row, column = part // 2, part % 2
    group = plane * PART_FAST + core

    def at(plane, row, column, core):
        return plane * plane_size + (row * 2 + column) * PART_FAST + core

    everyone = [(z, y, x, c) for z in range(planes) for y in range(2) for x in range(2) for c in range(2)]

    def permute(array, target):
        route = []
        for source in everyone:
            goal = target(*source)
            if goal is not None:
                route.append((at(*source), at(*goal)))
        return lax.ppermute(array, "tok", route)

    sources = [2 * (core ^ j // 2) + (column ^ j % 2) for j in range(PARTS)]
    place = jnp.stack([rank, part, core, group] + sources + [plane]).astype(jnp.int32)

    def weight_part():
        own = lax.dynamic_slice_in_dim(fast_init, part * PART_WIDTH, PART_WIDTH, 2)
        return jnp.transpose(own, (1, 2, 0))

    weights = weight_part()

    full = lambda a: pl.BlockSpec(a.shape, lambda h: (0,) * a.ndim)
    kv_width = 2 * PART_WIDTH + LANES
    shape = (planes, PARTS, PART_FAST, slots)
    orders = frame_order.reshape(sections, tok_dev)
    cut = pl.BlockSpec((tok_dev, PART_WIDTH), lambda h: (0, h))
    kv_out, q_out = call(
        functools.partial(pack_kernel, group_shift, low_shift, slots),
        [jax.ShapeDtypeStruct(shape + (kv_width,), BF16), jax.ShapeDtypeStruct(shape + (PART_WIDTH,), BF16)],
        [place, orders, learn_rates, queries, key_rows, value_rows],
        in_specs=[full(orders), full(learn_rates), cut, cut, cut],
        out_specs=[
            pl.BlockSpec((planes, 1, PART_FAST, slots, width), lambda h: (0, h, 0, 0, 0))
            for width in (kv_width, PART_WIDTH)
        ],
        grid=(PARTS,),
        scratch=[VMEM((tok_dev, tok_dev), BF16), VMEM((tok_dev, LANES), BF16)],
        smem=1, flops=2 * tok_dev * tok_dev * 3 * WIDTH,
    )

    def exchange(array):
        flat = array.reshape(sections, slots, array.shape[-1])
        return lax.all_to_all(flat, "tok", split_axis=0, concat_axis=0, tiled=True).reshape(group_rows, array.shape[-1])

    kv_in = exchange(kv_out)
    q_in = exchange(q_out)

    kv_seq, choose = call(
        functools.partial(place_kernel, low_shift),
        [jax.ShapeDtypeStruct((group_rows, 2 * PART_WIDTH), BF16), jax.ShapeDtypeStruct((group_rows, group_rows), BF16)],
        [kv_in], flops=2 * group_rows * group_rows * 2 * PART_WIDTH,
    )

    def neighbour(step):
        def target(z, y, x, c):
            goal = z * PART_FAST + c + step
            return (goal // PART_FAST, y, x, goal % PART_FAST) if 0 <= goal < groups else None

        return target

    kv_low = permute(kv_seq, neighbour(1))
    kv_high = permute(kv_seq, neighbour(-1))

    grad_shape = jax.ShapeDtypeStruct((HEAD_DIM, 3 * hidden), BF16)
    mine, other = call(
        functools.partial(grads_kernel, group_rows),
        [grad_shape, grad_shape], [place, kv_in, weights],
        scratch=[VMEM((group_rows, SPAN), BF16)] * 2 + [VMEM((group_rows, hidden), BF16)] * 3
        + [VMEM((PART_FAST, HEAD_DIM, 3 * hidden), BF16)],
        smem=1, flops=12 * group_rows * PART_WIDTH * hidden,
    )
    swap = lambda z, y, x, c: (z, y, x, 1 - c)
    pair = (mine.astype(F32) + permute(other, swap).astype(F32)).astype(BF16)

    piece = HEAD_DIM // planes
    assert piece * planes == HEAD_DIM and piece % 16 == 0

    def turned(step):
        return lambda z, y, x, c: ((z + step) % planes, y, x, c)

    def piece_of(which):
        return lax.dynamic_slice_in_dim(pair, which * piece, piece, 0)

    total = piece_of(plane).astype(F32)
    for step in range(1, planes):
        total += permute(piece_of((plane + step) % planes), turned(step)).astype(F32)
    total = total.astype(BF16)
    pieces = [total]
    for step in range(1, planes):
        pieces.append(permute(total, turned(step)))
    pieces_other = []
    for step in range(planes):
        pieces_other.append(permute(pieces[step], swap))

    block = min(LANES, group_rows)
    lane_block = lambda rows, shift: pl.BlockSpec((rows, ATT_DIM), lambda h: (0, h + shift))
    ids = window_ids.reshape(groups, group_rows)
    attended, query_seq = call(
        functools.partial(attention_kernel, block),
        [jax.ShapeDtypeStruct((group_rows, PART_WIDTH), F32), jax.ShapeDtypeStruct((group_rows, PART_WIDTH), BF16)],
        [place, choose, q_in, ids, kv_seq, kv_low, kv_high, kv_seq, kv_low, kv_high],
        in_specs=[full(choose), lane_block(group_rows, 0), full(ids)]
        + [lane_block(group_rows, 0)] * 3 + [lane_block(group_rows, PART_ATT)] * 3,
        out_specs=[lane_block(group_rows, 0)] * 2,
        grid=(PART_ATT,),
        scratch=[VMEM((group_rows // block, block, WINDOW + block), F32)],
        smem=1, flops=4 * group_rows * (WINDOW + block) * PART_WIDTH,
    )

    (combined,) = call(
        functools.partial(apply_kernel, group_rows),
        [jax.ShapeDtypeStruct((group_rows, PART_WIDTH), BF16)],
        [place, weights, query_seq, attended] + pieces + pieces_other,
        scratch=[VMEM((PART_FAST, 3, SPAN, hidden), BF16)],
        smem=1, flops=6 * group_rows * PART_WIDTH * hidden,
    )

    blocks = combined.reshape(PARTS, tok_dev, PART_WIDTH)
    parts = []
    for j in range(PARTS):
        goal = 2 * (column ^ j % 2) + (row ^ j // 2)
        send = lax.dynamic_index_in_dim(blocks, goal, 0, keepdims=False)
        parts.append(permute(send, lambda z, y, x, c, j=j: (z, c, x ^ j % 2, y ^ j // 2)))

    (out,) = call(
        norm_kernel,
        [jax.ShapeDtypeStruct((tok_dev, WIDTH), BF16)],
        [place] + parts + [norm_gain.reshape(1, WIDTH)],
        scratch=[VMEM((PARTS, tok_dev, PART_WIDTH), BF16)],
        smem=1, flops=6 * tok_dev * WIDTH,
    )
    return out


def solution(mesh):
    rows = P(("groups", "tok"), None)
    return jax.shard_map(
        shards,
        mesh=mesh,
        in_specs=(rows, rows, rows, rows, P("groups"), P("groups"), P(), P()),
        out_specs=rows,
        check_vma=False,
    )
```

```python
import functools
import math

import jax
import jax.numpy as jnp
from jax import lax
from jax.experimental import pallas as pl
from jax.experimental.pallas import tpu as pltpu
from jax.sharding import PartitionSpec as P


HEADS = 8
HEAD_DIM = 320
ATT_DIM = 128
WINDOW = 1024
WIDTH = 2560
ATT_HEADS = 20
LANES = 128
EPS = 1e-06

PARTS = math.gcd(HEADS, ATT_HEADS)
PART_WIDTH = WIDTH // PARTS
PART_FAST = HEADS // PARTS
PART_ATT = ATT_HEADS // PARTS
SPAN = -(-HEAD_DIM // LANES) * LANES


F32 = jnp.float32
BF16 = jnp.bfloat16
VMEM = pltpu.VMEM


def iota(shape, dim):
    return lax.broadcasted_iota(jnp.int32, shape, dim)


def dot(a, b, dims=((1,), (0,))):
    return lax.dot_general(a, b, (dims, ((), ())), preferred_element_type=F32)


def column_of(row):
    n = row.shape[1]
    square = jnp.broadcast_to(row.astype(F32), (n, n))
    diagonal = iota((n, n), 0) == iota((n, n), 1)
    return jnp.sum(jnp.where(diagonal, square, 0.0), axis=1, keepdims=True)


def call(kernel, outs, ins, scratch=(), smem=0, flops=0, grid=None, in_specs=None, out_specs=None):
    specs = [pl.BlockSpec(memory_space=pltpu.SMEM)] * smem
    specs += in_specs or [pl.BlockSpec(memory_space=VMEM)] * (len(ins) - smem)
    moved = sum(x.size * x.dtype.itemsize for x in list(ins) + list(outs))
    extra = {} if grid is None else {"grid": grid}
    return pl.pallas_call(
        kernel,
        out_shape=list(outs),
        in_specs=specs,
        out_specs=out_specs or [pl.BlockSpec(memory_space=VMEM)] * len(outs),
        scratch_shapes=list(scratch),
        compiler_params=pltpu.CompilerParams(vmem_limit_bytes=60 << 20),
        cost_estimate=pl.CostEstimate(flops=flops, bytes_accessed=moved, transcendentals=0),
        **extra,
    )(*ins)


def window_of(head):
    begin = min(head * HEAD_DIM // LANES * LANES, PART_WIDTH - SPAN)
    return begin, head * HEAD_DIM - begin


def heads_kernel(place_ref, rate_ref, key_ref, value_ref, *out_refs):
    n = key_ref.shape[0]
    step, part, core = pl.program_id(0), place_ref[1], place_ref[2]
    rates = rate_ref[...]
    lane = iota((n, SPAN), 1)
    rows = []
    for head in range(PART_FAST):
        begin, offset = window_of(head)

        def window(ref):
            rows = ref[:, begin : begin + SPAN].astype(F32)
            rows = pltpu.roll(rows, SPAN - offset, 1) if offset else rows
            return jnp.where(lane < HEAD_DIM, rows, 0.0)

        own = (step ^ part) * PART_FAST + head
        rate = jnp.sum(jnp.where(iota(rates.shape, 1) == own, rates, 0.0), axis=1, keepdims=True)
        keys = window(key_ref)
        for index in range(3):
            piece = rate.astype(BF16).astype(F32)
            rate = rate - piece
            keys = jnp.where(lane == HEAD_DIM + index, piece, keys)
        rows.append((keys, window(value_ref)))
    for flip in range(PART_FAST):
        chosen = [jnp.where(core == flip, first, second).astype(BF16) for first, second in zip(*rows)]
        for index in range(PARTS):
            @pl.when(step == index)
            def _():
                out_refs[index * PART_FAST + flip][:, :SPAN] = chosen[0]
                out_refs[index * PART_FAST + flip][:, SPAN:] = chosen[1]


def pack_kernel(group_shift, slots, place_ref, order_ref, query_ref, key_ref, value_ref, kv_ref, q_ref, choose_buf):
    n = query_ref.shape[0]
    planes, _, cores = kv_ref.shape[:3]

    @pl.when(pl.program_id(0) == 0)
    def _():
        pos = order_ref[pl.ds(place_ref[0], 1), :]
        group = lax.shift_right_logical(pos, group_shift)
        group_col = column_of(group).astype(jnp.int32)
        earlier = (group_col == group) & (iota((n, n), 0) < iota((n, n), 1))
        rank = jnp.sum(jnp.where(earlier, 1.0, 0.0), axis=0, keepdims=True)
        slot = group * slots + rank.astype(jnp.int32)
        choose_buf[...] = jnp.where(iota((n, n), 0) == slot, 1.0, 0.0).astype(BF16)

    def put_rows(ref, rows, begin):
        width = rows.shape[1]
        for plane in range(planes):
            for core in range(cores):
                at = (plane * cores + core) * slots
                ref[plane, 0, core, :, begin : begin + width] = rows[at : at + slots]

    choose = choose_buf[...]
    put_rows(kv_ref, dot(choose, key_ref[...]).astype(BF16), 0)
    put_rows(kv_ref, dot(choose, value_ref[...]).astype(BF16), PART_WIDTH)
    put_rows(q_ref, dot(choose, query_ref[...]).astype(BF16), 0)


def arrival_choice(group_shift, slots, orders, group, n):
    sources, rows = orders.shape
    low_shift = group_shift // 2
    mine = lax.shift_right_logical(orders, group_shift) == group
    before = jnp.where(iota((rows, rows), 0) < iota((rows, rows), 1), 1.0, 0.0).astype(BF16)
    rank = dot(jnp.where(mine, 1.0, 0.0).astype(BF16), before)
    within = orders & ((1 << group_shift) - 1)
    digits = (lax.shift_right_logical(within, low_shift).astype(F32), (within & ((1 << low_shift) - 1)).astype(F32))
    spread = jnp.where(iota((sources, n), 1) // slots == iota((sources, n), 0), 1.0, 0.0).astype(BF16)
    keep = iota((slots, n), 1) % slots == iota((slots, n), 0)
    column = iota((sources, slots), 1)
    pos = jnp.zeros((1, n), F32)
    for digit, weight in zip(digits, (float(1 << low_shift), 1.0)):
        table = jnp.zeros((sources, slots), F32)
        for k in range(slots):
            one = jnp.sum(jnp.where(mine & (rank == float(k)), digit, 0.0), axis=1, keepdims=True)
            table = jnp.where(column == k, one, table)
        wide = dot(table.astype(BF16), spread, ((0,), (0,)))
        pos += weight * jnp.sum(jnp.where(keep, wide, 0.0), axis=0, keepdims=True)
    return jnp.where(iota((n, n), 0) == pos.astype(jnp.int32), 1.0, 0.0).astype(BF16)


def place_kernel(group_shift, slots, place_ref, order_ref, kv_in_ref, kv_ref, choose_ref):
    choose = arrival_choice(group_shift, slots, order_ref[...], place_ref[3], choose_ref.shape[0])
    choose_ref[...] = choose
    for part in range(2):
        lanes = slice(part * PART_WIDTH, (part + 1) * PART_WIDTH)
        kv_ref[:, lanes] = dot(choose, kv_in_ref[:, lanes]).astype(BF16)


def grads_kernel(chunk, place_ref, weight_ref, *refs):
    kv_refs, (out_ref, weight_buf, key_buf, target_buf, dg_buf, du_buf, pr_buf) = refs[:-7], refs[-7:]
    block = kv_refs[0].shape[0]
    n = key_buf.shape[0]
    hidden = weight_ref.shape[2]
    first = pl.multiple_of(place_ref[2] * HEAD_DIM, 16)
    for index in range(3):
        weight_buf[index, :HEAD_DIM, :] = weight_ref[index, pl.ds(first, HEAD_DIM), :]
        weight_buf[index, HEAD_DIM:, :] = jnp.zeros((SPAN - HEAD_DIM, hidden), BF16)
    lane = iota((1, SPAN), 1)
    wanted = (lane >= HEAD_DIM) & (lane < HEAD_DIM + 3)
    for index, ref in enumerate(kv_refs):
        here = pl.ds(index * block, block)
        key = ref[:, :SPAN]
        rate = jnp.sum(jnp.where(wanted, key.astype(F32), 0.0), axis=1, keepdims=True)
        key_buf[here, :] = key
        target_buf[here, :] = (ref[:, SPAN:].astype(F32) * rate).astype(BF16)
    for at in range(0, n, chunk):
        here = pl.ds(at, chunk)
        gate = dot(key_buf[here, :], weight_buf[0])
        upward = dot(key_buf[here, :], weight_buf[1])
        backward = dot(target_buf[here, :], weight_buf[2])
        sigmoid = jax.nn.sigmoid(gate)
        active = gate * sigmoid
        pr_buf[here, :] = (active * upward).astype(BF16)
        du_buf[here, :] = (backward * active).astype(BF16)
        dg_buf[here, :] = (backward * upward * sigmoid * (1.0 + gate * (1.0 - sigmoid))).astype(BF16)
    for index, (left, right) in enumerate(((key_buf, dg_buf), (key_buf, du_buf), (target_buf, pr_buf))):
        total = dot(left[...], right[...], ((0,), (0,)))
        out_ref[:, index * hidden : (index + 1) * hidden] = total[:HEAD_DIM].astype(BF16)


def attention_kernel(block, place_ref, choose_ref, query_in_ref, ids_ref, key_ref, key_low_ref, key_high_ref, value_ref, value_low_ref, value_high_ref, out_ref, query_ref, bias):
    n = choose_ref.shape[0]
    half = WINDOW // 2
    group = place_ref[3]
    last = ids_ref.shape[0] - 1

    @pl.when(pl.program_id(0) == 0)
    def _():
        mid = ids_ref[pl.ds(group, 1), :]
        low = ids_ref[pl.ds(jnp.maximum(group - 1, 0), 1), :]
        high = ids_ref[pl.ds(jnp.minimum(group + 1, last), 1), :]
        low = jnp.where(group > 0, low, -1)
        high = jnp.where(group < last, high, -1)
        for at in range(0, n, block):
            own = column_of(mid[:, at : at + block]).astype(jnp.int32)
            ids = jnp.concatenate([low[:, at:], mid, high[:, : at + block]], axis=1)
            span = ids.shape[1]
            gap = iota((block, span), 1) - iota((block, span), 0) - half
            allowed = (gap < half) & (gap > -half) & (own == ids)
            bias[at // block, :, :] = jnp.where(allowed, 0.0, -1e30)

    query = dot(choose_ref[...], query_in_ref[...]).astype(BF16)
    query_ref[...] = query
    factor = ATT_DIM ** (-0.5) * math.log2(math.e)
    for at in range(0, n, block):
        part = query[at : at + block]
        stops = (0, half - at, half - at + n, half + n + block - half)
        keys = (key_low_ref[at:, :], key_ref[...], key_high_ref[: at + block, :])
        values = (value_low_ref[at:, :], value_ref[...], value_high_ref[: at + block, :])
        scores = []
        for index in range(3):
            lanes = slice(stops[index], stops[index] + keys[index].shape[0])
            scores.append(dot(part, keys[index], ((1,), (1,))) + bias[at // block, :, lanes])
        peak = functools.reduce(jnp.maximum, [jnp.max(s, axis=1, keepdims=True) for s in scores])
        total = jnp.zeros_like(peak)
        mixed = jnp.zeros((block, ATT_DIM), F32)
        for score, value in zip(scores, values):
            weight = jnp.exp2((score - peak) * factor)
            total += jnp.sum(weight, axis=1, keepdims=True)
            mixed += dot(weight.astype(BF16), value)
        out_ref[pl.ds(at, block), :] = mixed / total


def apply_kernel(place_ref, weight_ref, query_ref, attended_ref, *refs):
    hidden = weight_ref.shape[2]
    count = (len(refs) - 3) // 2
    mine_refs, other_refs, (out_ref, fresh, scales) = refs[:count], refs[count : 2 * count], refs[2 * count :]
    piece = mine_refs[0].shape[0]
    core = place_ref[2]
    for head in range(PART_FAST):
        _, offset = window_of(head)
        for index in range(3):
            lanes = slice(index * hidden, (index + 1) * hidden)
            anchor = jnp.full((1, hidden), EPS, F32)
            length = jnp.full((1, hidden), EPS, F32)
            for step in range(count):
                at = pl.multiple_of(place_ref[4 + PARTS + step], 16)
                base = weight_ref[index, pl.ds(at + head * HEAD_DIM, piece), :].astype(F32)
                grad = jnp.where(core == head, mine_refs[step][:, lanes], other_refs[step][:, lanes]).astype(F32)
                update = base + grad
                anchor += jnp.sum(base * base, axis=0, keepdims=True)
                length += jnp.sum(update * update, axis=0, keepdims=True)
                fresh[head, index, pl.ds(at + offset, piece), :] = update.astype(BF16)
            scales[head * 3 + index, :] = (jnp.sqrt(anchor) / jnp.sqrt(length))[0]
            if offset:
                fresh[head, index, :offset, :] = jnp.zeros((offset, hidden), BF16)
            if offset + HEAD_DIM < SPAN:
                fresh[head, index, offset + HEAD_DIM :, :] = jnp.zeros((SPAN - offset - HEAD_DIM, hidden), BF16)
    parts = []
    for head in range(PART_FAST):
        begin, _ = window_of(head)
        query = query_ref[:, begin : begin + SPAN]
        scale = [scales[head * 3 + index : head * 3 + index + 1, :] for index in range(3)]
        gate = dot(query, fresh[head, 0]) * scale[0]
        upward = dot(query, fresh[head, 1]) * (scale[1] * scale[2])
        product = (gate * jax.nn.sigmoid(gate) * upward).astype(BF16)
        parts.append((begin, dot(product, fresh[head, 2], ((1,), (1,)))))
    for lane in range(0, PART_WIDTH, LANES):
        total = attended_ref[:, lane : lane + LANES]
        for begin, value in parts:
            if begin <= lane < begin + SPAN:
                total += value[:, lane - begin : lane - begin + LANES]
        out_ref[:, lane : lane + LANES] = total.astype(BF16)


def norm_kernel(place_ref, *refs):
    part_refs, gain_ref, out_ref, buf = refs[:PARTS], refs[PARTS], refs[PARTS + 1], refs[PARTS + 2]
    square = jnp.zeros((out_ref.shape[0], 1), F32)
    for index, ref in enumerate(part_refs):
        rows = ref[...]
        buf[place_ref[4 + index]] = rows
        wide = rows.astype(F32)
        square += jnp.sum(wide * wide, axis=1, keepdims=True)
    factor = lax.rsqrt(square / WIDTH + EPS)
    for part in range(PARTS):
        lanes = slice(part * PART_WIDTH, (part + 1) * PART_WIDTH)
        out_ref[:, lanes] = (buf[part].astype(F32) * factor * gain_ref[:, lanes]).astype(BF16)


def shards(queries, key_rows, value_rows, learn_rates, frame_order, window_ids, fast_init, norm_gain):
    tok_dev = queries.shape[0]
    hidden = fast_init.shape[0]
    sections = lax.axis_size("tok")
    plane_size = PARTS * PART_FAST
    planes = sections // plane_size
    group_rows = tok_dev * PARTS
    groups = planes * PART_FAST
    slots = tok_dev // groups
    half = WINDOW // 2
    assert PART_FAST == 2 and half == group_rows and group_rows & (group_rows - 1) == 0
    group_shift = group_rows.bit_length() - 1

    rank = lax.axis_index("tok")
    plane = rank // plane_size
    part = rank // PART_FAST % PARTS
    core = rank % PART_FAST
    row, column = part // 2, part % 2
    group = plane * PART_FAST + core

    def at(plane, row, column, core):
        return plane * plane_size + (row * 2 + column) * PART_FAST + core

    everyone = [(z, y, x, c) for z in range(planes) for y in range(2) for x in range(2) for c in range(2)]

    def permute(array, target):
        route = []
        for source in everyone:
            goal = target(*source)
            if goal is not None:
                route.append((at(*source), at(*goal)))
        return lax.ppermute(array, "tok", route)

    sources = [2 * (core ^ j // 2) + (column ^ j % 2) for j in range(PARTS)]
    bits = planes.bit_length() - 1
    piece = HEAD_DIM >> bits
    assert planes == 1 << bits and piece << bits == HEAD_DIM and piece % 16 == 0

    def owned(plane):
        return sum((plane >> bit & 1) * (HEAD_DIM >> bit + 1) for bit in range(bits))

    masks = [0]
    for bit in reversed(range(bits)):
        masks += [mask ^ 1 << bit for mask in masks]
    starts = [owned(plane ^ mask) for mask in masks]
    place = jnp.stack([rank, part, core, group] + sources + starts).astype(jnp.int32)

    def weight_part():
        own = lax.dynamic_slice_in_dim(fast_init, part * PART_WIDTH, PART_WIDTH, 2)
        return jnp.transpose(own, (1, 2, 0))

    weights = weight_part()

    full = lambda a: pl.BlockSpec(a.shape, lambda h: (0,) * a.ndim)
    cut = pl.BlockSpec((tok_dev, PART_WIDTH), lambda h: (0, h))
    other_cut = pl.BlockSpec((tok_dev, PART_WIDTH), lambda h, place: (0, h ^ place[1]))
    whole = lambda shape: pl.BlockSpec(shape, lambda h, place: (0,) * len(shape))
    heads_out = pl.pallas_call(
        heads_kernel,
        out_shape=[jax.ShapeDtypeStruct((tok_dev, 2 * SPAN), BF16)] * plane_size,
        grid_spec=pltpu.PrefetchScalarGridSpec(
            num_scalar_prefetch=1,
            grid=(PARTS,),
            in_specs=[whole(learn_rates.shape), other_cut, other_cut],
            out_specs=[whole((tok_dev, 2 * SPAN))] * plane_size,
        ),
        compiler_params=pltpu.CompilerParams(vmem_limit_bytes=60 << 20),
        cost_estimate=pl.CostEstimate(flops=tok_dev * WIDTH, bytes_accessed=8 * tok_dev * WIDTH, transcendentals=0),
        name="heads",
    )(place, learn_rates, key_rows, value_rows)
    heads_in = [heads_out[0]]
    for j in range(1, plane_size):
        heads_in.append(permute(heads_out[j], lambda z, y, x, c, j=j: (z, y ^ j >> 2, x ^ j >> 1 & 1, c ^ j & 1)))

    shape = (planes, PARTS, PART_FAST, slots)
    orders = frame_order.reshape(sections, tok_dev)
    kv_out, q_out = call(
        functools.partial(pack_kernel, group_shift, slots),
        [jax.ShapeDtypeStruct(shape + (width,), BF16) for width in (2 * PART_WIDTH, PART_WIDTH)],
        [place, orders, queries, key_rows, value_rows],
        in_specs=[full(orders), cut, cut, cut],
        out_specs=[
            pl.BlockSpec((planes, 1, PART_FAST, slots, width), lambda h: (0, h, 0, 0, 0))
            for width in (2 * PART_WIDTH, PART_WIDTH)
        ],
        grid=(PARTS,),
        scratch=[VMEM((tok_dev, tok_dev), BF16)],
        smem=1, flops=2 * tok_dev * tok_dev * 3 * WIDTH,
    )

    def exchange(array):
        flat = array.reshape(sections, slots, array.shape[-1])
        return lax.all_to_all(flat, "tok", split_axis=0, concat_axis=0, tiled=True).reshape(group_rows, array.shape[-1])

    kv_in = exchange(kv_out)
    q_in = exchange(q_out)

    kv_seq, choose = call(
        functools.partial(place_kernel, group_shift, slots),
        [jax.ShapeDtypeStruct((group_rows, 2 * PART_WIDTH), BF16), jax.ShapeDtypeStruct((group_rows, group_rows), BF16)],
        [place, orders, kv_in], smem=1, flops=2 * group_rows * group_rows * 2 * PART_WIDTH,
    )

    def neighbour(step):
        def target(z, y, x, c):
            goal = z * PART_FAST + c + step
            return (goal // PART_FAST, y, x, goal % PART_FAST) if 0 <= goal < groups else None

        return target

    kv_low = permute(kv_seq, neighbour(1))
    kv_high = permute(kv_seq, neighbour(-1))

    tokens = plane_size * tok_dev
    (total,) = call(
        functools.partial(grads_kernel, tokens // 2),
        [jax.ShapeDtypeStruct((HEAD_DIM, 3 * hidden), BF16)], [place, weights] + heads_in,
        scratch=[VMEM((3, SPAN, hidden), BF16)] + [VMEM((tokens, SPAN), BF16)] * 2 + [VMEM((tokens, hidden), BF16)] * 3,
        smem=1, flops=12 * tokens * HEAD_DIM * hidden,
    )

    def across(bit):
        return lambda z, y, x, c: (z ^ 1 << bit, y, x, c)

    for bit in range(bits):
        size = HEAD_DIM >> bit + 1
        side = plane >> bit & 1
        came = permute(lax.dynamic_slice_in_dim(total, (1 - side) * size, size, 0), across(bit))
        kept = lax.dynamic_slice_in_dim(total, side * size, size, 0)
        total = (kept.astype(F32) + came.astype(F32)).astype(BF16)
    pieces = [total]
    for bit in reversed(range(bits)):
        fresh_pieces = []
        for held in pieces:
            fresh_pieces.append(permute(held, across(bit)))
        pieces += fresh_pieces
    swap = lambda z, y, x, c: (z, y, x, 1 - c)
    pieces_other = []
    for held in pieces:
        pieces_other.append(permute(held, swap))

    block = min(LANES, group_rows)
    lane_block = lambda rows, shift: pl.BlockSpec((rows, ATT_DIM), lambda h: (0, h + shift))
    ids = window_ids.reshape(groups, group_rows)
    attended, query_seq = call(
        functools.partial(attention_kernel, block),
        [jax.ShapeDtypeStruct((group_rows, PART_WIDTH), F32), jax.ShapeDtypeStruct((group_rows, PART_WIDTH), BF16)],
        [place, choose, q_in, ids, kv_seq, kv_low, kv_high, kv_seq, kv_low, kv_high],
        in_specs=[full(choose), lane_block(group_rows, 0), full(ids)]
        + [lane_block(group_rows, 0)] * 3 + [lane_block(group_rows, PART_ATT)] * 3,
        out_specs=[lane_block(group_rows, 0)] * 2,
        grid=(PART_ATT,),
        scratch=[VMEM((group_rows // block, block, WINDOW + block), F32)],
        smem=1, flops=4 * group_rows * (WINDOW + block) * PART_WIDTH,
    )

    (combined,) = call(
        apply_kernel,
        [jax.ShapeDtypeStruct((group_rows, PART_WIDTH), BF16)],
        [place, weights, query_seq, attended] + pieces + pieces_other,
        scratch=[VMEM((PART_FAST, 3, SPAN, hidden), BF16), VMEM((PART_FAST * 3, hidden), F32)],
        smem=1, flops=6 * group_rows * PART_WIDTH * hidden,
    )

    blocks = combined.reshape(PARTS, tok_dev, PART_WIDTH)
    parts = []
    for j in range(PARTS):
        goal = 2 * (column ^ j % 2) + (row ^ j // 2)
        send = lax.dynamic_index_in_dim(blocks, goal, 0, keepdims=False)
        parts.append(permute(send, lambda z, y, x, c, j=j: (z, c, x ^ j % 2, y ^ j // 2)))

    (out,) = call(
        norm_kernel,
        [jax.ShapeDtypeStruct((tok_dev, WIDTH), BF16)],
        [place] + parts + [norm_gain.reshape(1, WIDTH)],
        scratch=[VMEM((PARTS, tok_dev, PART_WIDTH), BF16)],
        smem=1, flops=6 * tok_dev * WIDTH,
    )
    return out


def solution(mesh):
    rows = P(("groups", "tok"), None)
    return jax.shard_map(
        shards,
        mesh=mesh,
        in_specs=(rows, rows, rows, rows, P("groups"), P("groups"), P(), P()),
        out_specs=rows,
        check_vma=False,
    )
```

```python
import functools
import math

import jax
import jax.numpy as jnp
from jax import lax
from jax.experimental import pallas as pl
from jax.experimental.pallas import tpu as pltpu
from jax.sharding import PartitionSpec as P


HEADS = 8
HEAD_DIM = 320
ATT_DIM = 128
WINDOW = 1024
WIDTH = 2560
ATT_HEADS = 20
LANES = 128
EPS = 1e-06

PARTS = math.gcd(HEADS, ATT_HEADS)
PART_WIDTH = WIDTH // PARTS
PART_FAST = HEADS // PARTS
PART_ATT = ATT_HEADS // PARTS
SPAN = -(-HEAD_DIM // LANES) * LANES


F32 = jnp.float32
BF16 = jnp.bfloat16
VMEM = pltpu.VMEM


def iota(shape, dim):
    return lax.broadcasted_iota(jnp.int32, shape, dim)


def dot(a, b, dims=((1,), (0,))):
    return lax.dot_general(a, b, (dims, ((), ())), preferred_element_type=F32)


def column_of(row):
    n = row.shape[1]
    square = jnp.broadcast_to(row.astype(F32), (n, n))
    diagonal = iota((n, n), 0) == iota((n, n), 1)
    return jnp.sum(jnp.where(diagonal, square, 0.0), axis=1, keepdims=True)


def call(kernel, outs, ins, scratch=(), smem=0, flops=0, grid=None, in_specs=None, out_specs=None):
    specs = [pl.BlockSpec(memory_space=pltpu.SMEM)] * smem
    specs += in_specs or [pl.BlockSpec(memory_space=VMEM)] * (len(ins) - smem)
    moved = sum(x.size * x.dtype.itemsize for x in list(ins) + list(outs))
    extra = {} if grid is None else {"grid": grid}
    return pl.pallas_call(
        kernel,
        out_shape=list(outs),
        in_specs=specs,
        out_specs=out_specs or [pl.BlockSpec(memory_space=VMEM)] * len(outs),
        scratch_shapes=list(scratch),
        compiler_params=pltpu.CompilerParams(vmem_limit_bytes=60 << 20),
        cost_estimate=pl.CostEstimate(flops=flops, bytes_accessed=moved, transcendentals=0),
        **extra,
    )(*ins)


def window_of(head):
    begin = min(head * HEAD_DIM // LANES * LANES, PART_WIDTH - SPAN)
    return begin, head * HEAD_DIM - begin


def heads_kernel(place_ref, rate_ref, key_ref, value_ref, *out_refs):
    n = key_ref.shape[0]
    step, part, core = pl.program_id(0), place_ref[1], place_ref[2]
    rates = rate_ref[...]
    lane = iota((n, SPAN), 1)
    rows = []
    for head in range(PART_FAST):
        begin, offset = window_of(head)

        def window(ref):
            rows = ref[:, begin : begin + SPAN].astype(F32)
            rows = pltpu.roll(rows, SPAN - offset, 1) if offset else rows
            return jnp.where(lane < HEAD_DIM, rows, 0.0)

        own = (step ^ part) * PART_FAST + head
        rate = jnp.sum(jnp.where(iota(rates.shape, 1) == own, rates, 0.0), axis=1, keepdims=True)
        keys = window(key_ref)
        for index in range(3):
            piece = rate.astype(BF16).astype(F32)
            rate = rate - piece
            keys = jnp.where(lane == HEAD_DIM + index, piece, keys)
        rows.append((keys, window(value_ref)))
    for flip in range(PART_FAST):
        chosen = [jnp.where(core == flip, first, second).astype(BF16) for first, second in zip(*rows)]
        for index in range(PARTS):
            @pl.when(step == index)
            def _():
                out_refs[index * PART_FAST + flip][:, :SPAN] = chosen[0]
                out_refs[index * PART_FAST + flip][:, SPAN:] = chosen[1]


def pack_kernel(group_shift, slots, place_ref, order_ref, query_ref, key_ref, value_ref, kv_ref, q_ref, choose_buf):
    n = query_ref.shape[0]
    planes, _, cores = kv_ref.shape[:3]

    @pl.when(pl.program_id(0) == 0)
    def _():
        pos = order_ref[pl.ds(place_ref[0], 1), :]
        group = lax.shift_right_logical(pos, group_shift)
        group_col = column_of(group).astype(jnp.int32)
        earlier = (group_col == group) & (iota((n, n), 0) < iota((n, n), 1))
        rank = jnp.sum(jnp.where(earlier, 1.0, 0.0), axis=0, keepdims=True)
        slot = group * slots + rank.astype(jnp.int32)
        choose_buf[...] = jnp.where(iota((n, n), 0) == slot, 1.0, 0.0).astype(BF16)

    def put_rows(ref, rows, begin):
        width = rows.shape[1]
        for plane in range(planes):
            for core in range(cores):
                at = (plane * cores + core) * slots
                ref[plane, 0, core, :, begin : begin + width] = rows[at : at + slots]

    choose = choose_buf[...]
    put_rows(kv_ref, dot(choose, key_ref[...]).astype(BF16), 0)
    put_rows(kv_ref, dot(choose, value_ref[...]).astype(BF16), PART_WIDTH)
    put_rows(q_ref, dot(choose, query_ref[...]).astype(BF16), 0)


def arrival_choice(group_shift, slots, orders, group, n):
    sources, rows = orders.shape
    low_shift = group_shift // 2
    mine = lax.shift_right_logical(orders, group_shift) == group
    before = jnp.where(iota((rows, rows), 0) < iota((rows, rows), 1), 1.0, 0.0).astype(BF16)
    rank = dot(jnp.where(mine, 1.0, 0.0).astype(BF16), before)
    within = orders & ((1 << group_shift) - 1)
    digits = (lax.shift_right_logical(within, low_shift).astype(F32), (within & ((1 << low_shift) - 1)).astype(F32))
    spread = jnp.where(iota((sources, n), 1) // slots == iota((sources, n), 0), 1.0, 0.0).astype(BF16)
    keep = iota((slots, n), 1) % slots == iota((slots, n), 0)
    column = iota((sources, slots), 1)
    pos = jnp.zeros((1, n), F32)
    for digit, weight in zip(digits, (float(1 << low_shift), 1.0)):
        table = jnp.zeros((sources, slots), F32)
        for k in range(slots):
            one = jnp.sum(jnp.where(mine & (rank == float(k)), digit, 0.0), axis=1, keepdims=True)
            table = jnp.where(column == k, one, table)
        wide = dot(table.astype(BF16), spread, ((0,), (0,)))
        pos += weight * jnp.sum(jnp.where(keep, wide, 0.0), axis=0, keepdims=True)
    return jnp.where(iota((n, n), 0) == pos.astype(jnp.int32), 1.0, 0.0).astype(BF16)


def place_kernel(group_shift, slots, place_ref, order_ref, kv_in_ref, kv_ref, choose_ref):
    choose = arrival_choice(group_shift, slots, order_ref[...], place_ref[3], choose_ref.shape[0])
    choose_ref[...] = choose
    for part in range(2):
        lanes = slice(part * PART_WIDTH, (part + 1) * PART_WIDTH)
        kv_ref[:, lanes] = dot(choose, kv_in_ref[:, lanes]).astype(BF16)


def grads_kernel(chunk, place_ref, weight_ref, *refs):
    kv_refs, (out_ref, weight_buf, key_buf, target_buf, dg_buf, du_buf, pr_buf) = refs[:-7], refs[-7:]
    block = kv_refs[0].shape[0]
    n = key_buf.shape[0]
    hidden = weight_ref.shape[2]
    first = pl.multiple_of(place_ref[2] * HEAD_DIM, 16)
    for index in range(3):
        weight_buf[index, :HEAD_DIM, :] = weight_ref[index, pl.ds(first, HEAD_DIM), :]
        weight_buf[index, HEAD_DIM:, :] = jnp.zeros((SPAN - HEAD_DIM, hidden), BF16)
    lane = iota((1, SPAN), 1)
    wanted = (lane >= HEAD_DIM) & (lane < HEAD_DIM + 3)
    for index, ref in enumerate(kv_refs):
        here = pl.ds(index * block, block)
        key = ref[:, :SPAN]
        rate = jnp.sum(jnp.where(wanted, key.astype(F32), 0.0), axis=1, keepdims=True)
        key_buf[here, :] = key
        target_buf[here, :] = (ref[:, SPAN:].astype(F32) * rate).astype(BF16)
    for at in range(0, n, chunk):
        here = pl.ds(at, chunk)
        gate = dot(key_buf[here, :], weight_buf[0])
        upward = dot(key_buf[here, :], weight_buf[1])
        backward = dot(target_buf[here, :], weight_buf[2])
        sigmoid = jax.nn.sigmoid(gate)
        active = gate * sigmoid
        pr_buf[here, :] = (active * upward).astype(BF16)
        du_buf[here, :] = (backward * active).astype(BF16)
        dg_buf[here, :] = (backward * upward * sigmoid * (1.0 + gate * (1.0 - sigmoid))).astype(BF16)
    for index, (left, right) in enumerate(((key_buf, dg_buf), (key_buf, du_buf), (target_buf, pr_buf))):
        total = dot(left[...], right[...], ((0,), (0,)))
        out_ref[:, index * hidden : (index + 1) * hidden] = total[:HEAD_DIM].astype(BF16)


def attention_kernel(block, place_ref, choose_ref, query_in_ref, ids_ref, key_ref, key_low_ref, key_high_ref, value_ref, value_low_ref, value_high_ref, out_ref, query_ref, bias):
    n = choose_ref.shape[0]
    half = WINDOW // 2
    group = place_ref[3]
    last = ids_ref.shape[0] - 1

    @pl.when(pl.program_id(0) == 0)
    def _():
        mid = ids_ref[pl.ds(group, 1), :]
        low = ids_ref[pl.ds(jnp.maximum(group - 1, 0), 1), :]
        high = ids_ref[pl.ds(jnp.minimum(group + 1, last), 1), :]
        low = jnp.where(group > 0, low, -1)
        high = jnp.where(group < last, high, -1)
        for at in range(0, n, block):
            own = column_of(mid[:, at : at + block]).astype(jnp.int32)
            ids = jnp.concatenate([low[:, at:], mid, high[:, : at + block]], axis=1)
            span = ids.shape[1]
            gap = iota((block, span), 1) - iota((block, span), 0) - half
            allowed = (gap < half) & (gap > -half) & (own == ids)
            bias[at // block, :, :] = jnp.where(allowed, 0.0, -1e30)

    query = dot(choose_ref[...], query_in_ref[...]).astype(BF16)
    query_ref[...] = query
    factor = ATT_DIM ** (-0.5) * math.log2(math.e)
    for at in range(0, n, block):
        part = query[at : at + block]
        stops = (0, half - at, half - at + n, half + n + block - half)
        keys = (key_low_ref[at:, :], key_ref[...], key_high_ref[: at + block, :])
        values = (value_low_ref[at:, :], value_ref[...], value_high_ref[: at + block, :])
        scores = []
        for index in range(3):
            lanes = slice(stops[index], stops[index] + keys[index].shape[0])
            scores.append(dot(part, keys[index], ((1,), (1,))) + bias[at // block, :, lanes])
        peak = functools.reduce(jnp.maximum, [jnp.max(s, axis=1, keepdims=True) for s in scores])
        total = jnp.zeros_like(peak)
        mixed = jnp.zeros((block, ATT_DIM), F32)
        for score, value in zip(scores, values):
            weight = jnp.exp2((score - peak) * factor)
            total += jnp.sum(weight, axis=1, keepdims=True)
            mixed += dot(weight.astype(BF16), value)
        out_ref[pl.ds(at, block), :] = mixed / total


def apply_kernel(place_ref, weight_ref, query_ref, attended_ref, *refs):
    hidden = weight_ref.shape[2]
    out_refs, (fresh, scales, rows_buf) = refs[-3 - PARTS : -3], refs[-3:]
    count = (len(refs) - 3 - PARTS) // 2
    mine_refs, other_refs = refs[:count], refs[count : 2 * count]
    piece = mine_refs[0].shape[0]
    core = place_ref[2]
    for head in range(PART_FAST):
        _, offset = window_of(head)
        for index in range(3):
            lanes = slice(index * hidden, (index + 1) * hidden)
            anchor = jnp.full((1, hidden), EPS, F32)
            length = jnp.full((1, hidden), EPS, F32)
            for step in range(count):
                at = pl.multiple_of(place_ref[4 + PARTS + step], 16)
                base = weight_ref[index, pl.ds(at + head * HEAD_DIM, piece), :].astype(F32)
                grad = jnp.where(core == head, mine_refs[step][:, lanes], other_refs[step][:, lanes]).astype(F32)
                update = base + grad
                anchor += jnp.sum(base * base, axis=0, keepdims=True)
                length += jnp.sum(update * update, axis=0, keepdims=True)
                fresh[head, index, pl.ds(at + offset, piece), :] = update.astype(BF16)
            scales[head * 3 + index, :] = (jnp.sqrt(anchor) / jnp.sqrt(length))[0]
            if offset:
                fresh[head, index, :offset, :] = jnp.zeros((offset, hidden), BF16)
            if offset + HEAD_DIM < SPAN:
                fresh[head, index, offset + HEAD_DIM :, :] = jnp.zeros((SPAN - offset - HEAD_DIM, hidden), BF16)
    parts = []
    for head in range(PART_FAST):
        begin, _ = window_of(head)
        query = query_ref[:, begin : begin + SPAN]
        scale = [scales[head * 3 + index : head * 3 + index + 1, :] for index in range(3)]
        gate = dot(query, fresh[head, 0]) * scale[0]
        upward = dot(query, fresh[head, 1]) * (scale[1] * scale[2])
        product = (gate * jax.nn.sigmoid(gate) * upward).astype(BF16)
        parts.append((begin, dot(product, fresh[head, 2], ((1,), (1,)))))
    for lane in range(0, PART_WIDTH, LANES):
        total = attended_ref[:, lane : lane + LANES]
        for begin, value in parts:
            if begin <= lane < begin + SPAN:
                total += value[:, lane - begin : lane - begin + LANES]
        rows_buf[:, lane : lane + LANES] = total.astype(BF16)
    block = out_refs[0].shape[0]
    for index, ref in enumerate(out_refs):
        begin = pl.multiple_of(place_ref[4 + PARTS + count + index] * block, block)
        ref[...] = rows_buf[pl.ds(begin, block), :]


def norm_kernel(place_ref, *refs):
    part_refs, gain_ref, out_ref, buf = refs[:PARTS], refs[PARTS], refs[PARTS + 1], refs[PARTS + 2]
    square = jnp.zeros((out_ref.shape[0], 1), F32)
    for index, ref in enumerate(part_refs):
        rows = ref[...]
        buf[place_ref[4 + index]] = rows
        wide = rows.astype(F32)
        square += jnp.sum(wide * wide, axis=1, keepdims=True)
    factor = lax.rsqrt(square / WIDTH + EPS)
    for part in range(PARTS):
        lanes = slice(part * PART_WIDTH, (part + 1) * PART_WIDTH)
        out_ref[:, lanes] = (buf[part].astype(F32) * factor * gain_ref[:, lanes]).astype(BF16)


def shards(queries, key_rows, value_rows, learn_rates, frame_order, window_ids, fast_init, norm_gain):
    tok_dev = queries.shape[0]
    hidden = fast_init.shape[0]
    sections = lax.axis_size("tok")
    plane_size = PARTS * PART_FAST
    planes = sections // plane_size
    group_rows = tok_dev * PARTS
    groups = planes * PART_FAST
    slots = tok_dev // groups
    half = WINDOW // 2
    assert PART_FAST == 2 and half == group_rows and group_rows & (group_rows - 1) == 0
    group_shift = group_rows.bit_length() - 1

    rank = lax.axis_index("tok")
    plane = rank // plane_size
    part = rank // PART_FAST % PARTS
    core = rank % PART_FAST
    row, column = part // 2, part % 2
    group = plane * PART_FAST + core

    def at(plane, row, column, core):
        return plane * plane_size + (row * 2 + column) * PART_FAST + core

    everyone = [(z, y, x, c) for z in range(planes) for y in range(2) for x in range(2) for c in range(2)]

    def permute(array, target):
        route = []
        for source in everyone:
            goal = target(*source)
            if goal is not None:
                route.append((at(*source), at(*goal)))
        return lax.ppermute(array, "tok", route)

    sources = [2 * (core ^ j // 2) + (column ^ j % 2) for j in range(PARTS)]
    bits = planes.bit_length() - 1
    piece = HEAD_DIM >> bits
    assert planes == 1 << bits and piece << bits == HEAD_DIM and piece % 16 == 0

    def owned(plane):
        return sum((plane >> bit & 1) * (HEAD_DIM >> bit + 1) for bit in range(bits))

    masks = [0]
    for bit in reversed(range(bits)):
        masks += [mask ^ 1 << bit for mask in masks]
    starts = [owned(plane ^ mask) for mask in masks]
    goals = [2 * (column ^ j % 2) + (row ^ j // 2) for j in range(PARTS)]
    place = jnp.stack([rank, part, core, group] + sources + starts + goals).astype(jnp.int32)

    def weight_part():
        own = lax.dynamic_slice_in_dim(fast_init, part * PART_WIDTH, PART_WIDTH, 2)
        return jnp.transpose(own, (1, 2, 0))

    weights = weight_part()

    full = lambda a: pl.BlockSpec(a.shape, lambda h: (0,) * a.ndim)
    cut = pl.BlockSpec((tok_dev, PART_WIDTH), lambda h: (0, h))
    other_cut = pl.BlockSpec((tok_dev, PART_WIDTH), lambda h, place: (0, h ^ place[1]))
    whole = lambda shape: pl.BlockSpec(shape, lambda h, place: (0,) * len(shape))
    heads_out = pl.pallas_call(
        heads_kernel,
        out_shape=[jax.ShapeDtypeStruct((tok_dev, 2 * SPAN), BF16)] * plane_size,
        grid_spec=pltpu.PrefetchScalarGridSpec(
            num_scalar_prefetch=1,
            grid=(PARTS,),
            in_specs=[whole(learn_rates.shape), other_cut, other_cut],
            out_specs=[whole((tok_dev, 2 * SPAN))] * plane_size,
        ),
        compiler_params=pltpu.CompilerParams(vmem_limit_bytes=60 << 20),
        cost_estimate=pl.CostEstimate(flops=tok_dev * WIDTH, bytes_accessed=8 * tok_dev * WIDTH, transcendentals=0),
        name="heads",
    )(place, learn_rates, key_rows, value_rows)
    heads_in = [heads_out[0]]
    for j in range(1, plane_size):
        heads_in.append(permute(heads_out[j], lambda z, y, x, c, j=j: (z, y ^ j >> 2, x ^ j >> 1 & 1, c ^ j & 1)))

    shape = (planes, PARTS, PART_FAST, slots)
    orders = frame_order.reshape(sections, tok_dev)
    kv_out, q_out = call(
        functools.partial(pack_kernel, group_shift, slots),
        [jax.ShapeDtypeStruct(shape + (width,), BF16) for width in (2 * PART_WIDTH, PART_WIDTH)],
        [place, orders, queries, key_rows, value_rows],
        in_specs=[full(orders), cut, cut, cut],
        out_specs=[
            pl.BlockSpec((planes, 1, PART_FAST, slots, width), lambda h: (0, h, 0, 0, 0))
            for width in (2 * PART_WIDTH, PART_WIDTH)
        ],
        grid=(PARTS,),
        scratch=[VMEM((tok_dev, tok_dev), BF16)],
        smem=1, flops=2 * tok_dev * tok_dev * 3 * WIDTH,
    )

    def exchange(array):
        flat = array.reshape(sections, slots, array.shape[-1])
        return lax.all_to_all(flat, "tok", split_axis=0, concat_axis=0, tiled=True).reshape(group_rows, array.shape[-1])

    kv_in = exchange(kv_out)
    q_in = exchange(q_out)

    kv_seq, choose = call(
        functools.partial(place_kernel, group_shift, slots),
        [jax.ShapeDtypeStruct((group_rows, 2 * PART_WIDTH), BF16), jax.ShapeDtypeStruct((group_rows, group_rows), BF16)],
        [place, orders, kv_in], smem=1, flops=2 * group_rows * group_rows * 2 * PART_WIDTH,
    )

    def neighbour(step):
        def target(z, y, x, c):
            goal = z * PART_FAST + c + step
            return (goal // PART_FAST, y, x, goal % PART_FAST) if 0 <= goal < groups else None

        return target

    kv_low = permute(kv_seq, neighbour(1))
    kv_high = permute(kv_seq, neighbour(-1))

    tokens = plane_size * tok_dev
    (total,) = call(
        functools.partial(grads_kernel, tokens // 2),
        [jax.ShapeDtypeStruct((HEAD_DIM, 3 * hidden), BF16)], [place, weights] + heads_in,
        scratch=[VMEM((3, SPAN, hidden), BF16)] + [VMEM((tokens, SPAN), BF16)] * 2 + [VMEM((tokens, hidden), BF16)] * 3,
        smem=1, flops=12 * tokens * HEAD_DIM * hidden,
    )

    def across(bit):
        return lambda z, y, x, c: (z ^ 1 << bit, y, x, c)

    for bit in range(bits):
        size = HEAD_DIM >> bit + 1
        side = plane >> bit & 1
        came = permute(lax.dynamic_slice_in_dim(total, (1 - side) * size, size, 0), across(bit))
        kept = lax.dynamic_slice_in_dim(total, side * size, size, 0)
        total = (kept.astype(F32) + came.astype(F32)).astype(BF16)
    pieces = [total]
    for bit in reversed(range(bits)):
        fresh_pieces = []
        for held in pieces:
            fresh_pieces.append(permute(held, across(bit)))
        pieces += fresh_pieces
    swap = lambda z, y, x, c: (z, y, x, 1 - c)
    pieces_other = []
    for held in pieces:
        pieces_other.append(permute(held, swap))

    block = min(LANES, group_rows)
    lane_block = lambda rows, shift: pl.BlockSpec((rows, ATT_DIM), lambda h: (0, h + shift))
    ids = window_ids.reshape(groups, group_rows)
    attended, query_seq = call(
        functools.partial(attention_kernel, block),
        [jax.ShapeDtypeStruct((group_rows, PART_WIDTH), F32), jax.ShapeDtypeStruct((group_rows, PART_WIDTH), BF16)],
        [place, choose, q_in, ids, kv_seq, kv_low, kv_high, kv_seq, kv_low, kv_high],
        in_specs=[full(choose), lane_block(group_rows, 0), full(ids)]
        + [lane_block(group_rows, 0)] * 3 + [lane_block(group_rows, PART_ATT)] * 3,
        out_specs=[lane_block(group_rows, 0)] * 2,
        grid=(PART_ATT,),
        scratch=[VMEM((group_rows // block, block, WINDOW + block), F32)],
        smem=1, flops=4 * group_rows * (WINDOW + block) * PART_WIDTH,
    )

    blocks = call(
        apply_kernel,
        [jax.ShapeDtypeStruct((tok_dev, PART_WIDTH), BF16)] * PARTS,
        [place, weights, query_seq, attended] + pieces + pieces_other,
        scratch=[
            VMEM((PART_FAST, 3, SPAN, hidden), BF16),
            VMEM((PART_FAST * 3, hidden), F32),
            VMEM((group_rows, PART_WIDTH), BF16),
        ],
        smem=1, flops=6 * group_rows * PART_WIDTH * hidden,
    )

    parts = []
    for j in range(PARTS):
        parts.append(permute(blocks[j], lambda z, y, x, c, j=j: (z, c, x ^ j % 2, y ^ j // 2)))

    (out,) = call(
        norm_kernel,
        [jax.ShapeDtypeStruct((tok_dev, WIDTH), BF16)],
        [place] + parts + [norm_gain.reshape(1, WIDTH)],
        scratch=[VMEM((PARTS, tok_dev, PART_WIDTH), BF16)],
        smem=1, flops=6 * tok_dev * WIDTH,
    )
    return out


def solution(mesh):
    rows = P(("groups", "tok"), None)
    return jax.shard_map(
        shards,
        mesh=mesh,
        in_specs=(rows, rows, rows, rows, P("groups"), P("groups"), P(), P()),
        out_specs=rows,
        check_vma=False,
    )
```

```python
import functools
import math

import jax
import jax.numpy as jnp
from jax import lax
from jax.experimental import pallas as pl
from jax.experimental.pallas import tpu as pltpu
from jax.sharding import PartitionSpec as P


HEADS = 8
HEAD_DIM = 320
ATT_DIM = 128
WINDOW = 1024
WIDTH = 2560
ATT_HEADS = 20
LANES = 128
EPS = 1e-06

PARTS = math.gcd(HEADS, ATT_HEADS)
PART_WIDTH = WIDTH // PARTS
PART_FAST = HEADS // PARTS
PART_ATT = ATT_HEADS // PARTS
SPAN = -(-HEAD_DIM // LANES) * LANES


F32 = jnp.float32
BF16 = jnp.bfloat16
VMEM = pltpu.VMEM


def iota(shape, dim):
    return lax.broadcasted_iota(jnp.int32, shape, dim)


def dot(a, b, dims=((1,), (0,))):
    return lax.dot_general(a, b, (dims, ((), ())), preferred_element_type=F32)


def column_of(row):
    n = row.shape[1]
    square = jnp.broadcast_to(row.astype(F32), (n, n))
    diagonal = iota((n, n), 0) == iota((n, n), 1)
    return jnp.sum(jnp.where(diagonal, square, 0.0), axis=1, keepdims=True)


def call(kernel, outs, ins, scratch=(), smem=0, flops=0, grid=None, in_specs=None, out_specs=None):
    specs = [pl.BlockSpec(memory_space=pltpu.SMEM)] * smem
    specs += in_specs or [pl.BlockSpec(memory_space=VMEM)] * (len(ins) - smem)
    moved = sum(x.size * x.dtype.itemsize for x in list(ins) + list(outs))
    extra = {} if grid is None else {"grid": grid}
    return pl.pallas_call(
        kernel,
        out_shape=list(outs),
        in_specs=specs,
        out_specs=out_specs or [pl.BlockSpec(memory_space=VMEM)] * len(outs),
        scratch_shapes=list(scratch),
        compiler_params=pltpu.CompilerParams(vmem_limit_bytes=60 << 20),
        cost_estimate=pl.CostEstimate(flops=flops, bytes_accessed=moved, transcendentals=0),
        **extra,
    )(*ins)


def window_of(head):
    begin = min(head * HEAD_DIM // LANES * LANES, PART_WIDTH - SPAN)
    return begin, head * HEAD_DIM - begin


def heads_kernel(place_ref, rate_ref, key_ref, value_ref, *out_refs):
    n, width = key_ref.shape
    step, part, core = pl.program_id(0), place_ref[1], place_ref[2]
    rates = rate_ref[...]
    lane = iota((n, SPAN), 1)
    for local in range(width // PART_WIDTH):
        index = step * (width // PART_WIDTH) + local
        own_part = index ^ part
        edge = lax.rem(own_part, width // PART_WIDTH) * PART_WIDTH
        rows = []
        for head in range(PART_FAST):
            begin, offset = window_of(head)

            def window(ref):
                rows = ref[:, pl.ds(pl.multiple_of(edge + begin, LANES), SPAN)].astype(F32)
                rows = pltpu.roll(rows, SPAN - offset, 1) if offset else rows
                return jnp.where(lane < HEAD_DIM, rows, 0.0)

            own = own_part * PART_FAST + head
            rate = jnp.sum(jnp.where(iota(rates.shape, 1) == own, rates, 0.0), axis=1, keepdims=True)
            keys = window(key_ref)
            for third in range(3):
                piece = rate.astype(BF16).astype(F32)
                rate = rate - piece
                keys = jnp.where(lane == HEAD_DIM + third, piece, keys)
            rows.append((keys, window(value_ref)))
        for flip in range(PART_FAST):
            chosen = [jnp.where(core == flip, first, second).astype(BF16) for first, second in zip(*rows)]
            for at in range(local, PARTS, width // PART_WIDTH):
                @pl.when(step == at // (width // PART_WIDTH))
                def _():
                    out_refs[at * PART_FAST + flip][:, :SPAN] = chosen[0]
                    out_refs[at * PART_FAST + flip][:, SPAN:] = chosen[1]


def pack_kernel(group_shift, slots, place_ref, order_ref, query_ref, key_ref, value_ref, out_ref, choose_buf):
    n = query_ref.shape[0]
    planes, parts, cores = out_ref.shape[:3]

    @pl.when(pl.program_id(0) == 0)
    def _():
        pos = order_ref[pl.ds(place_ref[0], 1), :]
        group = lax.shift_right_logical(pos, group_shift)
        group_col = column_of(group).astype(jnp.int32)
        earlier = (group_col == group) & (iota((n, n), 0) < iota((n, n), 1))
        rank = jnp.sum(jnp.where(earlier, 1.0, 0.0), axis=0, keepdims=True)
        slot = group * slots + rank.astype(jnp.int32)
        choose_buf[...] = jnp.where(iota((n, n), 0) == slot, 1.0, 0.0).astype(BF16)

    choose = choose_buf[...]
    for index, ref in enumerate((key_ref, value_ref, query_ref)):
        lanes = slice(index * PART_WIDTH, (index + 1) * PART_WIDTH)
        for part in range(parts):
            rows = dot(choose, ref[:, part * PART_WIDTH : (part + 1) * PART_WIDTH]).astype(BF16)
            for plane in range(planes):
                for core in range(cores):
                    at = (plane * cores + core) * slots
                    out_ref[plane, part, core, :, lanes] = rows[at : at + slots]


def arrival_choice(group_shift, slots, orders, group, n):
    sources, rows = orders.shape
    low_shift = group_shift // 2
    mine = lax.shift_right_logical(orders, group_shift) == group
    before = jnp.where(iota((rows, rows), 0) < iota((rows, rows), 1), 1.0, 0.0).astype(BF16)
    rank = dot(jnp.where(mine, 1.0, 0.0).astype(BF16), before)
    within = orders & ((1 << group_shift) - 1)
    digits = (lax.shift_right_logical(within, low_shift).astype(F32), (within & ((1 << low_shift) - 1)).astype(F32))
    spread = jnp.where(iota((sources, n), 1) // slots == iota((sources, n), 0), 1.0, 0.0).astype(BF16)
    keep = iota((slots, n), 1) % slots == iota((slots, n), 0)
    column = iota((sources, slots), 1)
    pos = jnp.zeros((1, n), F32)
    for digit, weight in zip(digits, (float(1 << low_shift), 1.0)):
        table = jnp.zeros((sources, slots), F32)
        for k in range(slots):
            one = jnp.sum(jnp.where(mine & (rank == float(k)), digit, 0.0), axis=1, keepdims=True)
            table = jnp.where(column == k, one, table)
        wide = dot(table.astype(BF16), spread, ((0,), (0,)))
        pos += weight * jnp.sum(jnp.where(keep, wide, 0.0), axis=0, keepdims=True)
    return jnp.where(iota((n, n), 0) == pos.astype(jnp.int32), 1.0, 0.0).astype(BF16)


def place_kernel(group_shift, slots, place_ref, order_ref, in_ref, kv_ref, q_ref):
    choose = arrival_choice(group_shift, slots, order_ref[...], place_ref[3], in_ref.shape[0])
    kv_ref[...] = dot(choose, in_ref[:, : 2 * PART_WIDTH]).astype(BF16)
    q_ref[...] = dot(choose, in_ref[:, 2 * PART_WIDTH :]).astype(BF16)


def grads_kernel(chunk, place_ref, weight_ref, *refs):
    kv_refs, (send_ref, keep_ref, weight_buf, key_buf, target_buf, dg_buf, du_buf, pr_buf, sums) = refs[:-9], refs[-9:]
    block = kv_refs[0].shape[0]
    n = key_buf.shape[0]
    hidden = weight_ref.shape[2]
    first = pl.multiple_of(place_ref[2] * HEAD_DIM, 16)
    for index in range(3):
        weight_buf[index, :HEAD_DIM, :] = weight_ref[index, pl.ds(first, HEAD_DIM), :]
        weight_buf[index, HEAD_DIM:, :] = jnp.zeros((SPAN - HEAD_DIM, hidden), BF16)
    lane = iota((1, SPAN), 1)
    wanted = (lane >= HEAD_DIM) & (lane < HEAD_DIM + 3)
    for index, ref in enumerate(kv_refs):
        here = pl.ds(index * block, block)
        key = ref[:, :SPAN]
        rate = jnp.sum(jnp.where(wanted, key.astype(F32), 0.0), axis=1, keepdims=True)
        key_buf[here, :] = key
        target_buf[here, :] = (ref[:, SPAN:].astype(F32) * rate).astype(BF16)
    for at in range(0, n, chunk):
        here = pl.ds(at, chunk)
        gate = dot(key_buf[here, :], weight_buf[0])
        upward = dot(key_buf[here, :], weight_buf[1])
        backward = dot(target_buf[here, :], weight_buf[2])
        sigmoid = jax.nn.sigmoid(gate)
        active = gate * sigmoid
        pr_buf[here, :] = (active * upward).astype(BF16)
        du_buf[here, :] = (backward * active).astype(BF16)
        dg_buf[here, :] = (backward * upward * sigmoid * (1.0 + gate * (1.0 - sigmoid))).astype(BF16)
    for index, (left, right) in enumerate(((key_buf, dg_buf), (key_buf, du_buf), (target_buf, pr_buf))):
        total = dot(left[...], right[...], ((0,), (0,)))
        sums[:, index * hidden : (index + 1) * hidden] = total[:HEAD_DIM].astype(BF16)
    half = send_ref.shape[0]
    side = place_ref[3] // PART_FAST & 1
    send_ref[...] = sums[pl.ds(pl.multiple_of((1 - side) * half, 16), half), :]
    keep_ref[...] = sums[pl.ds(pl.multiple_of(side * half, 16), half), :]


def attention_kernel(block, place_ref, query_ref, ids_ref, key_ref, key_low_ref, key_high_ref, value_ref, value_low_ref, value_high_ref, out_ref, bias):
    n = query_ref.shape[0]
    half = WINDOW // 2
    group = place_ref[3]
    last = ids_ref.shape[0] - 1

    @pl.when(pl.program_id(0) == 0)
    def _():
        mid = ids_ref[pl.ds(group, 1), :]
        low = ids_ref[pl.ds(jnp.maximum(group - 1, 0), 1), :]
        high = ids_ref[pl.ds(jnp.minimum(group + 1, last), 1), :]
        low = jnp.where(group > 0, low, -1)
        high = jnp.where(group < last, high, -1)
        for at in range(0, n, block):
            own = column_of(mid[:, at : at + block]).astype(jnp.int32)
            ids = jnp.concatenate([low[:, at:], mid, high[:, : at + block]], axis=1)
            span = ids.shape[1]
            gap = iota((block, span), 1) - iota((block, span), 0) - half
            allowed = (gap < half) & (gap > -half) & (own == ids)
            bias[at // block, :, :] = jnp.where(allowed, 0.0, -1e30)

    factor = ATT_DIM ** (-0.5) * math.log2(math.e)
    for at in range(0, n, block):
        part = query_ref[at : at + block, :]
        stops = (0, half - at, half - at + n, half + n + block - half)
        keys = (key_low_ref[at:, :], key_ref[...], key_high_ref[: at + block, :])
        values = (value_low_ref[at:, :], value_ref[...], value_high_ref[: at + block, :])
        scores = []
        for index in range(3):
            lanes = slice(stops[index], stops[index] + keys[index].shape[0])
            scores.append(dot(part, keys[index], ((1,), (1,))) + bias[at // block, :, lanes])
        peak = functools.reduce(jnp.maximum, [jnp.max(s, axis=1, keepdims=True) for s in scores])
        total = jnp.zeros_like(peak)
        mixed = jnp.zeros((block, ATT_DIM), F32)
        for score, value in zip(scores, values):
            weight = jnp.exp2((score - peak) * factor)
            total += jnp.sum(weight, axis=1, keepdims=True)
            mixed += dot(weight.astype(BF16), value)
        out_ref[pl.ds(at, block), :] = mixed / total


def apply_kernel(place_ref, weight_ref, query_ref, attended_ref, *refs):
    hidden = weight_ref.shape[2]
    out_refs, (fresh, scales, rows_buf) = refs[-3 - PARTS : -3], refs[-3:]
    count = (len(refs) - 3 - PARTS) // 2
    mine_refs, other_refs = refs[:count], refs[count : 2 * count]
    piece = mine_refs[0].shape[0]
    core = place_ref[2]
    for head in range(PART_FAST):
        _, offset = window_of(head)
        for index in range(3):
            lanes = slice(index * hidden, (index + 1) * hidden)
            anchor = jnp.full((1, hidden), EPS, F32)
            length = jnp.full((1, hidden), EPS, F32)
            for step in range(count):
                at = pl.multiple_of(place_ref[4 + PARTS + step], 16)
                base = weight_ref[index, pl.ds(at + head * HEAD_DIM, piece), :].astype(F32)
                grad = jnp.where(core == head, mine_refs[step][:, lanes], other_refs[step][:, lanes]).astype(F32)
                update = base + grad
                anchor += jnp.sum(base * base, axis=0, keepdims=True)
                length += jnp.sum(update * update, axis=0, keepdims=True)
                fresh[head, index, pl.ds(at + offset, piece), :] = update.astype(BF16)
            scales[head * 3 + index, :] = (jnp.sqrt(anchor) / jnp.sqrt(length))[0]
            if offset:
                fresh[head, index, :offset, :] = jnp.zeros((offset, hidden), BF16)
            if offset + HEAD_DIM < SPAN:
                fresh[head, index, offset + HEAD_DIM :, :] = jnp.zeros((SPAN - offset - HEAD_DIM, hidden), BF16)
    parts = []
    for head in range(PART_FAST):
        begin, _ = window_of(head)
        query = query_ref[:, begin : begin + SPAN]
        scale = [scales[head * 3 + index : head * 3 + index + 1, :] for index in range(3)]
        gate = dot(query, fresh[head, 0]) * scale[0]
        upward = dot(query, fresh[head, 1]) * (scale[1] * scale[2])
        product = (gate * jax.nn.sigmoid(gate) * upward).astype(BF16)
        parts.append((begin, dot(product, fresh[head, 2], ((1,), (1,)))))
    for lane in range(0, PART_WIDTH, LANES):
        total = attended_ref[:, lane : lane + LANES]
        for begin, value in parts:
            if begin <= lane < begin + SPAN:
                total += value[:, lane - begin : lane - begin + LANES]
        rows_buf[:, lane : lane + LANES] = total.astype(BF16)
    block = out_refs[0].shape[0]
    for index, ref in enumerate(out_refs):
        begin = pl.multiple_of(place_ref[4 + PARTS + count + index] * block, block)
        ref[...] = rows_buf[pl.ds(begin, block), :]


def norm_kernel(place_ref, *refs):
    part_refs, gain_ref, out_ref, buf = refs[:PARTS], refs[PARTS], refs[PARTS + 1], refs[PARTS + 2]
    square = jnp.zeros((out_ref.shape[0], 1), F32)
    for index, ref in enumerate(part_refs):
        rows = ref[...]
        buf[place_ref[4 + index]] = rows
        wide = rows.astype(F32)
        square += jnp.sum(wide * wide, axis=1, keepdims=True)
    factor = lax.rsqrt(square / WIDTH + EPS)
    for part in range(PARTS):
        lanes = slice(part * PART_WIDTH, (part + 1) * PART_WIDTH)
        out_ref[:, lanes] = (buf[part].astype(F32) * factor * gain_ref[:, lanes]).astype(BF16)


def shards(queries, key_rows, value_rows, learn_rates, frame_order, window_ids, fast_init, norm_gain):
    tok_dev = queries.shape[0]
    hidden = fast_init.shape[0]
    sections = lax.axis_size("tok")
    plane_size = PARTS * PART_FAST
    planes = sections // plane_size
    group_rows = tok_dev * PARTS
    groups = planes * PART_FAST
    slots = tok_dev // groups
    half = WINDOW // 2
    assert PART_FAST == 2 and half == group_rows and group_rows & (group_rows - 1) == 0
    group_shift = group_rows.bit_length() - 1

    rank = lax.axis_index("tok")
    plane = rank // plane_size
    part = rank // PART_FAST % PARTS
    core = rank % PART_FAST
    row, column = part // 2, part % 2
    group = plane * PART_FAST + core

    def at(plane, row, column, core):
        return plane * plane_size + (row * 2 + column) * PART_FAST + core

    everyone = [(z, y, x, c) for z in range(planes) for y in range(2) for x in range(2) for c in range(2)]

    def permute(array, target):
        route = []
        for source in everyone:
            goal = target(*source)
            if goal is not None:
                route.append((at(*source), at(*goal)))
        return lax.ppermute(array, "tok", route)

    sources = [2 * (core ^ j // 2) + (column ^ j % 2) for j in range(PARTS)]
    bits = planes.bit_length() - 1
    piece = HEAD_DIM >> bits
    assert planes == 1 << bits and piece << bits == HEAD_DIM and piece % 16 == 0

    def owned(plane):
        return sum((plane >> bit & 1) * (HEAD_DIM >> bit + 1) for bit in range(bits))

    masks = [0]
    for bit in reversed(range(bits)):
        masks += [mask ^ 1 << bit for mask in masks]
    starts = [owned(plane ^ mask) for mask in masks]
    goals = [2 * (column ^ j % 2) + (row ^ j // 2) for j in range(PARTS)]
    place = jnp.stack([rank, part, core, group] + sources + starts + goals).astype(jnp.int32)

    def weight_part():
        own = lax.dynamic_slice_in_dim(fast_init, part * PART_WIDTH, PART_WIDTH, 2)
        return jnp.transpose(own, (1, 2, 0))

    weights = weight_part()

    full = lambda a: pl.BlockSpec(a.shape, lambda h: (0,) * a.ndim)
    steps = 2
    together = PARTS // steps
    other_cut = pl.BlockSpec((tok_dev, WIDTH // steps), lambda h, place: (0, h ^ place[1] // together))
    whole = lambda shape: pl.BlockSpec(shape, lambda h, place: (0,) * len(shape))
    heads_out = pl.pallas_call(
        heads_kernel,
        out_shape=[jax.ShapeDtypeStruct((tok_dev, 2 * SPAN), BF16)] * plane_size,
        grid_spec=pltpu.PrefetchScalarGridSpec(
            num_scalar_prefetch=1,
            grid=(steps,),
            in_specs=[whole(learn_rates.shape), other_cut, other_cut],
            out_specs=[whole((tok_dev, 2 * SPAN))] * plane_size,
        ),
        compiler_params=pltpu.CompilerParams(vmem_limit_bytes=60 << 20),
        cost_estimate=pl.CostEstimate(flops=tok_dev * WIDTH, bytes_accessed=8 * tok_dev * WIDTH, transcendentals=0),
        name="heads",
    )(place, learn_rates, key_rows, value_rows)
    heads_in = [heads_out[0]]
    for j in range(1, plane_size):
        heads_in.append(permute(heads_out[j], lambda z, y, x, c, j=j: (z, y ^ j >> 2, x ^ j >> 1 & 1, c ^ j & 1)))

    orders = frame_order.reshape(sections, tok_dev)
    cut = pl.BlockSpec((tok_dev, WIDTH // steps), lambda h: (0, h))
    (packed,) = call(
        functools.partial(pack_kernel, group_shift, slots),
        [jax.ShapeDtypeStruct((planes, PARTS, PART_FAST, slots, 3 * PART_WIDTH), BF16)],
        [place, orders, queries, key_rows, value_rows],
        in_specs=[full(orders), cut, cut, cut],
        out_specs=[pl.BlockSpec((planes, together, PART_FAST, slots, 3 * PART_WIDTH), lambda h: (0, h, 0, 0, 0))],
        grid=(steps,),
        scratch=[VMEM((tok_dev, tok_dev), BF16)],
        smem=1, flops=2 * tok_dev * tok_dev * 3 * WIDTH,
    )
    arrived = lax.all_to_all(
        packed.reshape(sections, slots, 3 * PART_WIDTH), "tok", split_axis=0, concat_axis=0, tiled=True
    ).reshape(group_rows, 3 * PART_WIDTH)

    kv_seq, query_seq = call(
        functools.partial(place_kernel, group_shift, slots),
        [jax.ShapeDtypeStruct((group_rows, width), BF16) for width in (2 * PART_WIDTH, PART_WIDTH)],
        [place, orders, arrived], smem=1, flops=2 * group_rows * group_rows * 3 * PART_WIDTH,
    )

    def neighbour(step):
        def target(z, y, x, c):
            goal = z * PART_FAST + c + step
            return (goal // PART_FAST, y, x, goal % PART_FAST) if 0 <= goal < groups else None

        return target

    kv_low = permute(kv_seq, neighbour(1))
    kv_high = permute(kv_seq, neighbour(-1))

    tokens = plane_size * tok_dev
    send, keep = call(
        functools.partial(grads_kernel, tokens // 2),
        [jax.ShapeDtypeStruct((HEAD_DIM // 2, 3 * hidden), BF16)] * 2, [place, weights] + heads_in,
        scratch=[VMEM((3, SPAN, hidden), BF16)] + [VMEM((tokens, SPAN), BF16)] * 2
        + [VMEM((tokens, hidden), BF16)] * 3 + [VMEM((HEAD_DIM, 3 * hidden), BF16)],
        smem=1, flops=12 * tokens * HEAD_DIM * hidden,
    )

    def across(bit):
        return lambda z, y, x, c: (z ^ 1 << bit, y, x, c)

    def added(first, second):
        return (first.astype(F32) + second.astype(F32)).astype(BF16)

    for bit in range(bits):
        came = permute(send, across(bit))
        if bit + 1 < bits:
            size = HEAD_DIM >> bit + 2
            side = plane >> bit + 1 & 1
            cuts = [[lax.dynamic_slice_in_dim(a, at * size, size, 0) for a in (keep, came)] for at in (1 - side, side)]
            send = added(*cuts[0])
            keep = added(*cuts[1])
        else:
            total = added(keep, came)
    pieces = [total]
    for bit in reversed(range(bits)):
        fresh_pieces = []
        for held in pieces:
            fresh_pieces.append(permute(held, across(bit)))
        pieces += fresh_pieces
    swap = lambda z, y, x, c: (z, y, x, 1 - c)
    pieces_other = []
    for held in pieces:
        pieces_other.append(permute(held, swap))

    block = min(LANES, group_rows)
    lane_block = lambda rows, shift: pl.BlockSpec((rows, ATT_DIM), lambda h: (0, h + shift))
    ids = window_ids.reshape(groups, group_rows)
    (attended,) = call(
        functools.partial(attention_kernel, block),
        [jax.ShapeDtypeStruct((group_rows, PART_WIDTH), F32)],
        [place, query_seq, ids, kv_seq, kv_low, kv_high, kv_seq, kv_low, kv_high],
        in_specs=[lane_block(group_rows, 0), full(ids)]
        + [lane_block(group_rows, 0)] * 3 + [lane_block(group_rows, PART_ATT)] * 3,
        out_specs=[lane_block(group_rows, 0)],
        grid=(PART_ATT,),
        scratch=[VMEM((group_rows // block, block, WINDOW + block), F32)],
        smem=1, flops=4 * group_rows * (WINDOW + block) * PART_WIDTH,
    )

    blocks = call(
        apply_kernel,
        [jax.ShapeDtypeStruct((tok_dev, PART_WIDTH), BF16)] * PARTS,
        [place, weights, query_seq, attended] + pieces + pieces_other,
        scratch=[
            VMEM((PART_FAST, 3, SPAN, hidden), BF16),
            VMEM((PART_FAST * 3, hidden), F32),
            VMEM((group_rows, PART_WIDTH), BF16),
        ],
        smem=1, flops=6 * group_rows * PART_WIDTH * hidden,
    )

    parts = []
    for j in range(PARTS):
        parts.append(permute(blocks[j], lambda z, y, x, c, j=j: (z, c, x ^ j % 2, y ^ j // 2)))

    (out,) = call(
        norm_kernel,
        [jax.ShapeDtypeStruct((tok_dev, WIDTH), BF16)],
        [place] + parts + [norm_gain.reshape(1, WIDTH)],
        scratch=[VMEM((PARTS, tok_dev, PART_WIDTH), BF16)],
        smem=1, flops=6 * tok_dev * WIDTH,
    )
    return out


def solution(mesh):
    rows = P(("groups", "tok"), None)
    return jax.shard_map(
        shards,
        mesh=mesh,
        in_specs=(rows, rows, rows, rows, P("groups"), P("groups"), P(), P()),
        out_specs=rows,
        check_vma=False,
    )
```

```python
import functools
import math

import jax
import jax.numpy as jnp
from jax import lax
from jax.experimental import pallas as pl
from jax.experimental.pallas import tpu as pltpu
from jax.sharding import PartitionSpec as P


HEADS = 8
HEAD_DIM = 320
ATT_DIM = 128
WINDOW = 1024
WIDTH = 2560
ATT_HEADS = 20
LANES = 128
EPS = 1e-06

PARTS = math.gcd(HEADS, ATT_HEADS)
PART_WIDTH = WIDTH // PARTS
PART_FAST = HEADS // PARTS
PART_ATT = ATT_HEADS // PARTS
SPAN = -(-HEAD_DIM // LANES) * LANES


F32 = jnp.float32
BF16 = jnp.bfloat16
VMEM = pltpu.VMEM


def iota(shape, dim):
    return lax.broadcasted_iota(jnp.int32, shape, dim)


def dot(a, b, dims=((1,), (0,))):
    return lax.dot_general(a, b, (dims, ((), ())), preferred_element_type=F32)


def column_of(row):
    n = row.shape[1]
    square = jnp.broadcast_to(row.astype(F32), (n, n))
    diagonal = iota((n, n), 0) == iota((n, n), 1)
    return jnp.sum(jnp.where(diagonal, square, 0.0), axis=1, keepdims=True)


def call(kernel, outs, ins, scratch=(), smem=0, flops=0, grid=None, in_specs=None, out_specs=None):
    specs = [pl.BlockSpec(memory_space=pltpu.SMEM)] * smem
    specs += in_specs or [pl.BlockSpec(memory_space=VMEM)] * (len(ins) - smem)
    moved = sum(x.size * x.dtype.itemsize for x in list(ins) + list(outs))
    extra = {} if grid is None else {"grid": grid}
    return pl.pallas_call(
        kernel,
        out_shape=list(outs),
        in_specs=specs,
        out_specs=out_specs or [pl.BlockSpec(memory_space=VMEM)] * len(outs),
        scratch_shapes=list(scratch),
        compiler_params=pltpu.CompilerParams(vmem_limit_bytes=60 << 20),
        cost_estimate=pl.CostEstimate(flops=flops, bytes_accessed=moved, transcendentals=0),
        **extra,
    )(*ins)


def window_of(head):
    begin = min(head * HEAD_DIM // LANES * LANES, PART_WIDTH - SPAN)
    return begin, head * HEAD_DIM - begin


def heads_kernel(place_ref, rate_ref, key_ref, value_ref, *out_refs):
    n, width = key_ref.shape
    step, part, core = pl.program_id(0), place_ref[1], place_ref[2]
    lane = iota((n, SPAN), 1)
    for local in range(width // PART_WIDTH):
        index = step * (width // PART_WIDTH) + local
        own_part = index ^ part
        edge = lax.rem(own_part, width // PART_WIDTH) * PART_WIDTH
        rows = []
        for head in range(PART_FAST):
            begin, offset = window_of(head)

            def window(ref):
                rows = ref[:, pl.ds(pl.multiple_of(edge + begin, LANES), SPAN)].astype(F32)
                rows = pltpu.roll(rows, SPAN - offset, 1) if offset else rows
                return jnp.where(lane < HEAD_DIM, rows, 0.0)

            rate = column_of(rate_ref[pl.ds(own_part * PART_FAST + head, 1), :])
            keys = window(key_ref)
            for third in range(3):
                piece = rate.astype(BF16).astype(F32)
                rate = rate - piece
                keys = jnp.where(lane == HEAD_DIM + third, piece, keys)
            rows.append((keys, window(value_ref)))
        for flip in range(PART_FAST):
            chosen = [jnp.where(core == flip, first, second).astype(BF16) for first, second in zip(*rows)]
            for at in range(local, PARTS, width // PART_WIDTH):
                @pl.when(step == at // (width // PART_WIDTH))
                def _():
                    out_refs[at * PART_FAST + flip][:, :SPAN] = chosen[0]
                    out_refs[at * PART_FAST + flip][:, SPAN:] = chosen[1]


def pack_kernel(group_shift, slots, place_ref, order_ref, query_ref, key_ref, value_ref, out_ref, choose_buf):
    n = query_ref.shape[0]
    planes, parts, cores = out_ref.shape[:3]

    @pl.when(pl.program_id(0) == 0)
    def _():
        pos = order_ref[pl.ds(place_ref[0], 1), :]
        group = lax.shift_right_logical(pos, group_shift)
        group_col = column_of(group).astype(jnp.int32)
        earlier = (group_col == group) & (iota((n, n), 0) < iota((n, n), 1))
        rank = jnp.sum(jnp.where(earlier, 1.0, 0.0), axis=0, keepdims=True)
        slot = group * slots + rank.astype(jnp.int32)
        choose_buf[...] = jnp.where(iota((n, n), 0) == slot, 1.0, 0.0).astype(BF16)

    choose = choose_buf[...]
    for index, ref in enumerate((key_ref, value_ref, query_ref)):
        lanes = slice(index * PART_WIDTH, (index + 1) * PART_WIDTH)
        for part in range(parts):
            rows = dot(choose, ref[:, part * PART_WIDTH : (part + 1) * PART_WIDTH]).astype(BF16)
            for plane in range(planes):
                for core in range(cores):
                    at = (plane * cores + core) * slots
                    out_ref[plane, part, core, :, lanes] = rows[at : at + slots]


def arrival_choice(group_shift, slots, orders, group, n):
    sources, rows = orders.shape
    low_shift = group_shift // 2
    mine = lax.shift_right_logical(orders, group_shift) == group
    before = jnp.where(iota((rows, rows), 0) < iota((rows, rows), 1), 1.0, 0.0).astype(BF16)
    rank = dot(jnp.where(mine, 1.0, 0.0).astype(BF16), before)
    within = orders & ((1 << group_shift) - 1)
    digits = (lax.shift_right_logical(within, low_shift).astype(F32), (within & ((1 << low_shift) - 1)).astype(F32))
    spread = jnp.where(iota((sources, n), 1) // slots == iota((sources, n), 0), 1.0, 0.0).astype(BF16)
    keep = iota((slots, n), 1) % slots == iota((slots, n), 0)
    column = iota((sources, slots), 1)
    pos = jnp.zeros((1, n), F32)
    for digit, weight in zip(digits, (float(1 << low_shift), 1.0)):
        table = jnp.zeros((sources, slots), F32)
        for k in range(slots):
            one = jnp.sum(jnp.where(mine & (rank == float(k)), digit, 0.0), axis=1, keepdims=True)
            table = jnp.where(column == k, one, table)
        wide = dot(table.astype(BF16), spread, ((0,), (0,)))
        pos += weight * jnp.sum(jnp.where(keep, wide, 0.0), axis=0, keepdims=True)
    return jnp.where(iota((n, n), 0) == pos.astype(jnp.int32), 1.0, 0.0).astype(BF16)


def choose_kernel(group_shift, slots, place_ref, order_ref, choose_ref):
    choose_ref[...] = arrival_choice(group_shift, slots, order_ref[...], place_ref[3], choose_ref.shape[0])


def place_kernel(choose_ref, in_ref, kv_ref, q_ref):
    choose = choose_ref[...]
    kv_ref[...] = dot(choose, in_ref[:, : 2 * PART_WIDTH]).astype(BF16)
    q_ref[...] = dot(choose, in_ref[:, 2 * PART_WIDTH :]).astype(BF16)


def grads_kernel(chunk, last, place_ref, weight_ref, *refs):
    outs = 2 if last else 1
    weight_buf, key_buf, target_buf, delta_buf, pr_buf, sums = refs[-6:]
    out_refs, in_refs = refs[-6 - outs : -6], refs[: -6 - outs]
    kv_refs, early_ref = (in_refs[:-1], in_refs[-1]) if last else (in_refs, None)
    block = kv_refs[0].shape[0]
    n = key_buf.shape[0]
    hidden = weight_ref.shape[2]
    first = pl.multiple_of(place_ref[2] * HEAD_DIM, 16)
    for index in range(3):
        lanes = slice(index * hidden, (index + 1) * hidden)
        weight_buf[:HEAD_DIM, lanes] = weight_ref[index, pl.ds(first, HEAD_DIM), :]
    weight_buf[HEAD_DIM:, :] = jnp.zeros((SPAN - HEAD_DIM, 3 * hidden), BF16)
    lane = iota((1, SPAN), 1)
    wanted = (lane >= HEAD_DIM) & (lane < HEAD_DIM + 3)
    for index, ref in enumerate(kv_refs):
        here = pl.ds(index * block, block)
        key = ref[:, :SPAN]
        rate = jnp.sum(jnp.where(wanted, key.astype(F32), 0.0), axis=1, keepdims=True)
        key_buf[here, :] = key
        target_buf[here, :] = (ref[:, SPAN:].astype(F32) * rate).astype(BF16)
    for at in range(0, n, chunk):
        here = pl.ds(at, chunk)
        both = dot(key_buf[here, :], weight_buf[:, : 2 * hidden])
        gate, upward = both[:, :hidden], both[:, hidden:]
        backward = dot(target_buf[here, :], weight_buf[:, 2 * hidden :])
        sigmoid = jax.nn.sigmoid(gate)
        active = gate * sigmoid
        pr_buf[here, :] = (active * upward).astype(BF16)
        delta_buf[here, hidden:] = (backward * active).astype(BF16)
        delta_buf[here, :hidden] = (backward * upward * sigmoid * (1.0 + gate * (1.0 - sigmoid))).astype(BF16)
    for left, right, begin in ((key_buf, delta_buf, 0), (target_buf, pr_buf, 2 * hidden)):
        lanes = slice(begin, begin + right.shape[1])
        total = dot(left[...], right[...], ((0,), (0,)))[:HEAD_DIM]
        if last:
            sums[:, lanes] = (total + early_ref[:, lanes].astype(F32)).astype(BF16)
        else:
            out_refs[0][:, lanes] = total.astype(BF16)
    if last:
        half = out_refs[0].shape[0]
        side = place_ref[3] // PART_FAST & 1
        out_refs[0][...] = sums[pl.ds(pl.multiple_of((1 - side) * half, 16), half), :]
        out_refs[1][...] = sums[pl.ds(pl.multiple_of(side * half, 16), half), :]


FACTOR = ATT_DIM ** (-0.5) * math.log2(math.e)


def near_kernel(block, place_ref, query_ref, ids_ref, key_ref, value_ref, out_ref, stat_ref, bias):
    n = query_ref.shape[0]
    head = pl.program_id(0)

    @pl.when(head == 0)
    def _():
        ids = ids_ref[pl.ds(place_ref[3], 1), :]
        for at in range(0, n, block):
            own = column_of(ids[:, at : at + block]).astype(jnp.int32)
            gap = iota((block, n), 1) - iota((block, n), 0) - at
            allowed = (gap < WINDOW // 2) & (gap > -(WINDOW // 2)) & (own == ids)
            bias[at : at + block, :] = jnp.where(allowed, 0.0, -1e30)
        stat_ref[...] = jnp.zeros_like(stat_ref)

    lane = iota((block, LANES), 1)
    for at in range(0, n, block):
        here = slice(at, at + block)
        score = dot(query_ref[here, :], key_ref[...], ((1,), (1,))) + bias[here, :]
        peak = jnp.max(score, axis=1, keepdims=True)
        weight = jnp.exp2((score - peak) * FACTOR)
        total = jnp.sum(weight, axis=1, keepdims=True)
        out_ref[here, :] = dot(weight.astype(BF16), value_ref[...])
        stat = jnp.where(lane == 2 * head, peak, stat_ref[here, :])
        stat_ref[here, :] = jnp.where(lane == 2 * head + 1, total, stat)


def far_kernel(block, place_ref, query_ref, ids_ref, near_ref, stat_ref, key_low_ref, key_high_ref, value_low_ref, value_high_ref, out_ref, bias):
    n = query_ref.shape[0]
    half = WINDOW // 2
    head = pl.program_id(0)
    group = place_ref[3]
    last = ids_ref.shape[0] - 1

    @pl.when(head == 0)
    def _():
        mid = ids_ref[pl.ds(group, 1), :]
        low = jnp.where(group > 0, ids_ref[pl.ds(jnp.maximum(group - 1, 0), 1), :], -1)
        high = jnp.where(group < last, ids_ref[pl.ds(jnp.minimum(group + 1, last), 1), :], -1)
        for at in range(0, n, block):
            own = column_of(mid[:, at : at + block]).astype(jnp.int32)
            for ids, begin, end, shift in ((low, at, n, -n), (high, 0, at + block, n)):
                size = end - begin
                gap = iota((block, size), 1) + (begin + shift - at) - iota((block, size), 0)
                allowed = (gap < half) & (gap > -half) & (own == ids[:, begin:end])
                lanes = slice(begin - at, end - at) if shift < 0 else slice(n - at, n - at + size)
                bias[at : at + block, lanes] = jnp.where(allowed, 0.0, -1e30)

    lane = iota((block, LANES), 1)
    for at in range(0, n, block):
        here = slice(at, at + block)
        query = query_ref[here, :]
        low = dot(query, key_low_ref[at:, :], ((1,), (1,))) + bias[here, : n - at]
        high = dot(query, key_high_ref[: at + block, :], ((1,), (1,))) + bias[here, n - at :]
        stat = stat_ref[here, :]
        old_peak = jnp.sum(jnp.where(lane == 2 * head, stat, 0.0), axis=1, keepdims=True)
        old_total = jnp.sum(jnp.where(lane == 2 * head + 1, stat, 0.0), axis=1, keepdims=True)
        peak = jnp.maximum(jnp.max(low, axis=1, keepdims=True), jnp.max(high, axis=1, keepdims=True))
        peak = jnp.maximum(peak, old_peak)
        keep = jnp.exp2((old_peak - peak) * FACTOR)
        low = jnp.exp2((low - peak) * FACTOR)
        high = jnp.exp2((high - peak) * FACTOR)
        total = old_total * keep + jnp.sum(low, axis=1, keepdims=True) + jnp.sum(high, axis=1, keepdims=True)
        mixed = near_ref[here, :] * keep + dot(low.astype(BF16), value_low_ref[at:, :])
        mixed += dot(high.astype(BF16), value_high_ref[: at + block, :])
        out_ref[here, :] = mixed / total


def apply_kernel(place_ref, weight_ref, query_ref, attended_ref, *refs):
    hidden = weight_ref.shape[2]
    out_refs, (fresh, scales, rows_buf) = refs[-3 - PARTS : -3], refs[-3:]
    count = (len(refs) - 3 - PARTS) // 2
    mine_refs, other_refs = refs[:count], refs[count : 2 * count]
    piece = mine_refs[0].shape[0]
    core = place_ref[2]
    for head in range(PART_FAST):
        _, offset = window_of(head)
        for index in range(3):
            lanes = slice(index * hidden, (index + 1) * hidden)
            anchor = jnp.full((1, hidden), EPS, F32)
            length = jnp.full((1, hidden), EPS, F32)
            for step in range(count):
                at = pl.multiple_of(place_ref[4 + PARTS + step], 16)
                base = weight_ref[index, pl.ds(at + head * HEAD_DIM, piece), :].astype(F32)
                grad = jnp.where(core == head, mine_refs[step][:, lanes], other_refs[step][:, lanes]).astype(F32)
                update = base + grad
                anchor += jnp.sum(base * base, axis=0, keepdims=True)
                length += jnp.sum(update * update, axis=0, keepdims=True)
                fresh[head, index, pl.ds(at + offset, piece), :] = update.astype(BF16)
            scales[head * 3 + index, :] = (jnp.sqrt(anchor) / jnp.sqrt(length))[0]
            if offset:
                fresh[head, index, :offset, :] = jnp.zeros((offset, hidden), BF16)
            if offset + HEAD_DIM < SPAN:
                fresh[head, index, offset + HEAD_DIM :, :] = jnp.zeros((SPAN - offset - HEAD_DIM, hidden), BF16)
    parts = []
    for head in range(PART_FAST):
        begin, _ = window_of(head)
        query = query_ref[:, begin : begin + SPAN]
        scale = [scales[head * 3 + index : head * 3 + index + 1, :] for index in range(3)]
        gate = dot(query, fresh[head, 0]) * scale[0]
        upward = dot(query, fresh[head, 1]) * (scale[1] * scale[2])
        product = (gate * jax.nn.sigmoid(gate) * upward).astype(BF16)
        parts.append((begin, dot(product, fresh[head, 2], ((1,), (1,)))))
    for lane in range(0, PART_WIDTH, LANES):
        total = attended_ref[:, lane : lane + LANES]
        for begin, value in parts:
            if begin <= lane < begin + SPAN:
                total += value[:, lane - begin : lane - begin + LANES]
        rows_buf[:, lane : lane + LANES] = total.astype(BF16)
    block = out_refs[0].shape[0]
    for index, ref in enumerate(out_refs):
        begin = pl.multiple_of(place_ref[4 + PARTS + count + index] * block, block)
        ref[...] = rows_buf[pl.ds(begin, block), :]


def norm_kernel(place_ref, *refs):
    part_refs, gain_ref, out_ref, buf = refs[:PARTS], refs[PARTS], refs[PARTS + 1], refs[PARTS + 2]
    square = jnp.zeros((out_ref.shape[0], 1), F32)
    for index, ref in enumerate(part_refs):
        rows = ref[...]
        buf[place_ref[4 + index]] = rows
        wide = rows.astype(F32)
        square += jnp.sum(wide * wide, axis=1, keepdims=True)
    factor = lax.rsqrt(square / WIDTH + EPS)
    for part in range(PARTS):
        lanes = slice(part * PART_WIDTH, (part + 1) * PART_WIDTH)
        out_ref[:, lanes] = (buf[part].astype(F32) * factor * gain_ref[:, lanes]).astype(BF16)


def shards(queries, key_rows, value_rows, learn_rates, frame_order, window_ids, fast_init, norm_gain):
    tok_dev = queries.shape[0]
    hidden = fast_init.shape[0]
    sections = lax.axis_size("tok")
    plane_size = PARTS * PART_FAST
    planes = sections // plane_size
    group_rows = tok_dev * PARTS
    groups = planes * PART_FAST
    slots = tok_dev // groups
    half = WINDOW // 2
    assert PART_FAST == 2 and half == group_rows and group_rows & (group_rows - 1) == 0
    group_shift = group_rows.bit_length() - 1

    rank = lax.axis_index("tok")
    plane = rank // plane_size
    part = rank // PART_FAST % PARTS
    core = rank % PART_FAST
    row, column = part // 2, part % 2
    group = plane * PART_FAST + core

    def at(plane, row, column, core):
        return plane * plane_size + (row * 2 + column) * PART_FAST + core

    everyone = [(z, y, x, c) for z in range(planes) for y in range(2) for x in range(2) for c in range(2)]

    def permute(array, target):
        route = []
        for source in everyone:
            goal = target(*source)
            if goal is not None:
                route.append((at(*source), at(*goal)))
        return lax.ppermute(array, "tok", route)

    sources = [2 * (core ^ j // 2) + (column ^ j % 2) for j in range(PARTS)]
    bits = planes.bit_length() - 1
    piece = HEAD_DIM >> bits
    assert planes == 1 << bits and piece << bits == HEAD_DIM and piece % 16 == 0

    def owned(plane):
        return sum((plane >> bit & 1) * (HEAD_DIM >> bit + 1) for bit in range(bits))

    masks = [0]
    for bit in reversed(range(bits)):
        masks += [mask ^ 1 << bit for mask in masks]
    starts = [owned(plane ^ mask) for mask in masks]
    goals = [2 * (column ^ j % 2) + (row ^ j // 2) for j in range(PARTS)]
    place = jnp.stack([rank, part, core, group] + sources + starts + goals).astype(jnp.int32)

    def weight_part():
        own = lax.dynamic_slice_in_dim(fast_init, part * PART_WIDTH, PART_WIDTH, 2)
        return jnp.transpose(own, (1, 2, 0))

    weights = weight_part()

    full = lambda a: pl.BlockSpec(a.shape, lambda h: (0,) * a.ndim)
    steps = 2
    together = PARTS // steps
    other_cut = pl.BlockSpec((tok_dev, WIDTH // steps), lambda h, place: (0, h ^ place[1] // together))
    whole = lambda shape: pl.BlockSpec(shape, lambda h, place: (0,) * len(shape))
    heads_out = pl.pallas_call(
        heads_kernel,
        out_shape=[jax.ShapeDtypeStruct((tok_dev, 2 * SPAN), BF16)] * plane_size,
        grid_spec=pltpu.PrefetchScalarGridSpec(
            num_scalar_prefetch=1,
            grid=(steps,),
            in_specs=[whole(learn_rates.shape[::-1]), other_cut, other_cut],
            out_specs=[whole((tok_dev, 2 * SPAN))] * plane_size,
        ),
        compiler_params=pltpu.CompilerParams(vmem_limit_bytes=60 << 20),
        cost_estimate=pl.CostEstimate(flops=tok_dev * WIDTH, bytes_accessed=8 * tok_dev * WIDTH, transcendentals=0),
        name="heads",
    )(place, learn_rates.T, key_rows, value_rows)
    heads_in = [heads_out[0]]
    for j in range(1, plane_size):
        heads_in.append(permute(heads_out[j], lambda z, y, x, c, j=j: (z, y ^ j >> 2, x ^ j >> 1 & 1, c ^ j & 1)))

    orders = frame_order.reshape(sections, tok_dev)
    cut = pl.BlockSpec((tok_dev, WIDTH // steps), lambda h: (0, h))
    (packed,) = call(
        functools.partial(pack_kernel, group_shift, slots),
        [jax.ShapeDtypeStruct((planes, PARTS, PART_FAST, slots, 3 * PART_WIDTH), BF16)],
        [place, orders, queries, key_rows, value_rows],
        in_specs=[full(orders), cut, cut, cut],
        out_specs=[pl.BlockSpec((planes, together, PART_FAST, slots, 3 * PART_WIDTH), lambda h: (0, h, 0, 0, 0))],
        grid=(steps,),
        scratch=[VMEM((tok_dev, tok_dev), BF16)],
        smem=1, flops=2 * tok_dev * tok_dev * 3 * WIDTH,
    )
    arrived = lax.all_to_all(
        packed.reshape(sections, slots, 3 * PART_WIDTH), "tok", split_axis=0, concat_axis=0, tiled=True
    ).reshape(group_rows, 3 * PART_WIDTH)

    (choose,) = call(
        functools.partial(choose_kernel, group_shift, slots),
        [jax.ShapeDtypeStruct((group_rows, group_rows), BF16)],
        [place, orders], smem=1, flops=2 * group_rows * group_rows,
    )
    kv_seq, query_seq = call(
        place_kernel,
        [jax.ShapeDtypeStruct((group_rows, width), BF16) for width in (2 * PART_WIDTH, PART_WIDTH)],
        [choose, arrived], flops=2 * group_rows * group_rows * 3 * PART_WIDTH,
    )

    def neighbour(step):
        def target(z, y, x, c):
            goal = z * PART_FAST + c + step
            return (goal // PART_FAST, y, x, goal % PART_FAST) if 0 <= goal < groups else None

        return target

    kv_low = permute(kv_seq, neighbour(1))
    kv_high = permute(kv_seq, neighbour(-1))

    near = plane_size // 2
    tokens = near * tok_dev
    grad_scratch = [VMEM((SPAN, 3 * hidden), BF16)] + [VMEM((tokens, SPAN), BF16)] * 2
    grad_scratch += [VMEM((tokens, 2 * hidden), BF16), VMEM((tokens, hidden), BF16), VMEM((HEAD_DIM, 3 * hidden), BF16)]
    grad_flops = 12 * tokens * HEAD_DIM * hidden
    (early,) = call(
        functools.partial(grads_kernel, tokens, False),
        [jax.ShapeDtypeStruct((HEAD_DIM, 3 * hidden), BF16)], [place, weights] + heads_in[:near],
        scratch=grad_scratch, smem=1, flops=grad_flops,
    )
    send, keep = call(
        functools.partial(grads_kernel, tokens, True),
        [jax.ShapeDtypeStruct((HEAD_DIM // 2, 3 * hidden), BF16)] * 2,
        [place, weights] + heads_in[near:] + [early],
        scratch=grad_scratch, smem=1, flops=grad_flops,
    )

    def across(bit):
        return lambda z, y, x, c: (z ^ 1 << bit, y, x, c)

    def added(first, second):
        return (first.astype(F32) + second.astype(F32)).astype(BF16)

    for bit in range(bits):
        came = permute(send, across(bit))
        if bit + 1 < bits:
            size = HEAD_DIM >> bit + 2
            side = plane >> bit + 1 & 1
            cuts = [[lax.dynamic_slice_in_dim(a, at * size, size, 0) for a in (keep, came)] for at in (1 - side, side)]
            send = added(*cuts[0])
            keep = added(*cuts[1])
        else:
            total = added(keep, came)
    pieces = [total]
    for bit in reversed(range(bits)):
        fresh_pieces = []
        for held in pieces:
            fresh_pieces.append(permute(held, across(bit)))
        pieces += fresh_pieces
    swap = lambda z, y, x, c: (z, y, x, 1 - c)
    pieces_other = []
    for held in pieces:
        pieces_other.append(permute(held, swap))

    block = min(LANES, group_rows)
    lane_block = lambda rows, shift: pl.BlockSpec((rows, ATT_DIM), lambda h: (0, h + shift))
    ids = window_ids.reshape(groups, group_rows)
    wide = jax.ShapeDtypeStruct((group_rows, PART_WIDTH), F32)
    stat_shape = jax.ShapeDtypeStruct((group_rows, LANES), F32)
    assert block + group_rows == WINDOW // 2 + block and 2 * PART_ATT <= LANES
    near_mixed, stats = call(
        functools.partial(near_kernel, block),
        [wide, stat_shape],
        [place, query_seq, ids, kv_seq, kv_seq],
        in_specs=[lane_block(group_rows, 0), full(ids), lane_block(group_rows, 0), lane_block(group_rows, PART_ATT)],
        out_specs=[lane_block(group_rows, 0), full(stat_shape)],
        grid=(PART_ATT,), scratch=[VMEM((group_rows, group_rows), F32)],
        smem=1, flops=4 * group_rows * group_rows * PART_WIDTH,
    )
    (attended,) = call(
        functools.partial(far_kernel, block),
        [wide],
        [place, query_seq, ids, near_mixed, stats, kv_low, kv_high, kv_low, kv_high],
        in_specs=[lane_block(group_rows, 0), full(ids), lane_block(group_rows, 0), full(stats)]
        + [lane_block(group_rows, 0)] * 2 + [lane_block(group_rows, PART_ATT)] * 2,
        out_specs=[lane_block(group_rows, 0)],
        grid=(PART_ATT,), scratch=[VMEM((group_rows, group_rows + block), F32)],
        smem=1, flops=4 * group_rows * (group_rows + block) * PART_WIDTH,
    )

    blocks = call(
        apply_kernel,
        [jax.ShapeDtypeStruct((tok_dev, PART_WIDTH), BF16)] * PARTS,
        [place, weights, query_seq, attended] + pieces + pieces_other,
        scratch=[
            VMEM((PART_FAST, 3, SPAN, hidden), BF16),
            VMEM((PART_FAST * 3, hidden), F32),
            VMEM((group_rows, PART_WIDTH), BF16),
        ],
        smem=1, flops=6 * group_rows * PART_WIDTH * hidden,
    )

    parts = []
    for j in range(PARTS):
        parts.append(permute(blocks[j], lambda z, y, x, c, j=j: (z, c, x ^ j % 2, y ^ j // 2)))

    (out,) = call(
        norm_kernel,
        [jax.ShapeDtypeStruct((tok_dev, WIDTH), BF16)],
        [place] + parts + [norm_gain.reshape(1, WIDTH)],
        scratch=[VMEM((PARTS, tok_dev, PART_WIDTH), BF16)],
        smem=1, flops=6 * tok_dev * WIDTH,
    )
    return out


def solution(mesh):
    rows = P(("groups", "tok"), None)
    return jax.shard_map(
        shards,
        mesh=mesh,
        in_specs=(rows, rows, rows, rows, P("groups"), P("groups"), P(), P()),
        out_specs=rows,
        check_vma=False,
    )
```

```python
import functools
import math

import jax
import jax.numpy as jnp
from jax import lax
from jax.experimental import pallas as pl
from jax.experimental.pallas import tpu as pltpu
from jax.sharding import PartitionSpec as P


HEADS = 8
HEAD_DIM = 320
ATT_DIM = 128
WINDOW = 1024
WIDTH = 2560
ATT_HEADS = 20
LANES = 128
EPS = 1e-06

PARTS = math.gcd(HEADS, ATT_HEADS)
PART_WIDTH = WIDTH // PARTS
PART_FAST = HEADS // PARTS
PART_ATT = ATT_HEADS // PARTS
SPAN = -(-HEAD_DIM // LANES) * LANES


F32 = jnp.float32
BF16 = jnp.bfloat16
VMEM = pltpu.VMEM


def iota(shape, dim):
    return lax.broadcasted_iota(jnp.int32, shape, dim)


def dot(a, b, dims=((1,), (0,))):
    return lax.dot_general(a, b, (dims, ((), ())), preferred_element_type=F32)


def column_of(row):
    n = row.shape[1]
    square = jnp.broadcast_to(row.astype(F32), (n, n))
    diagonal = iota((n, n), 0) == iota((n, n), 1)
    return jnp.sum(jnp.where(diagonal, square, 0.0), axis=1, keepdims=True)


def call(kernel, outs, ins, scratch=(), smem=0, flops=0, grid=None, in_specs=None, out_specs=None):
    specs = [pl.BlockSpec(memory_space=pltpu.SMEM)] * smem
    specs += in_specs or [pl.BlockSpec(memory_space=VMEM)] * (len(ins) - smem)
    moved = sum(x.size * x.dtype.itemsize for x in list(ins) + list(outs))
    extra = {} if grid is None else {"grid": grid}
    return pl.pallas_call(
        kernel,
        out_shape=list(outs),
        in_specs=specs,
        out_specs=out_specs or [pl.BlockSpec(memory_space=VMEM)] * len(outs),
        scratch_shapes=list(scratch),
        compiler_params=pltpu.CompilerParams(vmem_limit_bytes=60 << 20),
        cost_estimate=pl.CostEstimate(flops=flops, bytes_accessed=moved, transcendentals=0),
        **extra,
    )(*ins)


def window_of(head):
    begin = min(head * HEAD_DIM // LANES * LANES, PART_WIDTH - SPAN)
    return begin, head * HEAD_DIM - begin


def heads_kernel(place_ref, rate_ref, key_ref, value_ref, *out_refs):
    n, width = key_ref.shape
    step, part, core = pl.program_id(0), place_ref[1], place_ref[2]
    lane = iota((n, SPAN), 1)
    for local in range(width // PART_WIDTH):
        index = step * (width // PART_WIDTH) + local
        own_part = index ^ part
        edge = lax.rem(own_part, width // PART_WIDTH) * PART_WIDTH
        rows = []
        for head in range(PART_FAST):
            begin, offset = window_of(head)

            def window(ref):
                rows = ref[:, pl.ds(pl.multiple_of(edge + begin, LANES), SPAN)].astype(F32)
                rows = pltpu.roll(rows, SPAN - offset, 1) if offset else rows
                return jnp.where(lane < HEAD_DIM, rows, 0.0)

            rate = column_of(rate_ref[pl.ds(own_part * PART_FAST + head, 1), :])
            keys = window(key_ref)
            for third in range(3):
                piece = rate.astype(BF16).astype(F32)
                rate = rate - piece
                keys = jnp.where(lane == HEAD_DIM + third, piece, keys)
            rows.append((keys, window(value_ref)))
        for flip in range(PART_FAST):
            chosen = [jnp.where(core == flip, first, second).astype(BF16) for first, second in zip(*rows)]
            for at in range(local, PARTS, width // PART_WIDTH):
                @pl.when(step == at // (width // PART_WIDTH))
                def _():
                    out_refs[at * PART_FAST + flip][:, :SPAN] = chosen[0]
                    out_refs[at * PART_FAST + flip][:, SPAN:] = chosen[1]


def pack_kernel(group_shift, slots, place_ref, order_ref, query_ref, key_ref, value_ref, out_ref, choose_buf):
    n = query_ref.shape[0]
    planes, parts, cores = out_ref.shape[:3]

    @pl.when(pl.program_id(0) == 0)
    def _():
        pos = order_ref[pl.ds(place_ref[0], 1), :]
        group = lax.shift_right_logical(pos, group_shift)
        group_col = column_of(group).astype(jnp.int32)
        earlier = (group_col == group) & (iota((n, n), 0) < iota((n, n), 1))
        rank = jnp.sum(jnp.where(earlier, 1.0, 0.0), axis=0, keepdims=True)
        slot = group * slots + rank.astype(jnp.int32)
        choose_buf[...] = jnp.where(iota((n, n), 0) == slot, 1.0, 0.0).astype(BF16)

    choose = choose_buf[...]
    for index, ref in enumerate((key_ref, value_ref, query_ref)):
        lanes = slice(index * PART_WIDTH, (index + 1) * PART_WIDTH)
        for part in range(parts):
            rows = dot(choose, ref[:, part * PART_WIDTH : (part + 1) * PART_WIDTH]).astype(BF16)
            for plane in range(planes):
                for core in range(cores):
                    at = (plane * cores + core) * slots
                    out_ref[plane, part, core, :, lanes] = rows[at : at + slots]


def arrival_choice(group_shift, slots, orders, group, n):
    sources, rows = orders.shape
    low_shift = group_shift // 2
    mine = lax.shift_right_logical(orders, group_shift) == group
    before = jnp.where(iota((rows, rows), 0) < iota((rows, rows), 1), 1.0, 0.0).astype(BF16)
    rank = dot(jnp.where(mine, 1.0, 0.0).astype(BF16), before)
    within = orders & ((1 << group_shift) - 1)
    digits = (lax.shift_right_logical(within, low_shift).astype(F32), (within & ((1 << low_shift) - 1)).astype(F32))
    spread = jnp.where(iota((sources, n), 1) // slots == iota((sources, n), 0), 1.0, 0.0).astype(BF16)
    keep = iota((slots, n), 1) % slots == iota((slots, n), 0)
    column = iota((sources, slots), 1)
    pos = jnp.zeros((1, n), F32)
    for digit, weight in zip(digits, (float(1 << low_shift), 1.0)):
        table = jnp.zeros((sources, slots), F32)
        for k in range(slots):
            one = jnp.sum(jnp.where(mine & (rank == float(k)), digit, 0.0), axis=1, keepdims=True)
            table = jnp.where(column == k, one, table)
        wide = dot(table.astype(BF16), spread, ((0,), (0,)))
        pos += weight * jnp.sum(jnp.where(keep, wide, 0.0), axis=0, keepdims=True)
    return jnp.where(iota((n, n), 0) == pos.astype(jnp.int32), 1.0, 0.0).astype(BF16)


def choose_kernel(group_shift, slots, place_ref, order_ref, choose_ref):
    choose_ref[...] = arrival_choice(group_shift, slots, order_ref[...], place_ref[3], choose_ref.shape[0])


def place_kernel(choose_ref, in_ref, kv_ref, q_ref):
    choose = choose_ref[...]
    kv_ref[...] = dot(choose, in_ref[:, : 2 * PART_WIDTH]).astype(BF16)
    q_ref[...] = dot(choose, in_ref[:, 2 * PART_WIDTH :]).astype(BF16)


def grads_kernel(chunk, last, place_ref, weight_ref, *refs):
    outs = 2 if last else 1
    weight_buf, key_buf, target_buf, delta_buf, pr_buf, sums = refs[-6:]
    out_refs, in_refs = refs[-6 - outs : -6], refs[: -6 - outs]
    kv_refs, early_ref = (in_refs[:-1], in_refs[-1]) if last else (in_refs, None)
    block = kv_refs[0].shape[0]
    n = key_buf.shape[0]
    hidden = weight_ref.shape[2]
    first = pl.multiple_of(place_ref[2] * HEAD_DIM, 16)
    for index in range(3):
        lanes = slice(index * hidden, (index + 1) * hidden)
        weight_buf[:HEAD_DIM, lanes] = weight_ref[index, pl.ds(first, HEAD_DIM), :]
    weight_buf[HEAD_DIM:, :] = jnp.zeros((SPAN - HEAD_DIM, 3 * hidden), BF16)
    lane = iota((1, SPAN), 1)
    wanted = (lane >= HEAD_DIM) & (lane < HEAD_DIM + 3)
    for index, ref in enumerate(kv_refs):
        here = pl.ds(index * block, block)
        key = ref[:, :SPAN]
        rate = jnp.sum(jnp.where(wanted, key.astype(F32), 0.0), axis=1, keepdims=True)
        key_buf[here, :] = key
        target_buf[here, :] = (ref[:, SPAN:].astype(F32) * rate).astype(BF16)
    for at in range(0, n, chunk):
        here = pl.ds(at, chunk)
        both = dot(key_buf[here, :], weight_buf[:, : 2 * hidden])
        gate, upward = both[:, :hidden], both[:, hidden:]
        backward = dot(target_buf[here, :], weight_buf[:, 2 * hidden :])
        sigmoid = jax.nn.sigmoid(gate)
        active = gate * sigmoid
        pr_buf[here, :] = (active * upward).astype(BF16)
        delta_buf[here, hidden:] = (backward * active).astype(BF16)
        delta_buf[here, :hidden] = (backward * upward * sigmoid * (1.0 + gate * (1.0 - sigmoid))).astype(BF16)
    for left, right, begin in ((key_buf, delta_buf, 0), (target_buf, pr_buf, 2 * hidden)):
        lanes = slice(begin, begin + right.shape[1])
        total = dot(left[...], right[...], ((0,), (0,)))[:HEAD_DIM]
        if last:
            sums[:, lanes] = (total + early_ref[:, lanes].astype(F32)).astype(BF16)
        else:
            out_refs[0][:, lanes] = total.astype(BF16)
    if last:
        half = out_refs[0].shape[0]
        side = place_ref[3] // PART_FAST & 1
        out_refs[0][...] = sums[pl.ds(pl.multiple_of((1 - side) * half, 16), half), :]
        out_refs[1][...] = sums[pl.ds(pl.multiple_of(side * half, 16), half), :]


FACTOR = ATT_DIM ** (-0.5) * math.log2(math.e)


def reach(before, index, count, block):
    at = pl.multiple_of(jnp.where(before, index, count - 1 - index) * block, block)
    return at, pl.multiple_of(jnp.where(before, at, 0), block), jnp.where(before, -count * block, count * block - at)


def block_ids(ids, index, count, block, turned):
    turn = count - 1 - index
    row = jnp.where(turned, ids[:, turn * block : (turn + 1) * block], ids[:, index * block : (index + 1) * block])
    return column_of(row).astype(jnp.int32)


def mask_of(own, ids, shift):
    gap = iota((own.shape[0], ids.shape[1]), 1) - iota((own.shape[0], ids.shape[1]), 0) + shift
    return jnp.where((gap < WINDOW // 2) & (gap > -(WINDOW // 2)) & (own == ids), 0.0, -1e30)


def near_kernel(block, place_ref, query_ref, ids_ref, key_ref, value_ref, chip_key_ref, chip_value_ref, out_ref, stat_ref, bias, chip_bias):
    n = query_ref.shape[0]
    count = n // block
    head = pl.program_id(0)
    core, group = place_ref[2], place_ref[3]
    second = core == 1

    @pl.when(head == 0)
    def _():
        ids = ids_ref[pl.ds(group, 1), :]
        for index in range(count):
            at = index * block
            bias[at : at + block, :] = mask_of(column_of(ids[:, at : at + block]).astype(jnp.int32), ids, -at)
        for index in range(count):
            _, _, shift = reach(second, count - 1 - index, count, block)
            size = (index + 1) * block
            own = block_ids(ids, index, count, block, second)
            other = ids_ref[pl.ds(group + 1 - 2 * core, 1), :]
            other = jnp.where(second, other[:, n - size :], other[:, :size])
            chip_bias[index, :, :size] = mask_of(own, other, shift)
        stat_ref[...] = jnp.zeros_like(stat_ref)

    lane = iota((block, LANES), 1)
    for index in range(count):
        at, start, _ = reach(second, count - 1 - index, count, block)
        size = (index + 1) * block
        here, there = pl.ds(at, block), pl.ds(start, size)
        query = query_ref[here, :]
        score = dot(query, key_ref[...], ((1,), (1,))) + bias[here, :]
        chip = dot(query, chip_key_ref[there, :], ((1,), (1,))) + chip_bias[index, :, :size]
        peak = jnp.maximum(jnp.max(score, axis=1, keepdims=True), jnp.max(chip, axis=1, keepdims=True))
        score = jnp.exp2((score - peak) * FACTOR)
        chip = jnp.exp2((chip - peak) * FACTOR)
        total = jnp.sum(score, axis=1, keepdims=True) + jnp.sum(chip, axis=1, keepdims=True)
        out_ref[here, :] = dot(score.astype(BF16), value_ref[...]) + dot(chip.astype(BF16), chip_value_ref[there, :])
        stat = jnp.where(lane == 2 * head, peak, stat_ref[here, :])
        stat_ref[here, :] = jnp.where(lane == 2 * head + 1, total, stat)


def far_kernel(block, first_goal, place_ref, query_ref, ids_ref, near_ref, stat_ref, fast_ref, key_ref, value_ref, *refs):
    out_refs, (bias, rows_buf) = refs[:-2], refs[-2:]
    n = query_ref.shape[0]
    count = n // block
    head = pl.program_id(0)
    core, group = place_ref[2], place_ref[3]
    last = ids_ref.shape[0] - 1
    first = core == 0

    @pl.when(head == 0)
    def _():
        beyond = group - 1 + 2 * core
        exists = (beyond >= 0) & (beyond <= last)
        ids = ids_ref[pl.ds(group, 1), :]
        for index in range(count):
            _, _, shift = reach(first, index, count, block)
            size = n - index * block
            own = block_ids(ids, index, count, block, core == 1)
            other = ids_ref[pl.ds(jnp.clip(beyond, 0, last), 1), :]
            other = jnp.where(first, other[:, n - size :], other[:, :size])
            bias[index, :, :size] = mask_of(own, jnp.where(exists, other, -1), shift)

    lane = iota((block, LANES), 1)
    for index in range(count):
        at, start, _ = reach(first, index, count, block)
        size = n - index * block
        here, there = pl.ds(at, block), pl.ds(start, size)
        score = dot(query_ref[here, :], key_ref[there, :], ((1,), (1,))) + bias[index, :, :size]
        stat = stat_ref[here, :]
        old_peak = jnp.sum(jnp.where(lane == 2 * head, stat, 0.0), axis=1, keepdims=True)
        old_total = jnp.sum(jnp.where(lane == 2 * head + 1, stat, 0.0), axis=1, keepdims=True)
        peak = jnp.maximum(jnp.max(score, axis=1, keepdims=True), old_peak)
        keep = jnp.exp2((old_peak - peak) * FACTOR)
        score = jnp.exp2((score - peak) * FACTOR)
        total = old_total * keep + jnp.sum(score, axis=1, keepdims=True)
        mixed = near_ref[here, :] * keep + dot(score.astype(BF16), value_ref[there, :])
        rows_buf[here, :] = (mixed / total + fast_ref[here, :]).astype(BF16)
    rows = out_refs[0].shape[0]
    for index, ref in enumerate(out_refs):
        begin = pl.multiple_of(place_ref[first_goal + index] * rows, rows)
        ref[...] = rows_buf[pl.ds(begin, rows), :]


def apply_kernel(place_ref, weight_ref, query_ref, *refs):
    hidden = weight_ref.shape[2]
    out_ref, fresh, scales = refs[-3:]
    count = (len(refs) - 3) // 2
    mine_refs, other_refs = refs[:count], refs[count : 2 * count]
    piece = mine_refs[0].shape[0]
    core = place_ref[2]
    for head in range(PART_FAST):
        _, offset = window_of(head)
        for index in range(3):
            lanes = slice(index * hidden, (index + 1) * hidden)
            anchor = jnp.full((1, hidden), EPS, F32)
            length = jnp.full((1, hidden), EPS, F32)
            for step in range(count):
                at = pl.multiple_of(place_ref[4 + PARTS + step], 16)
                base = weight_ref[index, pl.ds(at + head * HEAD_DIM, piece), :].astype(F32)
                grad = jnp.where(core == head, mine_refs[step][:, lanes], other_refs[step][:, lanes]).astype(F32)
                update = base + grad
                anchor += jnp.sum(base * base, axis=0, keepdims=True)
                length += jnp.sum(update * update, axis=0, keepdims=True)
                fresh[head, index, pl.ds(at + offset, piece), :] = update.astype(BF16)
            scales[head * 3 + index, :] = (jnp.sqrt(anchor) / jnp.sqrt(length))[0]
            if offset:
                fresh[head, index, :offset, :] = jnp.zeros((offset, hidden), BF16)
            if offset + HEAD_DIM < SPAN:
                fresh[head, index, offset + HEAD_DIM :, :] = jnp.zeros((SPAN - offset - HEAD_DIM, hidden), BF16)
    parts = []
    for head in range(PART_FAST):
        begin, _ = window_of(head)
        query = query_ref[:, begin : begin + SPAN]
        scale = [scales[head * 3 + index : head * 3 + index + 1, :] for index in range(3)]
        gate = dot(query, fresh[head, 0]) * scale[0]
        upward = dot(query, fresh[head, 1]) * (scale[1] * scale[2])
        product = (gate * jax.nn.sigmoid(gate) * upward).astype(BF16)
        parts.append((begin, dot(product, fresh[head, 2], ((1,), (1,)))))
    for lane in range(0, PART_WIDTH, LANES):
        inside = [value[:, lane - begin : lane - begin + LANES] for begin, value in parts if begin <= lane < begin + SPAN]
        out_ref[:, lane : lane + LANES] = functools.reduce(jnp.add, inside)


def norm_kernel(place_ref, *refs):
    part_refs, gain_ref, out_ref, buf = refs[:PARTS], refs[PARTS], refs[PARTS + 1], refs[PARTS + 2]
    square = jnp.zeros((out_ref.shape[0], 1), F32)
    for index, ref in enumerate(part_refs):
        rows = ref[...]
        buf[place_ref[4 + index]] = rows
        wide = rows.astype(F32)
        square += jnp.sum(wide * wide, axis=1, keepdims=True)
    factor = lax.rsqrt(square / WIDTH + EPS)
    for part in range(PARTS):
        lanes = slice(part * PART_WIDTH, (part + 1) * PART_WIDTH)
        out_ref[:, lanes] = (buf[part].astype(F32) * factor * gain_ref[:, lanes]).astype(BF16)


def shards(queries, key_rows, value_rows, learn_rates, frame_order, window_ids, fast_init, norm_gain):
    tok_dev = queries.shape[0]
    hidden = fast_init.shape[0]
    sections = lax.axis_size("tok")
    plane_size = PARTS * PART_FAST
    planes = sections // plane_size
    group_rows = tok_dev * PARTS
    groups = planes * PART_FAST
    slots = tok_dev // groups
    half = WINDOW // 2
    assert PART_FAST == 2 and half == group_rows and group_rows & (group_rows - 1) == 0
    group_shift = group_rows.bit_length() - 1

    rank = lax.axis_index("tok")
    plane = rank // plane_size
    part = rank // PART_FAST % PARTS
    core = rank % PART_FAST
    row, column = part // 2, part % 2
    group = plane * PART_FAST + core

    def at(plane, row, column, core):
        return plane * plane_size + (row * 2 + column) * PART_FAST + core

    everyone = [(z, y, x, c) for z in range(planes) for y in range(2) for x in range(2) for c in range(2)]

    def permute(array, target):
        route = []
        for source in everyone:
            goal = target(*source)
            if goal is not None:
                route.append((at(*source), at(*goal)))
        return lax.ppermute(array, "tok", route)

    sources = [2 * (core ^ j // 2) + (column ^ j % 2) for j in range(PARTS)]
    bits = planes.bit_length() - 1
    piece = HEAD_DIM >> bits
    assert planes == 1 << bits and piece << bits == HEAD_DIM and piece % 16 == 0

    def owned(plane):
        return sum((plane >> bit & 1) * (HEAD_DIM >> bit + 1) for bit in range(bits))

    masks = [0]
    for bit in reversed(range(bits)):
        masks += [mask ^ 1 << bit for mask in masks]
    starts = [owned(plane ^ mask) for mask in masks]
    goals = [2 * (column ^ j % 2) + (row ^ j // 2) for j in range(PARTS)]
    place = jnp.stack([rank, part, core, group] + sources + starts + goals).astype(jnp.int32)

    def weight_part():
        own = lax.dynamic_slice_in_dim(fast_init, part * PART_WIDTH, PART_WIDTH, 2)
        return jnp.transpose(own, (1, 2, 0))

    weights = weight_part()

    full = lambda a: pl.BlockSpec(a.shape, lambda h: (0,) * a.ndim)
    steps = 2
    together = PARTS // steps
    other_cut = pl.BlockSpec((tok_dev, WIDTH // steps), lambda h, place: (0, h ^ place[1] // together))
    whole = lambda shape: pl.BlockSpec(shape, lambda h, place: (0,) * len(shape))
    heads_out = pl.pallas_call(
        heads_kernel,
        out_shape=[jax.ShapeDtypeStruct((tok_dev, 2 * SPAN), BF16)] * plane_size,
        grid_spec=pltpu.PrefetchScalarGridSpec(
            num_scalar_prefetch=1,
            grid=(steps,),
            in_specs=[whole(learn_rates.shape[::-1]), other_cut, other_cut],
            out_specs=[whole((tok_dev, 2 * SPAN))] * plane_size,
        ),
        compiler_params=pltpu.CompilerParams(vmem_limit_bytes=60 << 20),
        cost_estimate=pl.CostEstimate(flops=tok_dev * WIDTH, bytes_accessed=8 * tok_dev * WIDTH, transcendentals=0),
        name="heads",
    )(place, learn_rates.T, key_rows, value_rows)
    heads_in = [heads_out[0]]
    for j in range(1, plane_size):
        heads_in.append(permute(heads_out[j], lambda z, y, x, c, j=j: (z, y ^ j >> 2, x ^ j >> 1 & 1, c ^ j & 1)))

    orders = frame_order.reshape(sections, tok_dev)
    cut = pl.BlockSpec((tok_dev, WIDTH // steps), lambda h: (0, h))
    (packed,) = call(
        functools.partial(pack_kernel, group_shift, slots),
        [jax.ShapeDtypeStruct((planes, PARTS, PART_FAST, slots, 3 * PART_WIDTH), BF16)],
        [place, orders, queries, key_rows, value_rows],
        in_specs=[full(orders), cut, cut, cut],
        out_specs=[pl.BlockSpec((planes, together, PART_FAST, slots, 3 * PART_WIDTH), lambda h: (0, h, 0, 0, 0))],
        grid=(steps,),
        scratch=[VMEM((tok_dev, tok_dev), BF16)],
        smem=1, flops=2 * tok_dev * tok_dev * 3 * WIDTH,
    )
    arrived = lax.all_to_all(
        packed.reshape(sections, slots, 3 * PART_WIDTH), "tok", split_axis=0, concat_axis=0, tiled=True
    ).reshape(group_rows, 3 * PART_WIDTH)

    (choose,) = call(
        functools.partial(choose_kernel, group_shift, slots),
        [jax.ShapeDtypeStruct((group_rows, group_rows), BF16)],
        [place, orders], smem=1, flops=2 * group_rows * group_rows,
    )
    kv_seq, query_seq = call(
        place_kernel,
        [jax.ShapeDtypeStruct((group_rows, width), BF16) for width in (2 * PART_WIDTH, PART_WIDTH)],
        [choose, arrived], flops=2 * group_rows * group_rows * 3 * PART_WIDTH,
    )

    swap = lambda z, y, x, c: (z, y, x, 1 - c)

    def beyond(z, y, x, c):
        goal = z + 2 * c - 1
        return (goal, y, x, 1 - c) if 0 <= goal < planes else None

    kv_chip = permute(kv_seq, swap)
    kv_far = permute(kv_seq, beyond)

    near = plane_size // 2
    tokens = near * tok_dev
    grad_scratch = [VMEM((SPAN, 3 * hidden), BF16)] + [VMEM((tokens, SPAN), BF16)] * 2
    grad_scratch += [VMEM((tokens, 2 * hidden), BF16), VMEM((tokens, hidden), BF16), VMEM((HEAD_DIM, 3 * hidden), BF16)]
    grad_flops = 12 * tokens * HEAD_DIM * hidden
    (early,) = call(
        functools.partial(grads_kernel, tokens, False),
        [jax.ShapeDtypeStruct((HEAD_DIM, 3 * hidden), BF16)], [place, weights] + heads_in[:near],
        scratch=grad_scratch, smem=1, flops=grad_flops,
    )
    send, keep = call(
        functools.partial(grads_kernel, tokens, True),
        [jax.ShapeDtypeStruct((HEAD_DIM // 2, 3 * hidden), BF16)] * 2,
        [place, weights] + heads_in[near:] + [early],
        scratch=grad_scratch, smem=1, flops=grad_flops,
    )

    def across(bit):
        return lambda z, y, x, c: (z ^ 1 << bit, y, x, c)

    def added(first, second):
        return (first.astype(F32) + second.astype(F32)).astype(BF16)

    for bit in range(bits):
        came = permute(send, across(bit))
        if bit + 1 < bits:
            size = HEAD_DIM >> bit + 2
            side = plane >> bit + 1 & 1
            cuts = [[lax.dynamic_slice_in_dim(a, at * size, size, 0) for a in (keep, came)] for at in (1 - side, side)]
            send = added(*cuts[0])
            keep = added(*cuts[1])
        else:
            total = added(keep, came)
    pieces = [total]
    for bit in reversed(range(bits)):
        fresh_pieces = []
        for held in pieces:
            fresh_pieces.append(permute(held, across(bit)))
        pieces += fresh_pieces
    pieces_other = []
    for held in pieces:
        pieces_other.append(permute(held, swap))

    block = min(LANES, group_rows)
    lane_block = lambda rows, shift: pl.BlockSpec((rows, ATT_DIM), lambda h: (0, h + shift))
    ids = window_ids.reshape(groups, group_rows)
    wide = jax.ShapeDtypeStruct((group_rows, PART_WIDTH), F32)
    stat_shape = jax.ShapeDtypeStruct((group_rows, LANES), F32)
    count = group_rows // block
    assert 2 * PART_ATT <= LANES
    keys, values = lane_block(group_rows, 0), lane_block(group_rows, PART_ATT)
    near_mixed, stats = call(
        functools.partial(near_kernel, block),
        [wide, stat_shape],
        [place, query_seq, ids, kv_seq, kv_seq, kv_chip, kv_chip],
        in_specs=[lane_block(group_rows, 0), full(ids), keys, values, keys, values],
        out_specs=[lane_block(group_rows, 0), full(stat_shape)],
        grid=(PART_ATT,),
        scratch=[VMEM((group_rows, group_rows), F32), VMEM((count, block, group_rows), F32)],
        smem=1, flops=6 * group_rows * group_rows * PART_WIDTH,
    )

    (fast_out,) = call(
        apply_kernel,
        [wide],
        [place, weights, query_seq] + pieces + pieces_other,
        scratch=[VMEM((PART_FAST, 3, SPAN, hidden), BF16), VMEM((PART_FAST * 3, hidden), F32)],
        smem=1, flops=6 * group_rows * PART_WIDTH * hidden,
    )

    blocks = call(
        functools.partial(far_kernel, block, 4 + PARTS + len(starts)),
        [jax.ShapeDtypeStruct((tok_dev, PART_WIDTH), BF16)] * PARTS,
        [place, query_seq, ids, near_mixed, stats, fast_out, kv_far, kv_far],
        in_specs=[lane_block(group_rows, 0), full(ids), lane_block(group_rows, 0), full(stats)]
        + [lane_block(group_rows, 0), keys, values],
        out_specs=[lane_block(tok_dev, 0)] * PARTS,
        grid=(PART_ATT,),
        scratch=[VMEM((count, block, group_rows), F32), VMEM((group_rows, ATT_DIM), BF16)],
        smem=1, flops=3 * group_rows * group_rows * PART_WIDTH,
    )

    parts = []
    for j in range(PARTS):
        parts.append(permute(blocks[j], lambda z, y, x, c, j=j: (z, c, x ^ j % 2, y ^ j // 2)))

    (out,) = call(
        norm_kernel,
        [jax.ShapeDtypeStruct((tok_dev, WIDTH), BF16)],
        [place] + parts + [norm_gain.reshape(1, WIDTH)],
        scratch=[VMEM((PARTS, tok_dev, PART_WIDTH), BF16)],
        smem=1, flops=6 * tok_dev * WIDTH,
    )
    return out


def solution(mesh):
    rows = P(("groups", "tok"), None)
    return jax.shard_map(
        shards,
        mesh=mesh,
        in_specs=(rows, rows, rows, rows, P("groups"), P("groups"), P(), P()),
        out_specs=rows,
        check_vma=False,
    )
```

```python
import functools
import math

import jax
import jax.numpy as jnp
from jax import lax
from jax.experimental import pallas as pl
from jax.experimental.pallas import tpu as pltpu
from jax.sharding import PartitionSpec as P


HEADS = 8
HEAD_DIM = 320
ATT_DIM = 128
WINDOW = 1024
WIDTH = 2560
ATT_HEADS = 20
LANES = 128
EPS = 1e-06

PARTS = math.gcd(HEADS, ATT_HEADS)
PART_WIDTH = WIDTH // PARTS
PART_FAST = HEADS // PARTS
PART_ATT = ATT_HEADS // PARTS
SPAN = -(-HEAD_DIM // LANES) * LANES


F32 = jnp.float32
BF16 = jnp.bfloat16
VMEM = pltpu.VMEM


def iota(shape, dim):
    return lax.broadcasted_iota(jnp.int32, shape, dim)


def dot(a, b, dims=((1,), (0,))):
    return lax.dot_general(a, b, (dims, ((), ())), preferred_element_type=F32)


def column_of(row):
    n = row.shape[1]
    square = jnp.broadcast_to(row.astype(F32), (n, n))
    diagonal = iota((n, n), 0) == iota((n, n), 1)
    return jnp.sum(jnp.where(diagonal, square, 0.0), axis=1, keepdims=True)


def call(kernel, outs, ins, scratch=(), smem=0, flops=0, grid=None, in_specs=None, out_specs=None, limit=60):
    specs = [pl.BlockSpec(memory_space=pltpu.SMEM)] * smem
    specs += in_specs or [pl.BlockSpec(memory_space=VMEM)] * (len(ins) - smem)
    moved = sum(x.size * x.dtype.itemsize for x in list(ins) + list(outs))
    extra = {} if grid is None else {"grid": grid}
    return pl.pallas_call(
        kernel,
        out_shape=list(outs),
        in_specs=specs,
        out_specs=out_specs or [pl.BlockSpec(memory_space=VMEM)] * len(outs),
        scratch_shapes=list(scratch),
        compiler_params=pltpu.CompilerParams(vmem_limit_bytes=limit << 20),
        cost_estimate=pl.CostEstimate(flops=flops, bytes_accessed=moved, transcendentals=0),
        **extra,
    )(*ins)


def window_of(head):
    begin = min(head * HEAD_DIM // LANES * LANES, PART_WIDTH - SPAN)
    return begin, head * HEAD_DIM - begin


def front_kernel(group_shift, slots, place_ref, order_ref, rate_ref, query_ref, key_ref, value_ref, *refs):
    out_ref, head_refs, choose_buf = refs[0], refs[1:-1], refs[-1]
    n, _ = key_ref.shape
    planes, together, cores = out_ref.shape[:3]
    step, part, core = pl.program_id(0), place_ref[1], place_ref[2]

    @pl.when(step == 0)
    def _():
        pos = order_ref[pl.ds(place_ref[0], 1), :]
        group = lax.shift_right_logical(pos, group_shift)
        group_col = column_of(group).astype(jnp.int32)
        earlier = (group_col == group) & (iota((n, n), 0) < iota((n, n), 1))
        rank = jnp.sum(jnp.where(earlier, 1.0, 0.0), axis=0, keepdims=True)
        slot = group * slots + rank.astype(jnp.int32)
        choose_buf[...] = jnp.where(iota((n, n), 0) == slot, 1.0, 0.0).astype(BF16)

    choose = choose_buf[...]
    for index, ref in enumerate((key_ref, value_ref, query_ref)):
        lanes = slice(index * PART_WIDTH, (index + 1) * PART_WIDTH)
        for local in range(together):
            rows = dot(choose, ref[:, local * PART_WIDTH : (local + 1) * PART_WIDTH]).astype(BF16)
            for plane in range(planes):
                for at in range(cores):
                    first = (plane * cores + at) * slots
                    out_ref[plane, local, at, :, lanes] = rows[first : first + slots]

    lane = iota((n, SPAN), 1)
    tail = PART_WIDTH - SPAN
    for local in range(together):
        target_part = step * together + local
        rows = []
        for head in range(PART_FAST):
            begin, offset = window_of(head)
            span = slice(local * PART_WIDTH + begin, local * PART_WIDTH + begin + SPAN)
            rate = column_of(rate_ref[pl.ds(target_part * PART_FAST + head, 1), :])
            keys = key_ref[:, span].astype(F32)
            targets = value_ref[:, span].astype(F32) * rate
            turn = SPAN - HEAD_DIM
            if offset:
                keys = pltpu.roll(keys, SPAN - offset, 1)
            if offset != turn:
                targets = pltpu.roll(targets, turn - offset, 1)
            rows.append((keys.astype(BF16), targets.astype(BF16)))
        for flip in range(PART_FAST):
            keys, targets = (jnp.where(core == flip, one, two) for one, two in zip(*rows))
            middle = jnp.where(iota((n, LANES), 1) < HEAD_DIM - tail, keys[:, tail:], targets[:, : SPAN - tail])
            for index in range(PARTS):
                @pl.when((target_part ^ part) == index)
                def _():
                    ref = head_refs[index * PART_FAST + flip]
                    ref[:, :tail] = keys[:, :tail]
                    ref[:, tail:SPAN] = middle
                    ref[:, SPAN:] = targets[:, SPAN - tail :]


def arrival_choice(group_shift, slots, orders, group, n):
    sources, rows = orders.shape
    low_shift = group_shift // 2
    mine = lax.shift_right_logical(orders, group_shift) == group
    before = jnp.where(iota((rows, rows), 0) < iota((rows, rows), 1), 1.0, 0.0).astype(BF16)
    rank = dot(jnp.where(mine, 1.0, 0.0).astype(BF16), before)
    within = orders & ((1 << group_shift) - 1)
    digits = (lax.shift_right_logical(within, low_shift).astype(F32), (within & ((1 << low_shift) - 1)).astype(F32))
    spread = jnp.where(iota((sources, n), 1) // slots == iota((sources, n), 0), 1.0, 0.0).astype(BF16)
    keep = iota((slots, n), 1) % slots == iota((slots, n), 0)
    column = iota((sources, slots), 1)
    pos = jnp.zeros((1, n), F32)
    for digit, weight in zip(digits, (float(1 << low_shift), 1.0)):
        table = jnp.zeros((sources, slots), F32)
        for k in range(slots):
            one = jnp.sum(jnp.where(mine & (rank == float(k)), digit, 0.0), axis=1, keepdims=True)
            table = jnp.where(column == k, one, table)
        wide = dot(table.astype(BF16), spread, ((0,), (0,)))
        pos += weight * jnp.sum(jnp.where(keep, wide, 0.0), axis=0, keepdims=True)
    return jnp.where(iota((n, n), 0) == pos.astype(jnp.int32), 1.0, 0.0).astype(BF16)


def choose_kernel(group_shift, slots, place_ref, order_ref, choose_ref):
    choose_ref[...] = arrival_choice(group_shift, slots, order_ref[...], place_ref[3], choose_ref.shape[0])


def place_kernel(choose_ref, in_ref, kv_ref, q_ref):
    choose = choose_ref[...]
    kv_ref[...] = dot(choose, in_ref[:, : 2 * PART_WIDTH]).astype(BF16)
    q_ref[...] = dot(choose, in_ref[:, 2 * PART_WIDTH :]).astype(BF16)


def grads_kernel(chunk, last, place_ref, weight_ref, *refs):
    outs = 2 if last else 1
    weight_buf, key_buf, target_buf, delta_buf, pr_buf, sums = refs[-6:]
    out_refs, in_refs = refs[-6 - outs : -6], refs[: -6 - outs]
    kv_refs, early_ref = (in_refs[:-1], in_refs[-1]) if last else (in_refs, None)
    block = kv_refs[0].shape[0]
    n = key_buf.shape[0]
    hidden = weight_ref.shape[2]
    first = pl.multiple_of(place_ref[2] * HEAD_DIM, 16)
    spare = SPAN - HEAD_DIM
    for index in range(3):
        lanes = slice(index * hidden, (index + 1) * hidden)
        begin, blank = (0, HEAD_DIM) if index < 2 else (spare, 0)
        weight_buf[begin : begin + HEAD_DIM, lanes] = weight_ref[index, pl.ds(first, HEAD_DIM), :]
        weight_buf[blank : blank + spare, lanes] = jnp.zeros((spare, hidden), BF16)
    for index, ref in enumerate(kv_refs):
        here = pl.ds(index * block, block)
        key_buf[here, :] = ref[:, :SPAN]
        target_buf[here, :] = ref[:, PART_WIDTH - SPAN :]
    for at in range(0, n, chunk):
        here = pl.ds(at, chunk)
        both = dot(key_buf[here, :], weight_buf[:, : 2 * hidden])
        gate, upward = both[:, :hidden], both[:, hidden:]
        backward = dot(target_buf[here, :], weight_buf[:, 2 * hidden :])
        sigmoid = jax.nn.sigmoid(gate)
        active = gate * sigmoid
        pr_buf[here, :] = (active * upward).astype(BF16)
        delta_buf[here, hidden:] = (backward * active).astype(BF16)
        delta_buf[here, :hidden] = (backward * upward * sigmoid * (1.0 + gate * (1.0 - sigmoid))).astype(BF16)
    for left, right, begin, row in ((key_buf, delta_buf, 0, 0), (target_buf, pr_buf, 2 * hidden, spare)):
        lanes = slice(begin, begin + right.shape[1])
        total = dot(left[...], right[...], ((0,), (0,)))[row : row + HEAD_DIM]
        if last:
            sums[:, lanes] = (total + early_ref[:, lanes].astype(F32)).astype(BF16)
        else:
            out_refs[0][:, lanes] = total.astype(BF16)
    if last:
        half = out_refs[0].shape[0]
        side = place_ref[3] // PART_FAST & 1
        out_refs[0][...] = sums[pl.ds(pl.multiple_of((1 - side) * half, 16), half), :]
        out_refs[1][...] = sums[pl.ds(pl.multiple_of(side * half, 16), half), :]


FACTOR = ATT_DIM ** (-0.5) * math.log2(math.e)


def reach(before, index, count, block):
    at = pl.multiple_of(jnp.where(before, index, count - 1 - index) * block, block)
    return at, pl.multiple_of(jnp.where(before, at, 0), block), jnp.where(before, -count * block, count * block - at)


def block_ids(ids, index, count, block, turned):
    turn = count - 1 - index
    row = jnp.where(turned, ids[:, turn * block : (turn + 1) * block], ids[:, index * block : (index + 1) * block])
    return column_of(row).astype(jnp.int32)


def mask_of(own, ids, shift):
    gap = iota((own.shape[0], ids.shape[1]), 1) - iota((own.shape[0], ids.shape[1]), 0) + shift
    return jnp.where((gap < WINDOW // 2) & (gap > -(WINDOW // 2)) & (own == ids), 0.0, -1e30)


def head_lanes(head):
    return pl.ds(pl.multiple_of(head * ATT_DIM, ATT_DIM), ATT_DIM), pl.ds(pl.multiple_of(PART_WIDTH + head * ATT_DIM, ATT_DIM), ATT_DIM)


def near_kernel(block, place_ref, query_ref, ids_ref, kv_ref, chip_ref, out_ref, stat_ref, bias, chip_bias):
    n = query_ref.shape[0]
    count = n // block
    core, group = place_ref[2], place_ref[3]
    second = core == 1
    ids = ids_ref[pl.ds(group, 1), :]
    for index in range(count):
        at = index * block
        bias[at : at + block, :] = mask_of(column_of(ids[:, at : at + block]).astype(jnp.int32), ids, -at)
    for index in range(count):
        _, _, shift = reach(second, count - 1 - index, count, block)
        size = (index + 1) * block
        own = block_ids(ids, index, count, block, second)
        other = ids_ref[pl.ds(group + 1 - 2 * core, 1), :]
        other = jnp.where(second, other[:, n - size :], other[:, :size])
        chip_bias[index, :, :size] = mask_of(own, other, shift)
    stat_ref[...] = jnp.zeros_like(stat_ref)
    lane = iota((block, LANES), 1)

    @pl.loop(0, PART_ATT)
    def _(head):
        keys, values = head_lanes(head)
        for index in range(count):
            at, start, _ = reach(second, count - 1 - index, count, block)
            size = (index + 1) * block
            here, there = pl.ds(at, block), pl.ds(start, size)
            query = query_ref[here, keys]
            score = dot(query, kv_ref[:, keys], ((1,), (1,))) + bias[here, :]
            chip = dot(query, chip_ref[there, keys], ((1,), (1,))) + chip_bias[index, :, :size]
            peak = jnp.maximum(jnp.max(score, axis=1, keepdims=True), jnp.max(chip, axis=1, keepdims=True))
            score = jnp.exp2((score - peak) * FACTOR)
            chip = jnp.exp2((chip - peak) * FACTOR)
            total = jnp.sum(score, axis=1, keepdims=True) + jnp.sum(chip, axis=1, keepdims=True)
            out_ref[here, keys] = dot(score.astype(BF16), kv_ref[:, values]) + dot(chip.astype(BF16), chip_ref[there, values])
            stat = jnp.where(lane == 2 * head, peak, stat_ref[here, :])
            stat_ref[here, :] = jnp.where(lane == 2 * head + 1, total, stat)


def far_kernel(block, place_ref, query_ref, ids_ref, near_ref, stat_ref, kv_ref, out_ref, bias):
    n = query_ref.shape[0]
    count = n // block
    core, group = place_ref[2], place_ref[3]
    last = ids_ref.shape[0] - 1
    first = core == 0
    beyond = group - 1 + 2 * core
    exists = (beyond >= 0) & (beyond <= last)
    ids = ids_ref[pl.ds(group, 1), :]
    for index in range(count):
        _, _, shift = reach(first, index, count, block)
        size = n - index * block
        own = block_ids(ids, index, count, block, core == 1)
        other = ids_ref[pl.ds(jnp.clip(beyond, 0, last), 1), :]
        other = jnp.where(first, other[:, n - size :], other[:, :size])
        bias[index, :, :size] = mask_of(own, jnp.where(exists, other, -1), shift)
    lane = iota((block, LANES), 1)

    @pl.loop(0, PART_ATT)
    def _(head):
        keys, values = head_lanes(head)
        for index in range(count):
            at, start, _ = reach(first, index, count, block)
            size = n - index * block
            here, there = pl.ds(at, block), pl.ds(start, size)
            score = dot(query_ref[here, keys], kv_ref[there, keys], ((1,), (1,))) + bias[index, :, :size]
            stat = stat_ref[here, :]
            old_peak = jnp.sum(jnp.where(lane == 2 * head, stat, 0.0), axis=1, keepdims=True)
            old_total = jnp.sum(jnp.where(lane == 2 * head + 1, stat, 0.0), axis=1, keepdims=True)
            peak = jnp.maximum(jnp.max(score, axis=1, keepdims=True), old_peak)
            keep = jnp.exp2((old_peak - peak) * FACTOR)
            score = jnp.exp2((score - peak) * FACTOR)
            total = old_total * keep + jnp.sum(score, axis=1, keepdims=True)
            mixed = near_ref[here, keys] * keep + dot(score.astype(BF16), kv_ref[there, values])
            out_ref[here, keys] = mixed / total


def apply_kernel(place_ref, weight_ref, query_ref, attended_ref, *refs):
    hidden = weight_ref.shape[2]
    out_refs, (fresh, scales, rows_buf) = refs[-3 - PARTS : -3], refs[-3:]
    count = (len(refs) - 3 - PARTS) // 2
    mine_refs, other_refs = refs[:count], refs[count : 2 * count]
    piece = mine_refs[0].shape[0]
    core = place_ref[2]
    for head in range(PART_FAST):
        _, offset = window_of(head)
        for index in range(3):
            lanes = slice(index * hidden, (index + 1) * hidden)
            anchor = jnp.full((1, hidden), EPS, F32)
            length = jnp.full((1, hidden), EPS, F32)
            for step in range(count):
                at = pl.multiple_of(place_ref[4 + PARTS + step], 16)
                base = weight_ref[index, pl.ds(at + head * HEAD_DIM, piece), :].astype(F32)
                grad = jnp.where(core == head, mine_refs[step][:, lanes], other_refs[step][:, lanes]).astype(F32)
                update = base + grad
                anchor += jnp.sum(base * base, axis=0, keepdims=True)
                length += jnp.sum(update * update, axis=0, keepdims=True)
                fresh[head, index, pl.ds(at + offset, piece), :] = update.astype(BF16)
            scales[head * 3 + index, :] = (jnp.sqrt(anchor) / jnp.sqrt(length))[0]
            if offset:
                fresh[head, index, :offset, :] = jnp.zeros((offset, hidden), BF16)
            if offset + HEAD_DIM < SPAN:
                fresh[head, index, offset + HEAD_DIM :, :] = jnp.zeros((SPAN - offset - HEAD_DIM, hidden), BF16)
    parts = []
    for head in range(PART_FAST):
        begin, _ = window_of(head)
        query = query_ref[:, begin : begin + SPAN]
        scale = [scales[head * 3 + index : head * 3 + index + 1, :] for index in range(3)]
        gate = dot(query, fresh[head, 0]) * scale[0]
        upward = dot(query, fresh[head, 1]) * (scale[1] * scale[2])
        product = (gate * jax.nn.sigmoid(gate) * upward).astype(BF16)
        parts.append((begin, dot(product, fresh[head, 2], ((1,), (1,)))))
    for lane in range(0, PART_WIDTH, LANES):
        inside = [value[:, lane - begin : lane - begin + LANES] for begin, value in parts if begin <= lane < begin + SPAN]
        rows_buf[:, lane : lane + LANES] = functools.reduce(jnp.add, inside, attended_ref[:, lane : lane + LANES]).astype(BF16)
    block = out_refs[0].shape[0]
    for index, ref in enumerate(out_refs):
        begin = pl.multiple_of(place_ref[4 + PARTS + count + index] * block, block)
        ref[...] = rows_buf[pl.ds(begin, block), :]


def norm_kernel(place_ref, *refs):
    part_refs, gain_ref, out_ref, buf = refs[:PARTS], refs[PARTS], refs[PARTS + 1], refs[PARTS + 2]
    square = jnp.zeros((out_ref.shape[0], 1), F32)
    for index, ref in enumerate(part_refs):
        rows = ref[...]
        buf[place_ref[4 + index]] = rows
        wide = rows.astype(F32)
        square += jnp.sum(wide * wide, axis=1, keepdims=True)
    factor = lax.rsqrt(square / WIDTH + EPS)
    for part in range(PARTS):
        lanes = slice(part * PART_WIDTH, (part + 1) * PART_WIDTH)
        out_ref[:, lanes] = (buf[part].astype(F32) * factor * gain_ref[:, lanes]).astype(BF16)


def shards(queries, key_rows, value_rows, learn_rates, frame_order, window_ids, fast_init, norm_gain):
    tok_dev = queries.shape[0]
    hidden = fast_init.shape[0]
    sections = lax.axis_size("tok")
    plane_size = PARTS * PART_FAST
    planes = sections // plane_size
    group_rows = tok_dev * PARTS
    groups = planes * PART_FAST
    slots = tok_dev // groups
    half = WINDOW // 2
    assert PART_FAST == 2 and half == group_rows and group_rows & (group_rows - 1) == 0
    group_shift = group_rows.bit_length() - 1

    rank = lax.axis_index("tok")
    plane = rank // plane_size
    part = rank // PART_FAST % PARTS
    core = rank % PART_FAST
    row, column = part // 2, part % 2
    group = plane * PART_FAST + core

    def at(plane, row, column, core):
        return plane * plane_size + (row * 2 + column) * PART_FAST + core

    everyone = [(z, y, x, c) for z in range(planes) for y in range(2) for x in range(2) for c in range(2)]

    def permute(array, target):
        route = []
        for source in everyone:
            goal = target(*source)
            if goal is not None:
                route.append((at(*source), at(*goal)))
        return lax.ppermute(array, "tok", route)

    sources = [2 * (core ^ j // 2) + (column ^ j % 2) for j in range(PARTS)]
    bits = planes.bit_length() - 1
    piece = HEAD_DIM >> bits
    assert planes == 1 << bits and piece << bits == HEAD_DIM and piece % 16 == 0

    def owned(plane):
        return sum((plane >> bit & 1) * (HEAD_DIM >> bit + 1) for bit in range(bits))

    masks = [0]
    for bit in reversed(range(bits)):
        masks += [mask ^ 1 << bit for mask in masks]
    starts = [owned(plane ^ mask) for mask in masks]
    goals = [2 * (column ^ j % 2) + (row ^ j // 2) for j in range(PARTS)]
    place = jnp.stack([rank, part, core, group] + sources + starts + goals).astype(jnp.int32)

    def weight_part():
        own = lax.dynamic_slice_in_dim(fast_init, part * PART_WIDTH, PART_WIDTH, 2)
        return jnp.transpose(own, (1, 2, 0))

    weights = weight_part()

    full = lambda a: pl.BlockSpec(a.shape, lambda h: (0,) * a.ndim)
    steps = 2
    together = PARTS // steps
    orders = frame_order.reshape(sections, tok_dev)
    rates = learn_rates.T
    cut = pl.BlockSpec((tok_dev, WIDTH // steps), lambda h: (0, h))
    head_shape = jax.ShapeDtypeStruct((tok_dev, 2 * HEAD_DIM), BF16)
    packed, *heads_out = call(
        functools.partial(front_kernel, group_shift, slots),
        [jax.ShapeDtypeStruct((planes, PARTS, PART_FAST, slots, 3 * PART_WIDTH), BF16)] + [head_shape] * plane_size,
        [place, orders, rates, queries, key_rows, value_rows],
        in_specs=[full(orders), full(rates), cut, cut, cut],
        out_specs=[pl.BlockSpec((planes, together, PART_FAST, slots, 3 * PART_WIDTH), lambda h: (0, h, 0, 0, 0))]
        + [full(head_shape)] * plane_size,
        grid=(steps,),
        scratch=[VMEM((tok_dev, tok_dev), BF16)],
        smem=1, flops=2 * tok_dev * tok_dev * 3 * WIDTH,
    )
    heads_in = [heads_out[0]]
    for j in range(1, plane_size):
        heads_in.append(permute(heads_out[j], lambda z, y, x, c, j=j: (z, y ^ j >> 2, x ^ j >> 1 & 1, c ^ j & 1)))

    arrived = lax.all_to_all(
        packed.reshape(sections, slots, 3 * PART_WIDTH), "tok", split_axis=0, concat_axis=0, tiled=True
    ).reshape(group_rows, 3 * PART_WIDTH)

    (choose,) = call(
        functools.partial(choose_kernel, group_shift, slots),
        [jax.ShapeDtypeStruct((group_rows, group_rows), BF16)],
        [place, orders], smem=1, flops=2 * group_rows * group_rows,
    )
    kv_seq, query_seq = call(
        place_kernel,
        [jax.ShapeDtypeStruct((group_rows, width), BF16) for width in (2 * PART_WIDTH, PART_WIDTH)],
        [choose, arrived], flops=2 * group_rows * group_rows * 3 * PART_WIDTH,
    )

    swap = lambda z, y, x, c: (z, y, x, 1 - c)

    def beyond(z, y, x, c):
        goal = z + 2 * c - 1
        return (goal, y, x, 1 - c) if 0 <= goal < planes else None

    kv_chip = permute(kv_seq, swap)
    kv_far = permute(kv_seq, beyond)

    near = plane_size // 2
    tokens = near * tok_dev
    grad_scratch = [VMEM((SPAN, 3 * hidden), BF16)] + [VMEM((tokens, SPAN), BF16)] * 2
    grad_scratch += [VMEM((tokens, 2 * hidden), BF16), VMEM((tokens, hidden), BF16), VMEM((HEAD_DIM, 3 * hidden), BF16)]
    grad_flops = 12 * tokens * HEAD_DIM * hidden
    (early,) = call(
        functools.partial(grads_kernel, tokens, False),
        [jax.ShapeDtypeStruct((HEAD_DIM, 3 * hidden), BF16)], [place, weights] + heads_in[:near],
        scratch=grad_scratch, smem=1, flops=grad_flops,
    )
    send, keep = call(
        functools.partial(grads_kernel, tokens, True),
        [jax.ShapeDtypeStruct((HEAD_DIM // 2, 3 * hidden), BF16)] * 2,
        [place, weights] + heads_in[near:] + [early],
        scratch=grad_scratch, smem=1, flops=grad_flops,
    )

    def across(bit):
        return lambda z, y, x, c: (z ^ 1 << bit, y, x, c)

    def added(first, second):
        return (first.astype(F32) + second.astype(F32)).astype(BF16)

    for bit in range(bits):
        came = permute(send, across(bit))
        if bit + 1 < bits:
            size = HEAD_DIM >> bit + 2
            side = plane >> bit + 1 & 1
            cuts = [[lax.dynamic_slice_in_dim(a, at * size, size, 0) for a in (keep, came)] for at in (1 - side, side)]
            send = added(*cuts[0])
            keep = added(*cuts[1])
        else:
            total = added(keep, came)
    pieces = [total]
    for bit in reversed(range(bits)):
        fresh_pieces = []
        for held in pieces:
            fresh_pieces.append(permute(held, across(bit)))
        pieces += fresh_pieces
    pieces_other = []
    for held in pieces:
        pieces_other.append(permute(held, swap))

    block = min(LANES, group_rows)
    count = group_rows // block
    ids = window_ids.reshape(groups, group_rows)
    wide = jax.ShapeDtypeStruct((group_rows, PART_WIDTH), F32)
    assert 2 * PART_ATT <= LANES
    near_mixed, stats = call(
        functools.partial(near_kernel, block),
        [wide, jax.ShapeDtypeStruct((group_rows, LANES), F32)],
        [place, query_seq, ids, kv_seq, kv_chip],
        scratch=[VMEM((group_rows, group_rows), F32), VMEM((count, block, group_rows), F32)],
        smem=1, flops=6 * group_rows * group_rows * PART_WIDTH, limit=24,
    )
    (attended,) = call(
        functools.partial(far_kernel, block),
        [wide],
        [place, query_seq, ids, near_mixed, stats, kv_far],
        scratch=[VMEM((count, block, group_rows), F32)],
        smem=1, flops=3 * group_rows * group_rows * PART_WIDTH, limit=24,
    )

    blocks = call(
        apply_kernel,
        [jax.ShapeDtypeStruct((tok_dev, PART_WIDTH), BF16)] * PARTS,
        [place, weights, query_seq, attended] + pieces + pieces_other,
        scratch=[
            VMEM((PART_FAST, 3, SPAN, hidden), BF16),
            VMEM((PART_FAST * 3, hidden), F32),
            VMEM((group_rows, PART_WIDTH), BF16),
        ],
        smem=1, flops=6 * group_rows * PART_WIDTH * hidden, limit=40,
    )

    parts = []
    for j in range(PARTS):
        parts.append(permute(blocks[j], lambda z, y, x, c, j=j: (z, c, x ^ j % 2, y ^ j // 2)))

    (out,) = call(
        norm_kernel,
        [jax.ShapeDtypeStruct((tok_dev, WIDTH), BF16)],
        [place] + parts + [norm_gain.reshape(1, WIDTH)],
        scratch=[VMEM((PARTS, tok_dev, PART_WIDTH), BF16)],
        smem=1, flops=6 * tok_dev * WIDTH,
    )
    return out


def solution(mesh):
    rows = P(("groups", "tok"), None)
    return jax.shard_map(
        shards,
        mesh=mesh,
        in_specs=(rows, rows, rows, rows, P("groups"), P("groups"), P(), P()),
        out_specs=rows,
        check_vma=False,
    )
```

```python
import functools
import math

import jax
import jax.numpy as jnp
from jax import lax
from jax.experimental import pallas as pl
from jax.experimental.pallas import tpu as pltpu
from jax.sharding import PartitionSpec as P


HEADS = 8
HEAD_DIM = 320
ATT_DIM = 128
WINDOW = 1024
WIDTH = 2560
ATT_HEADS = 20
LANES = 128
EPS = 1e-06

PARTS = math.gcd(HEADS, ATT_HEADS)
PART_WIDTH = WIDTH // PARTS
PART_FAST = HEADS // PARTS
PART_ATT = ATT_HEADS // PARTS
SPAN = -(-HEAD_DIM // LANES) * LANES


F32 = jnp.float32
BF16 = jnp.bfloat16
VMEM = pltpu.VMEM


def iota(shape, dim):
    return lax.broadcasted_iota(jnp.int32, shape, dim)


def dot(a, b, dims=((1,), (0,))):
    return lax.dot_general(a, b, (dims, ((), ())), preferred_element_type=F32)


def column_of(row):
    n = row.shape[1]
    square = jnp.broadcast_to(row.astype(F32), (n, n))
    diagonal = iota((n, n), 0) == iota((n, n), 1)
    return jnp.sum(jnp.where(diagonal, square, 0.0), axis=1, keepdims=True)


def call(kernel, outs, ins, scratch=(), smem=0, flops=0, grid=None, in_specs=None, out_specs=None, limit=60):
    specs = [pl.BlockSpec(memory_space=pltpu.SMEM)] * smem
    specs += in_specs or [pl.BlockSpec(memory_space=VMEM)] * (len(ins) - smem)
    moved = sum(x.size * x.dtype.itemsize for x in list(ins) + list(outs))
    extra = {} if grid is None else {"grid": grid}
    return pl.pallas_call(
        kernel,
        out_shape=list(outs),
        in_specs=specs,
        out_specs=out_specs or [pl.BlockSpec(memory_space=VMEM)] * len(outs),
        scratch_shapes=list(scratch),
        compiler_params=pltpu.CompilerParams(vmem_limit_bytes=limit << 20),
        cost_estimate=pl.CostEstimate(flops=flops, bytes_accessed=moved, transcendentals=0),
        **extra,
    )(*ins)


def window_of(head):
    begin = min(head * HEAD_DIM // LANES * LANES, PART_WIDTH - SPAN)
    return begin, head * HEAD_DIM - begin


def front_kernel(group_shift, slots, place_ref, order_ref, rate_ref, query_ref, key_ref, value_ref, *refs):
    out_ref, head_refs, choose_buf = refs[0], refs[1:-1], refs[-1]
    n, _ = key_ref.shape
    planes, together, cores = out_ref.shape[:3]
    step, part, core = pl.program_id(0), place_ref[1], place_ref[2]

    @pl.when(step == 0)
    def _():
        pos = order_ref[pl.ds(place_ref[0], 1), :]
        group = lax.shift_right_logical(pos, group_shift)
        group_col = column_of(group).astype(jnp.int32)
        earlier = (group_col == group) & (iota((n, n), 0) < iota((n, n), 1))
        rank = jnp.sum(jnp.where(earlier, 1.0, 0.0), axis=0, keepdims=True)
        slot = group * slots + rank.astype(jnp.int32)
        choose_buf[...] = jnp.where(iota((n, n), 0) == slot, 1.0, 0.0).astype(BF16)

    choose = choose_buf[...]
    for index, ref in enumerate((key_ref, value_ref, query_ref)):
        lanes = slice(index * PART_WIDTH, (index + 1) * PART_WIDTH)
        for local in range(together):
            rows = dot(choose, ref[:, local * PART_WIDTH : (local + 1) * PART_WIDTH]).astype(BF16)
            for plane in range(planes):
                for at in range(cores):
                    first = (plane * cores + at) * slots
                    out_ref[plane, local, at, :, lanes] = rows[first : first + slots]

    lane = iota((n, SPAN), 1)
    tail = PART_WIDTH - SPAN
    for local in range(together):
        target_part = step * together + local
        rows = []
        for head in range(PART_FAST):
            begin, offset = window_of(head)
            span = slice(local * PART_WIDTH + begin, local * PART_WIDTH + begin + SPAN)
            rate = column_of(rate_ref[pl.ds(target_part * PART_FAST + head, 1), :])
            keys = key_ref[:, span].astype(F32)
            targets = value_ref[:, span].astype(F32) * rate
            turn = SPAN - HEAD_DIM
            if offset:
                keys = pltpu.roll(keys, SPAN - offset, 1)
            if offset != turn:
                targets = pltpu.roll(targets, turn - offset, 1)
            rows.append((keys.astype(BF16), targets.astype(BF16)))
        for flip in range(PART_FAST):
            keys, targets = (jnp.where(core == flip, one, two) for one, two in zip(*rows))
            middle = jnp.where(iota((n, LANES), 1) < HEAD_DIM - tail, keys[:, tail:], targets[:, : SPAN - tail])
            for index in range(PARTS):
                @pl.when((target_part ^ part) == index)
                def _():
                    ref = head_refs[index * PART_FAST + flip]
                    ref[:, :tail] = keys[:, :tail]
                    ref[:, tail:SPAN] = middle
                    ref[:, SPAN:] = targets[:, SPAN - tail :]


def arrival_choice(group_shift, slots, orders, group, n):
    sources, rows = orders.shape
    low_shift = group_shift // 2
    mine = lax.shift_right_logical(orders, group_shift) == group
    before = jnp.where(iota((rows, rows), 0) < iota((rows, rows), 1), 1.0, 0.0).astype(BF16)
    rank = dot(jnp.where(mine, 1.0, 0.0).astype(BF16), before)
    within = orders & ((1 << group_shift) - 1)
    digits = (lax.shift_right_logical(within, low_shift).astype(F32), (within & ((1 << low_shift) - 1)).astype(F32))
    spread = jnp.where(iota((sources, n), 1) // slots == iota((sources, n), 0), 1.0, 0.0).astype(BF16)
    keep = iota((slots, n), 1) % slots == iota((slots, n), 0)
    column = iota((sources, slots), 1)
    pos = jnp.zeros((1, n), F32)
    for digit, weight in zip(digits, (float(1 << low_shift), 1.0)):
        table = jnp.zeros((sources, slots), F32)
        for k in range(slots):
            one = jnp.sum(jnp.where(mine & (rank == float(k)), digit, 0.0), axis=1, keepdims=True)
            table = jnp.where(column == k, one, table)
        wide = dot(table.astype(BF16), spread, ((0,), (0,)))
        pos += weight * jnp.sum(jnp.where(keep, wide, 0.0), axis=0, keepdims=True)
    return jnp.where(iota((n, n), 0) == pos.astype(jnp.int32), 1.0, 0.0).astype(BF16)


def choose_kernel(group_shift, slots, place_ref, order_ref, choose_ref):
    choose_ref[...] = arrival_choice(group_shift, slots, order_ref[...], place_ref[3], choose_ref.shape[0])


def place_kernel(choose_ref, in_ref, kv_ref, q_ref):
    choose = choose_ref[...]
    kv_ref[...] = dot(choose, in_ref[:, : 2 * PART_WIDTH]).astype(BF16)
    q_ref[...] = dot(choose, in_ref[:, 2 * PART_WIDTH :]).astype(BF16)


def grads_kernel(chunk, first_start, outs, place_ref, weight_ref, *refs):
    last = outs > 1
    weight_buf, key_buf, target_buf, delta_buf, pr_buf, sums = refs[-6:]
    out_refs, in_refs = refs[-6 - outs : -6], refs[: -6 - outs]
    kv_refs, early_ref = (in_refs[:-1], in_refs[-1]) if last else (in_refs, None)
    block = kv_refs[0].shape[0]
    n = key_buf.shape[0]
    hidden = weight_ref.shape[2]
    first = pl.multiple_of(place_ref[2] * HEAD_DIM, 16)
    spare = SPAN - HEAD_DIM
    for index in range(3):
        lanes = slice(index * hidden, (index + 1) * hidden)
        begin, blank = (0, HEAD_DIM) if index < 2 else (spare, 0)
        weight_buf[begin : begin + HEAD_DIM, lanes] = weight_ref[index, pl.ds(first, HEAD_DIM), :]
        weight_buf[blank : blank + spare, lanes] = jnp.zeros((spare, hidden), BF16)
    for index, ref in enumerate(kv_refs):
        here = pl.ds(index * block, block)
        key_buf[here, :] = ref[:, :SPAN]
        target_buf[here, :] = ref[:, PART_WIDTH - SPAN :]
    for at in range(0, n, chunk):
        here = pl.ds(at, chunk)
        both = dot(key_buf[here, :], weight_buf[:, : 2 * hidden])
        gate, upward = both[:, :hidden], both[:, hidden:]
        backward = dot(target_buf[here, :], weight_buf[:, 2 * hidden :])
        sigmoid = jax.nn.sigmoid(gate)
        active = gate * sigmoid
        pr_buf[here, :] = (active * upward).astype(BF16)
        delta_buf[here, hidden:] = (backward * active).astype(BF16)
        delta_buf[here, :hidden] = (backward * upward * sigmoid * (1.0 + gate * (1.0 - sigmoid))).astype(BF16)
    for left, right, begin, row in ((key_buf, delta_buf, 0, 0), (target_buf, pr_buf, 2 * hidden, spare)):
        lanes = slice(begin, begin + right.shape[1])
        total = dot(left[...], right[...], ((0,), (0,)))[row : row + HEAD_DIM]
        if last:
            sums[:, lanes] = (total + early_ref[:, lanes].astype(F32)).astype(BF16)
        else:
            out_refs[0][:, lanes] = total.astype(BF16)
    if last:
        for index, ref in enumerate(out_refs):
            begin = pl.multiple_of(place_ref[first_start + index], 16)
            ref[...] = sums[pl.ds(begin, ref.shape[0]), :]


FACTOR = ATT_DIM ** (-0.5) * math.log2(math.e)


def reach(before, index, count, block):
    at = pl.multiple_of(jnp.where(before, index, count - 1 - index) * block, block)
    return at, pl.multiple_of(jnp.where(before, at, 0), block), jnp.where(before, -count * block, count * block - at)


def block_ids(ids, index, count, block, turned):
    turn = count - 1 - index
    row = jnp.where(turned, ids[:, turn * block : (turn + 1) * block], ids[:, index * block : (index + 1) * block])
    return column_of(row).astype(jnp.int32)


def mask_of(own, ids, shift):
    gap = iota((own.shape[0], ids.shape[1]), 1) - iota((own.shape[0], ids.shape[1]), 0) + shift
    return jnp.where((gap < WINDOW // 2) & (gap > -(WINDOW // 2)) & (own == ids), 0.0, -1e30)


def head_lanes(head):
    return pl.ds(pl.multiple_of(head * ATT_DIM, ATT_DIM), ATT_DIM), pl.ds(pl.multiple_of(PART_WIDTH + head * ATT_DIM, ATT_DIM), ATT_DIM)


def near_kernel(block, place_ref, query_ref, ids_ref, kv_ref, chip_ref, out_ref, stat_ref, bias, chip_bias):
    n = query_ref.shape[0]
    count = n // block
    core, group = place_ref[2], place_ref[3]
    second = core == 1
    ids = ids_ref[pl.ds(group, 1), :]
    for index in range(count):
        at = index * block
        bias[at : at + block, :] = mask_of(column_of(ids[:, at : at + block]).astype(jnp.int32), ids, -at)
    for index in range(count):
        _, _, shift = reach(second, count - 1 - index, count, block)
        size = (index + 1) * block
        own = block_ids(ids, index, count, block, second)
        other = ids_ref[pl.ds(group + 1 - 2 * core, 1), :]
        other = jnp.where(second, other[:, n - size :], other[:, :size])
        chip_bias[index, :, :size] = mask_of(own, other, shift)
    stat_ref[...] = jnp.zeros_like(stat_ref)
    lane = iota((block, LANES), 1)

    @pl.loop(0, PART_ATT)
    def _(head):
        keys, values = head_lanes(head)
        for index in range(count):
            at, start, _ = reach(second, count - 1 - index, count, block)
            size = (index + 1) * block
            here, there = pl.ds(at, block), pl.ds(start, size)
            query = query_ref[here, keys]
            score = dot(query, kv_ref[:, keys], ((1,), (1,))) + bias[here, :]
            chip = dot(query, chip_ref[there, keys], ((1,), (1,))) + chip_bias[index, :, :size]
            peak = jnp.maximum(jnp.max(score, axis=1, keepdims=True), jnp.max(chip, axis=1, keepdims=True))
            score = jnp.exp2((score - peak) * FACTOR)
            chip = jnp.exp2((chip - peak) * FACTOR)
            total = jnp.sum(score, axis=1, keepdims=True) + jnp.sum(chip, axis=1, keepdims=True)
            out_ref[here, keys] = dot(score.astype(BF16), kv_ref[:, values]) + dot(chip.astype(BF16), chip_ref[there, values])
            stat = jnp.where(lane == 2 * head, peak, stat_ref[here, :])
            stat_ref[here, :] = jnp.where(lane == 2 * head + 1, total, stat)


def far_kernel(block, place_ref, query_ref, ids_ref, near_ref, stat_ref, kv_ref, out_ref, bias):
    n = query_ref.shape[0]
    count = n // block
    core, group = place_ref[2], place_ref[3]
    last = ids_ref.shape[0] - 1
    first = core == 0
    beyond = group - 1 + 2 * core
    exists = (beyond >= 0) & (beyond <= last)
    ids = ids_ref[pl.ds(group, 1), :]
    for index in range(count):
        _, _, shift = reach(first, index, count, block)
        size = n - index * block
        own = block_ids(ids, index, count, block, core == 1)
        other = ids_ref[pl.ds(jnp.clip(beyond, 0, last), 1), :]
        other = jnp.where(first, other[:, n - size :], other[:, :size])
        bias[index, :, :size] = mask_of(own, jnp.where(exists, other, -1), shift)
    lane = iota((block, LANES), 1)

    @pl.loop(0, PART_ATT)
    def _(head):
        keys, values = head_lanes(head)
        for index in range(count):
            at, start, _ = reach(first, index, count, block)
            size = n - index * block
            here, there = pl.ds(at, block), pl.ds(start, size)
            score = dot(query_ref[here, keys], kv_ref[there, keys], ((1,), (1,))) + bias[index, :, :size]
            stat = stat_ref[here, :]
            old_peak = jnp.sum(jnp.where(lane == 2 * head, stat, 0.0), axis=1, keepdims=True)
            old_total = jnp.sum(jnp.where(lane == 2 * head + 1, stat, 0.0), axis=1, keepdims=True)
            peak = jnp.maximum(jnp.max(score, axis=1, keepdims=True), old_peak)
            keep = jnp.exp2((old_peak - peak) * FACTOR)
            score = jnp.exp2((score - peak) * FACTOR)
            total = old_total * keep + jnp.sum(score, axis=1, keepdims=True)
            mixed = near_ref[here, keys] * keep + dot(score.astype(BF16), kv_ref[there, values])
            out_ref[here, keys] = mixed / total


def apply_kernel(first_goal, first_rows, place_ref, weight_ref, query_ref, attended_ref, *refs):
    hidden = weight_ref.shape[2]
    out_refs, (fresh, scales, rows_buf) = refs[-3 - PARTS : -3], refs[-3:]
    count = (len(refs) - 3 - PARTS) // 2
    mine_refs, other_refs = refs[:count], refs[count : 2 * count]
    core = place_ref[2]
    for head in range(PART_FAST):
        _, offset = window_of(head)
        for index in range(3):
            lanes = slice(index * hidden, (index + 1) * hidden)
            anchor = jnp.full((1, hidden), EPS, F32)
            length = jnp.full((1, hidden), EPS, F32)
            for step in range(count):
                piece = mine_refs[step].shape[0]
                at = pl.multiple_of(place_ref[first_rows + step], 16)
                base = weight_ref[index, pl.ds(at + head * HEAD_DIM, piece), :].astype(F32)
                grad = jnp.where(core == head, mine_refs[step][:, lanes], other_refs[step][:, lanes]).astype(F32)
                update = base + grad
                anchor += jnp.sum(base * base, axis=0, keepdims=True)
                length += jnp.sum(update * update, axis=0, keepdims=True)
                fresh[head, index, pl.ds(at + offset, piece), :] = update.astype(BF16)
            scales[head * 3 + index, :] = (jnp.sqrt(anchor) / jnp.sqrt(length))[0]
            if offset:
                fresh[head, index, :offset, :] = jnp.zeros((offset, hidden), BF16)
            if offset + HEAD_DIM < SPAN:
                fresh[head, index, offset + HEAD_DIM :, :] = jnp.zeros((SPAN - offset - HEAD_DIM, hidden), BF16)
    parts = []
    for head in range(PART_FAST):
        begin, _ = window_of(head)
        query = query_ref[:, begin : begin + SPAN]
        scale = [scales[head * 3 + index : head * 3 + index + 1, :] for index in range(3)]
        gate = dot(query, fresh[head, 0]) * scale[0]
        upward = dot(query, fresh[head, 1]) * (scale[1] * scale[2])
        product = (gate * jax.nn.sigmoid(gate) * upward).astype(BF16)
        parts.append((begin, dot(product, fresh[head, 2], ((1,), (1,)))))
    for lane in range(0, PART_WIDTH, LANES):
        inside = [value[:, lane - begin : lane - begin + LANES] for begin, value in parts if begin <= lane < begin + SPAN]
        rows_buf[:, lane : lane + LANES] = functools.reduce(jnp.add, inside, attended_ref[:, lane : lane + LANES]).astype(BF16)
    block = out_refs[0].shape[0]
    for index, ref in enumerate(out_refs):
        begin = pl.multiple_of(place_ref[first_goal + index] * block, block)
        ref[...] = rows_buf[pl.ds(begin, block), :]


def norm_kernel(place_ref, *refs):
    part_refs, gain_ref, out_ref, buf = refs[:PARTS], refs[PARTS], refs[PARTS + 1], refs[PARTS + 2]
    square = jnp.zeros((out_ref.shape[0], 1), F32)
    for index, ref in enumerate(part_refs):
        rows = ref[...]
        buf[place_ref[4 + index]] = rows
        wide = rows.astype(F32)
        square += jnp.sum(wide * wide, axis=1, keepdims=True)
    factor = lax.rsqrt(square / WIDTH + EPS)
    for part in range(PARTS):
        lanes = slice(part * PART_WIDTH, (part + 1) * PART_WIDTH)
        out_ref[:, lanes] = (buf[part].astype(F32) * factor * gain_ref[:, lanes]).astype(BF16)


def gather_layout(bits, piece, relay):
    layout = [(0, 0, piece)]
    for bit in reversed(range(bits)):
        for mask, begin, size in list(layout):
            cuts = [(begin, size)]
            if mask == 0 and bit == bits - 1 and bits > 1:
                cuts = [(0, relay), (relay, piece - relay)]
            layout += [(mask ^ 1 << bit, first, count) for first, count in cuts]
    return layout


def shards(queries, key_rows, value_rows, learn_rates, frame_order, window_ids, fast_init, norm_gain):
    tok_dev = queries.shape[0]
    hidden = fast_init.shape[0]
    sections = lax.axis_size("tok")
    plane_size = PARTS * PART_FAST
    planes = sections // plane_size
    group_rows = tok_dev * PARTS
    groups = planes * PART_FAST
    slots = tok_dev // groups
    half = WINDOW // 2
    assert PART_FAST == 2 and half == group_rows and group_rows & (group_rows - 1) == 0
    group_shift = group_rows.bit_length() - 1

    rank = lax.axis_index("tok")
    plane = rank // plane_size
    part = rank // PART_FAST % PARTS
    core = rank % PART_FAST
    row, column = part // 2, part % 2
    group = plane * PART_FAST + core

    def at(plane, row, column, core):
        return plane * plane_size + (row * 2 + column) * PART_FAST + core

    everyone = [(z, y, x, c) for z in range(planes) for y in range(2) for x in range(2) for c in range(2)]

    def permute(array, target):
        route = []
        for source in everyone:
            goal = target(*source)
            if goal is not None:
                route.append((at(*source), at(*goal)))
        return lax.ppermute(array, "tok", route)

    sources = [2 * (core ^ j // 2) + (column ^ j % 2) for j in range(PARTS)]
    bits = planes.bit_length() - 1
    piece = HEAD_DIM >> bits
    assert planes == 1 << bits and piece << bits == HEAD_DIM and piece % 16 == 0

    def owned(plane):
        return sum((plane >> bit & 1) * (HEAD_DIM >> bit + 1) for bit in range(bits))

    relay = -(-piece // 32) * 16
    layout = gather_layout(bits, piece, relay)
    starts = [owned(plane ^ mask) for mask in range(planes)]
    rows_from = [starts[mask] + begin for mask, begin, _ in layout]
    goals = [2 * (column ^ j % 2) + (row ^ j // 2) for j in range(PARTS)]
    first_start = 4 + PARTS
    first_goal = first_start + planes
    first_rows = first_goal + PARTS
    place = jnp.stack([rank, part, core, group] + sources + starts + goals + rows_from).astype(jnp.int32)

    def weight_part():
        own = lax.dynamic_slice_in_dim(fast_init, part * PART_WIDTH, PART_WIDTH, 2)
        return jnp.transpose(own, (1, 2, 0))

    weights = weight_part()

    full = lambda a: pl.BlockSpec(a.shape, lambda h: (0,) * a.ndim)
    steps = 2
    together = PARTS // steps
    orders = frame_order.reshape(sections, tok_dev)
    rates = learn_rates.T
    cut = pl.BlockSpec((tok_dev, WIDTH // steps), lambda h: (0, h))
    head_shape = jax.ShapeDtypeStruct((tok_dev, 2 * HEAD_DIM), BF16)
    packed, *heads_out = call(
        functools.partial(front_kernel, group_shift, slots),
        [jax.ShapeDtypeStruct((planes, PARTS, PART_FAST, slots, 3 * PART_WIDTH), BF16)] + [head_shape] * plane_size,
        [place, orders, rates, queries, key_rows, value_rows],
        in_specs=[full(orders), full(rates), cut, cut, cut],
        out_specs=[pl.BlockSpec((planes, together, PART_FAST, slots, 3 * PART_WIDTH), lambda h: (0, h, 0, 0, 0))]
        + [full(head_shape)] * plane_size,
        grid=(steps,),
        scratch=[VMEM((tok_dev, tok_dev), BF16)],
        smem=1, flops=2 * tok_dev * tok_dev * 3 * WIDTH,
    )
    heads_in = [heads_out[0]]
    send_order = [2, 3, 6, 7, 4, 5, 1]
    for j in range(1, plane_size):
        heads_in.append(permute(heads_out[j], lambda z, y, x, c, j=j: (z, y ^ j >> 2, x ^ j >> 1 & 1, c ^ j & 1)))

    arrived = lax.all_to_all(
        packed.reshape(sections, slots, 3 * PART_WIDTH), "tok", split_axis=0, concat_axis=0, tiled=True
    ).reshape(group_rows, 3 * PART_WIDTH)

    (choose,) = call(
        functools.partial(choose_kernel, group_shift, slots),
        [jax.ShapeDtypeStruct((group_rows, group_rows), BF16)],
        [place, orders], smem=1, flops=2 * group_rows * group_rows,
    )
    kv_seq, query_seq = call(
        place_kernel,
        [jax.ShapeDtypeStruct((group_rows, width), BF16) for width in (2 * PART_WIDTH, PART_WIDTH)],
        [choose, arrived], flops=2 * group_rows * group_rows * 3 * PART_WIDTH,
    )

    swap = lambda z, y, x, c: (z, y, x, 1 - c)

    def beyond(z, y, x, c):
        goal = z + 2 * c - 1
        return (goal, y, x, 1 - c) if 0 <= goal < planes else None

    kv_chip = permute(kv_seq, swap)
    kv_far = permute(kv_seq, beyond)

    near = plane_size // 2
    tokens = near * tok_dev
    by_arrival = [heads_in[0]] + [heads_in[j] for j in send_order]
    early_heads, late_heads = by_arrival[:near], by_arrival[near:]
    grad_scratch = [VMEM((SPAN, 3 * hidden), BF16)] + [VMEM((tokens, SPAN), BF16)] * 2
    grad_scratch += [VMEM((tokens, 2 * hidden), BF16), VMEM((tokens, hidden), BF16), VMEM((HEAD_DIM, 3 * hidden), BF16)]
    grad_flops = 12 * tokens * HEAD_DIM * hidden
    (early,) = call(
        functools.partial(grads_kernel, tokens, first_start, 1),
        [jax.ShapeDtypeStruct((HEAD_DIM, 3 * hidden), BF16)], [place, weights] + early_heads,
        scratch=grad_scratch, smem=1, flops=grad_flops,
    )
    quarters = call(
        functools.partial(grads_kernel, tokens, first_start, planes),
        [jax.ShapeDtypeStruct((piece, 3 * hidden), BF16)] * planes,
        [place, weights] + late_heads + [early],
        scratch=grad_scratch, smem=1, flops=grad_flops,
    )

    def across(bit):
        return lambda z, y, x, c: (z ^ 1 << bit, y, x, c)

    def added(first, second):
        return (first.astype(F32) + second.astype(F32)).astype(BF16)

    held = dict(enumerate(quarters))
    for bit in range(bits):
        flip = 1 << bit
        for mask in sorted([mask for mask in held if mask & flip], reverse=True):
            came = permute(held.pop(mask), across(bit))
            kept = held[mask ^ flip]
            held[mask ^ flip] = added(kept, came)
    total = held[0]
    pieces = [total]
    sent = {(0, 0, piece): total}
    for mask, begin, size in layout[1:]:
        bit = [bit for bit in range(bits) if mask >> bit & 1][0]
        source = (mask ^ 1 << bit, begin, size)
        if source not in sent:
            sent[source] = added(kept[begin : begin + size], came[begin : begin + size])
        sent[mask, begin, size] = permute(sent[source], across(bit))
        pieces.append(sent[mask, begin, size])
    pieces_other = []
    for held_piece in pieces:
        pieces_other.append(permute(held_piece, swap))

    block = min(LANES, group_rows)
    count = group_rows // block
    ids = window_ids.reshape(groups, group_rows)
    wide = jax.ShapeDtypeStruct((group_rows, PART_WIDTH), F32)
    assert 2 * PART_ATT <= LANES
    near_mixed, stats = call(
        functools.partial(near_kernel, block),
        [wide, jax.ShapeDtypeStruct((group_rows, LANES), F32)],
        [place, query_seq, ids, kv_seq, kv_chip],
        scratch=[VMEM((group_rows, group_rows), F32), VMEM((count, block, group_rows), F32)],
        smem=1, flops=6 * group_rows * group_rows * PART_WIDTH, limit=24,
    )
    (attended,) = call(
        functools.partial(far_kernel, block),
        [wide],
        [place, query_seq, ids, near_mixed, stats, kv_far],
        scratch=[VMEM((count, block, group_rows), F32)],
        smem=1, flops=3 * group_rows * group_rows * PART_WIDTH, limit=24,
    )

    blocks = call(
        functools.partial(apply_kernel, first_goal, first_rows),
        [jax.ShapeDtypeStruct((tok_dev, PART_WIDTH), BF16)] * PARTS,
        [place, weights, query_seq, attended] + pieces + pieces_other,
        scratch=[
            VMEM((PART_FAST, 3, SPAN, hidden), BF16),
            VMEM((PART_FAST * 3, hidden), F32),
            VMEM((group_rows, PART_WIDTH), BF16),
        ],
        smem=1, flops=6 * group_rows * PART_WIDTH * hidden, limit=40,
    )

    parts = []
    for j in range(PARTS):
        parts.append(permute(blocks[j], lambda z, y, x, c, j=j: (z, c, x ^ j % 2, y ^ j // 2)))

    (out,) = call(
        norm_kernel,
        [jax.ShapeDtypeStruct((tok_dev, WIDTH), BF16)],
        [place] + parts + [norm_gain.reshape(1, WIDTH)],
        scratch=[VMEM((PARTS, tok_dev, PART_WIDTH), BF16)],
        smem=1, flops=6 * tok_dev * WIDTH,
    )
    return out


def solution(mesh):
    rows = P(("groups", "tok"), None)
    return jax.shard_map(
        shards,
        mesh=mesh,
        in_specs=(rows, rows, rows, rows, P("groups"), P("groups"), P(), P()),
        out_specs=rows,
        check_vma=False,
    )
```

```python
import functools
import math

import jax
import jax.numpy as jnp
from jax import lax
from jax.experimental import pallas as pl
from jax.experimental.pallas import tpu as pltpu
from jax.sharding import PartitionSpec as P


HEADS = 8
HEAD_DIM = 320
ATT_DIM = 128
WINDOW = 1024
WIDTH = 2560
ATT_HEADS = 20
LANES = 128
EPS = 1e-06

PARTS = math.gcd(HEADS, ATT_HEADS)
PART_WIDTH = WIDTH // PARTS
PART_FAST = HEADS // PARTS
PART_ATT = ATT_HEADS // PARTS
SPAN = -(-HEAD_DIM // LANES) * LANES


F32 = jnp.float32
BF16 = jnp.bfloat16
VMEM = pltpu.VMEM


def iota(shape, dim):
    return lax.broadcasted_iota(jnp.int32, shape, dim)


def dot(a, b, dims=((1,), (0,))):
    return lax.dot_general(a, b, (dims, ((), ())), preferred_element_type=F32)


def column_of(row):
    n = row.shape[1]
    square = jnp.broadcast_to(row.astype(F32), (n, n))
    diagonal = iota((n, n), 0) == iota((n, n), 1)
    return jnp.sum(jnp.where(diagonal, square, 0.0), axis=1, keepdims=True)


def call(kernel, outs, ins, scratch=(), smem=0, flops=0, grid=None, in_specs=None, out_specs=None, limit=60):
    specs = [pl.BlockSpec(memory_space=pltpu.SMEM)] * smem
    specs += in_specs or [pl.BlockSpec(memory_space=VMEM)] * (len(ins) - smem)
    moved = sum(x.size * x.dtype.itemsize for x in list(ins) + list(outs))
    extra = {} if grid is None else {"grid": grid}
    return pl.pallas_call(
        kernel,
        out_shape=list(outs),
        in_specs=specs,
        out_specs=out_specs or [pl.BlockSpec(memory_space=VMEM)] * len(outs),
        scratch_shapes=list(scratch),
        compiler_params=pltpu.CompilerParams(vmem_limit_bytes=limit << 20),
        cost_estimate=pl.CostEstimate(flops=flops, bytes_accessed=moved, transcendentals=0),
        **extra,
    )(*ins)


def window_of(head):
    begin = min(head * HEAD_DIM // LANES * LANES, PART_WIDTH - SPAN)
    return begin, head * HEAD_DIM - begin


def front_kernel(group_shift, slots, place_ref, order_ref, rate_ref, query_ref, key_ref, value_ref, *refs):
    out_ref, head_refs, choose_buf = refs[0], refs[1:-1], refs[-1]
    n, _ = key_ref.shape
    planes, together, cores = out_ref.shape[:3]
    step, part, core = pl.program_id(0), place_ref[1], place_ref[2]

    @pl.when(step == 0)
    def _():
        pos = order_ref[pl.ds(place_ref[0], 1), :]
        group = lax.shift_right_logical(pos, group_shift)
        group_col = column_of(group).astype(jnp.int32)
        earlier = (group_col == group) & (iota((n, n), 0) < iota((n, n), 1))
        rank = jnp.sum(jnp.where(earlier, 1.0, 0.0), axis=0, keepdims=True)
        slot = group * slots + rank.astype(jnp.int32)
        choose_buf[...] = jnp.where(iota((n, n), 0) == slot, 1.0, 0.0).astype(BF16)

    choose = choose_buf[...]
    for index, ref in enumerate((key_ref, value_ref, query_ref)):
        lanes = slice(index * PART_WIDTH, (index + 1) * PART_WIDTH)
        for local in range(together):
            rows = dot(choose, ref[:, local * PART_WIDTH : (local + 1) * PART_WIDTH]).astype(BF16)
            for plane in range(planes):
                for at in range(cores):
                    first = (plane * cores + at) * slots
                    out_ref[plane, local, at, :, lanes] = rows[first : first + slots]

    lane = iota((n, SPAN), 1)
    tail = PART_WIDTH - SPAN
    for local in range(together):
        target_part = step * together + local
        rows = []
        for head in range(PART_FAST):
            begin, offset = window_of(head)
            span = slice(local * PART_WIDTH + begin, local * PART_WIDTH + begin + SPAN)
            rate = column_of(rate_ref[pl.ds(target_part * PART_FAST + head, 1), :])
            keys = key_ref[:, span].astype(F32)
            targets = value_ref[:, span].astype(F32) * rate
            turn = SPAN - HEAD_DIM
            if offset:
                keys = pltpu.roll(keys, SPAN - offset, 1)
            if offset != turn:
                targets = pltpu.roll(targets, turn - offset, 1)
            rows.append((keys.astype(BF16), targets.astype(BF16)))
        for flip in range(PART_FAST):
            keys, targets = (jnp.where(core == flip, one, two) for one, two in zip(*rows))
            middle = jnp.where(iota((n, LANES), 1) < HEAD_DIM - tail, keys[:, tail:], targets[:, : SPAN - tail])
            for index in range(PARTS):
                @pl.when((target_part ^ part) == index)
                def _():
                    ref = head_refs[index * PART_FAST + flip]
                    ref[:, :tail] = keys[:, :tail]
                    ref[:, tail:SPAN] = middle
                    ref[:, SPAN:] = targets[:, SPAN - tail :]


def arrival_choice(group_shift, slots, orders, group, n):
    sources, rows = orders.shape
    low_shift = group_shift // 2
    mine = lax.shift_right_logical(orders, group_shift) == group
    before = jnp.where(iota((rows, rows), 0) < iota((rows, rows), 1), 1.0, 0.0).astype(BF16)
    rank = dot(jnp.where(mine, 1.0, 0.0).astype(BF16), before)
    within = orders & ((1 << group_shift) - 1)
    digits = (lax.shift_right_logical(within, low_shift).astype(F32), (within & ((1 << low_shift) - 1)).astype(F32))
    spread = jnp.where(iota((sources, n), 1) // slots == iota((sources, n), 0), 1.0, 0.0).astype(BF16)
    keep = iota((slots, n), 1) % slots == iota((slots, n), 0)
    column = iota((sources, slots), 1)
    pos = jnp.zeros((1, n), F32)
    for digit, weight in zip(digits, (float(1 << low_shift), 1.0)):
        table = jnp.zeros((sources, slots), F32)
        for k in range(slots):
            one = jnp.sum(jnp.where(mine & (rank == float(k)), digit, 0.0), axis=1, keepdims=True)
            table = jnp.where(column == k, one, table)
        wide = dot(table.astype(BF16), spread, ((0,), (0,)))
        pos += weight * jnp.sum(jnp.where(keep, wide, 0.0), axis=0, keepdims=True)
    return jnp.where(iota((n, n), 0) == pos.astype(jnp.int32), 1.0, 0.0).astype(BF16)


def choose_kernel(group_shift, slots, place_ref, order_ref, choose_ref):
    choose_ref[...] = arrival_choice(group_shift, slots, order_ref[...], place_ref[3], choose_ref.shape[0])


def place_kernel(choose_ref, in_ref, kv_ref, q_ref):
    choose = choose_ref[...]
    kv_ref[...] = dot(choose, in_ref[:, : 2 * PART_WIDTH]).astype(BF16)
    q_ref[...] = dot(choose, in_ref[:, 2 * PART_WIDTH :]).astype(BF16)


def grads_kernel(chunk, first_start, outs, place_ref, weight_ref, *refs):
    last = outs > 1
    weight_buf, key_buf, target_buf, delta_buf, pr_buf, sums = refs[-6:]
    out_refs, in_refs = refs[-6 - outs : -6], refs[: -6 - outs]
    kv_refs, early_ref = (in_refs[:-1], in_refs[-1]) if last else (in_refs, None)
    block = kv_refs[0].shape[0]
    n = key_buf.shape[0]
    hidden = weight_ref.shape[2]
    first = pl.multiple_of(place_ref[2] * HEAD_DIM, 16)
    spare = SPAN - HEAD_DIM
    for index in range(3):
        lanes = slice(index * hidden, (index + 1) * hidden)
        begin, blank = (0, HEAD_DIM) if index < 2 else (spare, 0)
        weight_buf[begin : begin + HEAD_DIM, lanes] = weight_ref[index, pl.ds(first, HEAD_DIM), :]
        weight_buf[blank : blank + spare, lanes] = jnp.zeros((spare, hidden), BF16)
    for index, ref in enumerate(kv_refs):
        here = pl.ds(index * block, block)
        key_buf[here, :] = ref[:, :SPAN]
        target_buf[here, :] = ref[:, PART_WIDTH - SPAN :]
    for at in range(0, n, chunk):
        here = pl.ds(at, chunk)
        both = dot(key_buf[here, :], weight_buf[:, : 2 * hidden])
        gate, upward = both[:, :hidden], both[:, hidden:]
        backward = dot(target_buf[here, :], weight_buf[:, 2 * hidden :])
        sigmoid = jax.nn.sigmoid(gate)
        active = gate * sigmoid
        pr_buf[here, :] = (active * upward).astype(BF16)
        delta_buf[here, hidden:] = (backward * active).astype(BF16)
        delta_buf[here, :hidden] = (backward * upward * sigmoid * (1.0 + gate * (1.0 - sigmoid))).astype(BF16)
    for left, right, begin, row in ((key_buf, delta_buf, 0, 0), (target_buf, pr_buf, 2 * hidden, spare)):
        lanes = slice(begin, begin + right.shape[1])
        total = dot(left[...], right[...], ((0,), (0,)))[row : row + HEAD_DIM]
        if last:
            sums[:, lanes] = (total + early_ref[:, lanes].astype(F32)).astype(BF16)
        else:
            out_refs[0][:, lanes] = total.astype(BF16)
    if last:
        for index, ref in enumerate(out_refs):
            begin = pl.multiple_of(place_ref[first_start + index], 16)
            ref[...] = sums[pl.ds(begin, ref.shape[0]), :]


FACTOR = ATT_DIM ** (-0.5) * math.log2(math.e)


def reach(before, index, count, block):
    at = pl.multiple_of(jnp.where(before, index, count - 1 - index) * block, block)
    return at, pl.multiple_of(jnp.where(before, at, 0), block), jnp.where(before, -count * block, count * block - at)


def block_ids(ids, index, count, block, turned):
    turn = count - 1 - index
    row = jnp.where(turned, ids[:, turn * block : (turn + 1) * block], ids[:, index * block : (index + 1) * block])
    return column_of(row).astype(jnp.int32)


def mask_of(own, ids, shift):
    gap = iota((own.shape[0], ids.shape[1]), 1) - iota((own.shape[0], ids.shape[1]), 0) + shift
    return jnp.where((gap < WINDOW // 2) & (gap > -(WINDOW // 2)) & (own == ids), 0.0, -1e30)


def head_lanes(head):
    return pl.ds(pl.multiple_of(head * ATT_DIM, ATT_DIM), ATT_DIM), pl.ds(pl.multiple_of(PART_WIDTH + head * ATT_DIM, ATT_DIM), ATT_DIM)


def near_kernel(block, place_ref, query_ref, ids_ref, kv_ref, chip_ref, out_ref, stat_ref, bias, chip_bias):
    n = query_ref.shape[0]
    count = n // block
    core, group = place_ref[2], place_ref[3]
    second = core == 1
    ids = ids_ref[pl.ds(group, 1), :]
    for index in range(count):
        at = index * block
        bias[at : at + block, :] = mask_of(column_of(ids[:, at : at + block]).astype(jnp.int32), ids, -at)
    for index in range(count):
        _, _, shift = reach(second, count - 1 - index, count, block)
        size = (index + 1) * block
        own = block_ids(ids, index, count, block, second)
        other = ids_ref[pl.ds(group + 1 - 2 * core, 1), :]
        other = jnp.where(second, other[:, n - size :], other[:, :size])
        chip_bias[index, :, :size] = mask_of(own, other, shift)
    stat_ref[...] = jnp.zeros_like(stat_ref)
    lane = iota((block, LANES), 1)

    @pl.loop(0, PART_ATT)
    def _(head):
        keys, values = head_lanes(head)
        for index in range(count):
            at, start, _ = reach(second, count - 1 - index, count, block)
            size = (index + 1) * block
            here, there = pl.ds(at, block), pl.ds(start, size)
            query = query_ref[here, keys]
            score = dot(query, kv_ref[:, keys], ((1,), (1,))) + bias[here, :]
            chip = dot(query, chip_ref[there, keys], ((1,), (1,))) + chip_bias[index, :, :size]
            peak = jnp.maximum(jnp.max(score, axis=1, keepdims=True), jnp.max(chip, axis=1, keepdims=True))
            score = jnp.exp2((score - peak) * FACTOR)
            chip = jnp.exp2((chip - peak) * FACTOR)
            total = jnp.sum(score, axis=1, keepdims=True) + jnp.sum(chip, axis=1, keepdims=True)
            out_ref[here, keys] = dot(score.astype(BF16), kv_ref[:, values]) + dot(chip.astype(BF16), chip_ref[there, values])
            stat = jnp.where(lane == 2 * head, peak, stat_ref[here, :])
            stat_ref[here, :] = jnp.where(lane == 2 * head + 1, total, stat)


def far_kernel(block, place_ref, query_ref, ids_ref, near_ref, stat_ref, kv_ref, out_ref, bias):
    n = query_ref.shape[0]
    count = n // block
    core, group = place_ref[2], place_ref[3]
    last = ids_ref.shape[0] - 1
    first = core == 0
    beyond = group - 1 + 2 * core
    exists = (beyond >= 0) & (beyond <= last)
    ids = ids_ref[pl.ds(group, 1), :]
    for index in range(count):
        _, _, shift = reach(first, index, count, block)
        size = n - index * block
        own = block_ids(ids, index, count, block, core == 1)
        other = ids_ref[pl.ds(jnp.clip(beyond, 0, last), 1), :]
        other = jnp.where(first, other[:, n - size :], other[:, :size])
        bias[index, :, :size] = mask_of(own, jnp.where(exists, other, -1), shift)
    lane = iota((block, LANES), 1)

    @pl.loop(0, PART_ATT)
    def _(head):
        keys, values = head_lanes(head)
        for index in range(count):
            at, start, _ = reach(first, index, count, block)
            size = n - index * block
            here, there = pl.ds(at, block), pl.ds(start, size)
            score = dot(query_ref[here, keys], kv_ref[there, keys], ((1,), (1,))) + bias[index, :, :size]
            stat = stat_ref[here, :]
            old_peak = jnp.sum(jnp.where(lane == 2 * head, stat, 0.0), axis=1, keepdims=True)
            old_total = jnp.sum(jnp.where(lane == 2 * head + 1, stat, 0.0), axis=1, keepdims=True)
            peak = jnp.maximum(jnp.max(score, axis=1, keepdims=True), old_peak)
            keep = jnp.exp2((old_peak - peak) * FACTOR)
            score = jnp.exp2((score - peak) * FACTOR)
            total = old_total * keep + jnp.sum(score, axis=1, keepdims=True)
            mixed = near_ref[here, keys] * keep + dot(score.astype(BF16), kv_ref[there, values])
            out_ref[here, keys] = mixed / total


def apply_kernel(first_goal, first_rows, place_ref, weight_ref, query_ref, attended_ref, *refs):
    hidden = weight_ref.shape[2]
    out_refs, (fresh, scales, rows_buf) = refs[-3 - PARTS : -3], refs[-3:]
    count = (len(refs) - 3 - PARTS) // 2
    mine_refs, other_refs = refs[:count], refs[count : 2 * count]
    core = place_ref[2]
    for head in range(PART_FAST):
        _, offset = window_of(head)
        for index in range(3):
            lanes = slice(index * hidden, (index + 1) * hidden)
            anchor = jnp.full((1, hidden), EPS, F32)
            length = jnp.full((1, hidden), EPS, F32)
            for step in range(count):
                piece = mine_refs[step].shape[0]
                at = pl.multiple_of(place_ref[first_rows + step], 16)
                base = weight_ref[index, pl.ds(at + head * HEAD_DIM, piece), :].astype(F32)
                grad = jnp.where(core == head, mine_refs[step][:, lanes], other_refs[step][:, lanes]).astype(F32)
                update = base + grad
                anchor += jnp.sum(base * base, axis=0, keepdims=True)
                length += jnp.sum(update * update, axis=0, keepdims=True)
                fresh[head, index, pl.ds(at + offset, piece), :] = update.astype(BF16)
            scales[head * 3 + index, :] = (jnp.sqrt(anchor) / jnp.sqrt(length))[0]
            if offset:
                fresh[head, index, :offset, :] = jnp.zeros((offset, hidden), BF16)
            if offset + HEAD_DIM < SPAN:
                fresh[head, index, offset + HEAD_DIM :, :] = jnp.zeros((SPAN - offset - HEAD_DIM, hidden), BF16)
    parts = []
    for head in range(PART_FAST):
        begin, _ = window_of(head)
        query = query_ref[:, begin : begin + SPAN]
        scale = [scales[head * 3 + index : head * 3 + index + 1, :] for index in range(3)]
        gate = dot(query, fresh[head, 0]) * scale[0]
        upward = dot(query, fresh[head, 1]) * (scale[1] * scale[2])
        product = (gate * jax.nn.sigmoid(gate) * upward).astype(BF16)
        parts.append((begin, dot(product, fresh[head, 2], ((1,), (1,)))))
    for lane in range(0, PART_WIDTH, LANES):
        inside = [value[:, lane - begin : lane - begin + LANES] for begin, value in parts if begin <= lane < begin + SPAN]
        rows_buf[:, lane : lane + LANES] = functools.reduce(jnp.add, inside, attended_ref[:, lane : lane + LANES]).astype(BF16)
    block = out_refs[0].shape[0]
    for index, ref in enumerate(out_refs):
        begin = pl.multiple_of(place_ref[first_goal + index] * block, block)
        ref[...] = rows_buf[pl.ds(begin, block), :]


def norm_kernel(place_ref, gain_ref, *refs):
    part_refs, (out_ref, buf, sems) = refs[:PARTS], refs[PARTS:]
    copies = []
    for index, ref in enumerate(part_refs):
        begin = pl.multiple_of(place_ref[4 + index] * PART_WIDTH, LANES)
        copies.append(pltpu.make_async_copy(ref, buf.at[:, pl.ds(begin, PART_WIDTH)], sems.at[index]))
    for copy in copies:
        copy.start()
    for copy in copies:
        copy.wait()
    rows = buf[...].astype(F32)
    square = jnp.sum(rows * rows, axis=1, keepdims=True)
    out_ref[...] = (rows * lax.rsqrt(square / WIDTH + EPS) * gain_ref[...]).astype(BF16)


def gather_layout(bits, piece, relay):
    layout = [(0, 0, piece)]
    for bit in reversed(range(bits)):
        for mask, begin, size in list(layout):
            cuts = [(begin, size)]
            if mask == 0 and bit == bits - 1 and bits > 1:
                cuts = [(0, relay), (relay, piece - relay)]
            layout += [(mask ^ 1 << bit, first, count) for first, count in cuts]
    return layout


def shards(queries, key_rows, value_rows, learn_rates, frame_order, window_ids, fast_init, norm_gain):
    tok_dev = queries.shape[0]
    hidden = fast_init.shape[0]
    sections = lax.axis_size("tok")
    plane_size = PARTS * PART_FAST
    planes = sections // plane_size
    group_rows = tok_dev * PARTS
    groups = planes * PART_FAST
    slots = tok_dev // groups
    half = WINDOW // 2
    assert PART_FAST == 2 and half == group_rows and group_rows & (group_rows - 1) == 0
    group_shift = group_rows.bit_length() - 1

    rank = lax.axis_index("tok")
    plane = rank // plane_size
    part = rank // PART_FAST % PARTS
    core = rank % PART_FAST
    row, column = part // 2, part % 2
    group = plane * PART_FAST + core

    def at(plane, row, column, core):
        return plane * plane_size + (row * 2 + column) * PART_FAST + core

    everyone = [(z, y, x, c) for z in range(planes) for y in range(2) for x in range(2) for c in range(2)]

    def permute(array, target):
        route = []
        for source in everyone:
            goal = target(*source)
            if goal is not None:
                route.append((at(*source), at(*goal)))
        return lax.ppermute(array, "tok", route)

    sources = [2 * (core ^ j // 2) + (column ^ j % 2) for j in range(PARTS)]
    bits = planes.bit_length() - 1
    piece = HEAD_DIM >> bits
    assert planes == 1 << bits and piece << bits == HEAD_DIM and piece % 16 == 0

    def owned(plane):
        return sum((plane >> bit & 1) * (HEAD_DIM >> bit + 1) for bit in range(bits))

    relay = -(-piece // 32) * 16
    layout = gather_layout(bits, piece, relay)
    starts = [owned(plane ^ mask) for mask in range(planes)]
    rows_from = [starts[mask] + begin for mask, begin, _ in layout]
    goals = [2 * (column ^ j % 2) + (row ^ j // 2) for j in range(PARTS)]
    first_start = 4 + PARTS
    first_goal = first_start + planes
    first_rows = first_goal + PARTS
    place = jnp.stack([rank, part, core, group] + sources + starts + goals + rows_from).astype(jnp.int32)

    def weight_part():
        own = lax.dynamic_slice_in_dim(fast_init, part * PART_WIDTH, PART_WIDTH, 2)
        return jnp.transpose(own, (1, 2, 0))

    weights = weight_part()

    full = lambda a: pl.BlockSpec(a.shape, lambda h: (0,) * a.ndim)
    steps = 2
    together = PARTS // steps
    orders = frame_order.reshape(sections, tok_dev)
    rates = learn_rates.T
    cut = pl.BlockSpec((tok_dev, WIDTH // steps), lambda h: (0, h))
    head_shape = jax.ShapeDtypeStruct((tok_dev, 2 * HEAD_DIM), BF16)
    packed, *heads_out = call(
        functools.partial(front_kernel, group_shift, slots),
        [jax.ShapeDtypeStruct((planes, PARTS, PART_FAST, slots, 3 * PART_WIDTH), BF16)] + [head_shape] * plane_size,
        [place, orders, rates, queries, key_rows, value_rows],
        in_specs=[full(orders), full(rates), cut, cut, cut],
        out_specs=[pl.BlockSpec((planes, together, PART_FAST, slots, 3 * PART_WIDTH), lambda h: (0, h, 0, 0, 0))]
        + [full(head_shape)] * plane_size,
        grid=(steps,),
        scratch=[VMEM((tok_dev, tok_dev), BF16)],
        smem=1, flops=2 * tok_dev * tok_dev * 3 * WIDTH,
    )
    heads_in = [heads_out[0]]
    send_order = [2, 3, 6, 7, 4, 5, 1]
    for j in range(1, plane_size):
        heads_in.append(permute(heads_out[j], lambda z, y, x, c, j=j: (z, y ^ j >> 2, x ^ j >> 1 & 1, c ^ j & 1)))

    arrived = lax.all_to_all(
        packed.reshape(sections, slots, 3 * PART_WIDTH), "tok", split_axis=0, concat_axis=0, tiled=True
    ).reshape(group_rows, 3 * PART_WIDTH)

    (choose,) = call(
        functools.partial(choose_kernel, group_shift, slots),
        [jax.ShapeDtypeStruct((group_rows, group_rows), BF16)],
        [place, orders], smem=1, flops=2 * group_rows * group_rows,
    )
    kv_seq, query_seq = call(
        place_kernel,
        [jax.ShapeDtypeStruct((group_rows, width), BF16) for width in (2 * PART_WIDTH, PART_WIDTH)],
        [choose, arrived], flops=2 * group_rows * group_rows * 3 * PART_WIDTH,
    )

    swap = lambda z, y, x, c: (z, y, x, 1 - c)

    def beyond(z, y, x, c):
        goal = z + 2 * c - 1
        return (goal, y, x, 1 - c) if 0 <= goal < planes else None

    kv_chip = permute(kv_seq, swap)
    kv_far = permute(kv_seq, beyond)

    near = plane_size // 2
    tokens = near * tok_dev
    by_arrival = [heads_in[0]] + [heads_in[j] for j in send_order]
    early_heads, late_heads = by_arrival[:near], by_arrival[near:]
    grad_scratch = [VMEM((SPAN, 3 * hidden), BF16)] + [VMEM((tokens, SPAN), BF16)] * 2
    grad_scratch += [VMEM((tokens, 2 * hidden), BF16), VMEM((tokens, hidden), BF16), VMEM((HEAD_DIM, 3 * hidden), BF16)]
    grad_flops = 12 * tokens * HEAD_DIM * hidden
    (early,) = call(
        functools.partial(grads_kernel, tokens, first_start, 1),
        [jax.ShapeDtypeStruct((HEAD_DIM, 3 * hidden), BF16)], [place, weights] + early_heads,
        scratch=grad_scratch, smem=1, flops=grad_flops,
    )
    quarters = call(
        functools.partial(grads_kernel, tokens, first_start, planes),
        [jax.ShapeDtypeStruct((piece, 3 * hidden), BF16)] * planes,
        [place, weights] + late_heads + [early],
        scratch=grad_scratch, smem=1, flops=grad_flops,
    )

    def across(bit):
        return lambda z, y, x, c: (z ^ 1 << bit, y, x, c)

    def added(first, second):
        return (first.astype(F32) + second.astype(F32)).astype(BF16)

    held = dict(enumerate(quarters))
    for bit in range(bits):
        flip = 1 << bit
        for mask in sorted([mask for mask in held if mask & flip], reverse=True):
            came = permute(held.pop(mask), across(bit))
            kept = held[mask ^ flip]
            held[mask ^ flip] = added(kept, came)
    total = held[0]
    pieces = [total]
    sent = {(0, 0, piece): total}
    for mask, begin, size in layout[1:]:
        bit = [bit for bit in range(bits) if mask >> bit & 1][0]
        source = (mask ^ 1 << bit, begin, size)
        if source not in sent:
            sent[source] = added(kept[begin : begin + size], came[begin : begin + size])
        sent[mask, begin, size] = permute(sent[source], across(bit))
        pieces.append(sent[mask, begin, size])
    pieces_other = []
    for held_piece in pieces:
        pieces_other.append(permute(held_piece, swap))

    block = min(LANES, group_rows)
    count = group_rows // block
    ids = window_ids.reshape(groups, group_rows)
    wide = jax.ShapeDtypeStruct((group_rows, PART_WIDTH), F32)
    assert 2 * PART_ATT <= LANES
    near_mixed, stats = call(
        functools.partial(near_kernel, block),
        [wide, jax.ShapeDtypeStruct((group_rows, LANES), F32)],
        [place, query_seq, ids, kv_seq, kv_chip],
        scratch=[VMEM((group_rows, group_rows), F32), VMEM((count, block, group_rows), F32)],
        smem=1, flops=6 * group_rows * group_rows * PART_WIDTH, limit=24,
    )
    (attended,) = call(
        functools.partial(far_kernel, block),
        [wide],
        [place, query_seq, ids, near_mixed, stats, kv_far],
        scratch=[VMEM((count, block, group_rows), F32)],
        smem=1, flops=3 * group_rows * group_rows * PART_WIDTH, limit=24,
    )

    blocks = call(
        functools.partial(apply_kernel, first_goal, first_rows),
        [jax.ShapeDtypeStruct((tok_dev, PART_WIDTH), BF16)] * PARTS,
        [place, weights, query_seq, attended] + pieces + pieces_other,
        scratch=[
            VMEM((PART_FAST, 3, SPAN, hidden), BF16),
            VMEM((PART_FAST * 3, hidden), F32),
            VMEM((group_rows, PART_WIDTH), BF16),
        ],
        smem=1, flops=6 * group_rows * PART_WIDTH * hidden, limit=40,
    )

    parts = []
    for j in range(PARTS):
        parts.append(permute(blocks[j], lambda z, y, x, c, j=j: (z, c, x ^ j % 2, y ^ j // 2)))

    (out,) = call(
        norm_kernel,
        [jax.ShapeDtypeStruct((tok_dev, WIDTH), BF16)],
        [place, norm_gain.reshape(1, WIDTH)] + parts,
        in_specs=[pl.BlockSpec(memory_space=VMEM)] + [pl.BlockSpec(memory_space=pltpu.HBM)] * PARTS,
        scratch=[VMEM((tok_dev, WIDTH), BF16), pltpu.SemaphoreType.DMA((PARTS,))],
        smem=1, flops=6 * tok_dev * WIDTH,
    )
    return out


def solution(mesh):
    rows = P(("groups", "tok"), None)
    return jax.shard_map(
        shards,
        mesh=mesh,
        in_specs=(rows, rows, rows, rows, P("groups"), P("groups"), P(), P()),
        out_specs=rows,
        check_vma=False,
    )
```

```python
import functools
import math

import jax
import jax.numpy as jnp
from jax import lax
from jax.experimental import pallas as pl
from jax.experimental.pallas import tpu as pltpu
from jax.sharding import PartitionSpec as P


HEADS = 8
HEAD_DIM = 320
ATT_DIM = 128
WINDOW = 1024
WIDTH = 2560
ATT_HEADS = 20
LANES = 128
EPS = 1e-06

PARTS = math.gcd(HEADS, ATT_HEADS)
PART_WIDTH = WIDTH // PARTS
PART_FAST = HEADS // PARTS
PART_ATT = ATT_HEADS // PARTS
SPAN = -(-HEAD_DIM // LANES) * LANES


VMEM_BYTES = 67043328

F32 = jnp.float32
BF16 = jnp.bfloat16
VMEM = pltpu.VMEM


def iota(shape, dim):
    return lax.broadcasted_iota(jnp.int32, shape, dim)


def dot(a, b, dims=((1,), (0,))):
    return lax.dot_general(a, b, (dims, ((), ())), preferred_element_type=F32)


def column_of(row):
    n = row.shape[1]
    square = jnp.broadcast_to(row.astype(F32), (n, n))
    diagonal = iota((n, n), 0) == iota((n, n), 1)
    return jnp.sum(jnp.where(diagonal, square, 0.0), axis=1, keepdims=True)


def call(kernel, outs, ins, scratch=(), smem=0, flops=0, grid=None, in_specs=None, out_specs=None, limit=60):
    specs = [pl.BlockSpec(memory_space=pltpu.SMEM)] * smem
    specs += in_specs or [pl.BlockSpec(memory_space=VMEM)] * (len(ins) - smem)
    moved = sum(x.size * x.dtype.itemsize for x in list(ins) + list(outs))
    extra = {} if grid is None else {"grid": grid}
    return pl.pallas_call(
        kernel,
        out_shape=list(outs),
        in_specs=specs,
        out_specs=out_specs or [pl.BlockSpec(memory_space=VMEM)] * len(outs),
        scratch_shapes=list(scratch),
        compiler_params=pltpu.CompilerParams(vmem_limit_bytes=min(limit << 20, VMEM_BYTES)),
        cost_estimate=pl.CostEstimate(flops=flops, bytes_accessed=moved, transcendentals=0),
        **extra,
    )(*ins)


def window_of(head):
    begin = min(head * HEAD_DIM // LANES * LANES, PART_WIDTH - SPAN)
    return begin, head * HEAD_DIM - begin


def front_kernel(group_shift, slots, place_ref, order_ref, rate_ref, query_ref, key_ref, value_ref, *refs):
    out_ref, head_refs, choose_buf = refs[0], refs[1:-1], refs[-1]
    n, _ = key_ref.shape
    planes, together, cores = out_ref.shape[:3]
    step, part, core = pl.program_id(0), place_ref[1], place_ref[2]

    @pl.when(step == 0)
    def _():
        pos = order_ref[pl.ds(place_ref[0], 1), :]
        group = lax.shift_right_logical(pos, group_shift)
        group_col = column_of(group).astype(jnp.int32)
        earlier = (group_col == group) & (iota((n, n), 0) < iota((n, n), 1))
        rank = jnp.sum(jnp.where(earlier, 1.0, 0.0), axis=0, keepdims=True)
        slot = group * slots + rank.astype(jnp.int32)
        choose_buf[...] = jnp.where(iota((n, n), 0) == slot, 1.0, 0.0).astype(BF16)

    choose = choose_buf[...]
    for index, ref in enumerate((key_ref, value_ref, query_ref)):
        lanes = slice(index * PART_WIDTH, (index + 1) * PART_WIDTH)
        for local in range(together):
            rows = dot(choose, ref[:, local * PART_WIDTH : (local + 1) * PART_WIDTH]).astype(BF16)
            for plane in range(planes):
                for at in range(cores):
                    first = (plane * cores + at) * slots
                    out_ref[plane, local, at, :, lanes] = rows[first : first + slots]

    lane = iota((n, SPAN), 1)
    tail = PART_WIDTH - SPAN
    for local in range(together):
        target_part = step * together + local
        rows = []
        for head in range(PART_FAST):
            begin, offset = window_of(head)
            span = slice(local * PART_WIDTH + begin, local * PART_WIDTH + begin + SPAN)
            rate = column_of(rate_ref[pl.ds(target_part * PART_FAST + head, 1), :])
            keys = key_ref[:, span].astype(F32)
            targets = value_ref[:, span].astype(F32) * rate
            turn = SPAN - HEAD_DIM
            if offset:
                keys = pltpu.roll(keys, SPAN - offset, 1)
            if offset != turn:
                targets = pltpu.roll(targets, turn - offset, 1)
            rows.append((keys.astype(BF16), targets.astype(BF16)))
        for flip in range(PART_FAST):
            keys, targets = (jnp.where(core == flip, one, two) for one, two in zip(*rows))
            middle = jnp.where(iota((n, LANES), 1) < HEAD_DIM - tail, keys[:, tail:], targets[:, : SPAN - tail])
            for index in range(PARTS):
                @pl.when((target_part ^ part) == index)
                def _():
                    ref = head_refs[index * PART_FAST + flip]
                    ref[:, :tail] = keys[:, :tail]
                    ref[:, tail:SPAN] = middle
                    ref[:, SPAN:] = targets[:, SPAN - tail :]


def arrival_choice(group_shift, slots, orders, group, n):
    sources, rows = orders.shape
    low_shift = group_shift // 2
    mine = lax.shift_right_logical(orders, group_shift) == group
    before = jnp.where(iota((rows, rows), 0) < iota((rows, rows), 1), 1.0, 0.0).astype(BF16)
    rank = dot(jnp.where(mine, 1.0, 0.0).astype(BF16), before)
    within = orders & ((1 << group_shift) - 1)
    digits = (lax.shift_right_logical(within, low_shift).astype(F32), (within & ((1 << low_shift) - 1)).astype(F32))
    spread = jnp.where(iota((sources, n), 1) // slots == iota((sources, n), 0), 1.0, 0.0).astype(BF16)
    keep = iota((slots, n), 1) % slots == iota((slots, n), 0)
    column = iota((sources, slots), 1)
    pos = jnp.zeros((1, n), F32)
    for digit, weight in zip(digits, (float(1 << low_shift), 1.0)):
        table = jnp.zeros((sources, slots), F32)
        for k in range(slots):
            one = jnp.sum(jnp.where(mine & (rank == float(k)), digit, 0.0), axis=1, keepdims=True)
            table = jnp.where(column == k, one, table)
        wide = dot(table.astype(BF16), spread, ((0,), (0,)))
        pos += weight * jnp.sum(jnp.where(keep, wide, 0.0), axis=0, keepdims=True)
    return jnp.where(iota((n, n), 0) == pos.astype(jnp.int32), 1.0, 0.0).astype(BF16)


def choose_kernel(group_shift, slots, place_ref, order_ref, choose_ref):
    choose_ref[...] = arrival_choice(group_shift, slots, order_ref[...], place_ref[3], choose_ref.shape[0])


def place_kernel(choose_ref, in_ref, kv_ref, q_ref):
    choose = choose_ref[...]
    kv_ref[...] = dot(choose, in_ref[:, : 2 * PART_WIDTH]).astype(BF16)
    q_ref[...] = dot(choose, in_ref[:, 2 * PART_WIDTH :]).astype(BF16)


def grads_kernel(chunk, first_start, outs, place_ref, weight_ref, *refs):
    last = outs > 1
    weight_buf, key_buf, target_buf, delta_buf, pr_buf, sums = refs[-6:]
    out_refs, in_refs = refs[-6 - outs : -6], refs[: -6 - outs]
    kv_refs, early_ref = (in_refs[:-1], in_refs[-1]) if last else (in_refs, None)
    block = kv_refs[0].shape[0]
    n = key_buf.shape[0]
    hidden = weight_ref.shape[2]
    first = pl.multiple_of(place_ref[2] * HEAD_DIM, 16)
    spare = SPAN - HEAD_DIM
    for index in range(3):
        lanes = slice(index * hidden, (index + 1) * hidden)
        begin, blank = (0, HEAD_DIM) if index < 2 else (spare, 0)
        weight_buf[begin : begin + HEAD_DIM, lanes] = weight_ref[index, pl.ds(first, HEAD_DIM), :]
        weight_buf[blank : blank + spare, lanes] = jnp.zeros((spare, hidden), BF16)
    for index, ref in enumerate(kv_refs):
        here = pl.ds(index * block, block)
        key_buf[here, :] = ref[:, :SPAN]
        target_buf[here, :] = ref[:, PART_WIDTH - SPAN :]
    for at in range(0, n, chunk):
        here = pl.ds(at, chunk)
        both = dot(key_buf[here, :], weight_buf[:, : 2 * hidden])
        gate, upward = both[:, :hidden], both[:, hidden:]
        backward = dot(target_buf[here, :], weight_buf[:, 2 * hidden :])
        sigmoid = jax.nn.sigmoid(gate)
        active = gate * sigmoid
        pr_buf[here, :] = (active * upward).astype(BF16)
        delta_buf[here, hidden:] = (backward * active).astype(BF16)
        delta_buf[here, :hidden] = (backward * upward * sigmoid * (1.0 + gate * (1.0 - sigmoid))).astype(BF16)
    for left, right, begin, row in ((key_buf, delta_buf, 0, 0), (target_buf, pr_buf, 2 * hidden, spare)):
        lanes = slice(begin, begin + right.shape[1])
        total = dot(left[...], right[...], ((0,), (0,)))[row : row + HEAD_DIM]
        if last:
            sums[:, lanes] = (total + early_ref[:, lanes].astype(F32)).astype(BF16)
        else:
            out_refs[0][:, lanes] = total.astype(BF16)
    if last:
        for index, ref in enumerate(out_refs):
            begin = pl.multiple_of(place_ref[first_start + index], 16)
            ref[...] = sums[pl.ds(begin, ref.shape[0]), :]


FACTOR = ATT_DIM ** (-0.5) * math.log2(math.e)


def reach(before, index, count, block):
    at = pl.multiple_of(jnp.where(before, index, count - 1 - index) * block, block)
    return at, pl.multiple_of(jnp.where(before, at, 0), block), jnp.where(before, -count * block, count * block - at)


def block_ids(ids, index, count, block, turned):
    turn = count - 1 - index
    row = jnp.where(turned, ids[:, turn * block : (turn + 1) * block], ids[:, index * block : (index + 1) * block])
    return column_of(row).astype(jnp.int32)


def mask_of(own, ids, shift):
    gap = iota((own.shape[0], ids.shape[1]), 1) - iota((own.shape[0], ids.shape[1]), 0) + shift
    return jnp.where((gap < WINDOW // 2) & (gap > -(WINDOW // 2)) & (own == ids), 0.0, -1e30)


def head_lanes(head):
    return pl.ds(pl.multiple_of(head * ATT_DIM, ATT_DIM), ATT_DIM), pl.ds(pl.multiple_of(PART_WIDTH + head * ATT_DIM, ATT_DIM), ATT_DIM)


def near_kernel(block, place_ref, query_ref, ids_ref, kv_ref, chip_ref, out_ref, stat_ref, bias, chip_bias):
    n = query_ref.shape[0]
    count = n // block
    core, group = place_ref[2], place_ref[3]
    second = core == 1
    ids = ids_ref[pl.ds(group, 1), :]
    for index in range(count):
        at = index * block
        bias[at : at + block, :] = mask_of(column_of(ids[:, at : at + block]).astype(jnp.int32), ids, -at)
    for index in range(count):
        _, _, shift = reach(second, count - 1 - index, count, block)
        size = (index + 1) * block
        own = block_ids(ids, index, count, block, second)
        other = ids_ref[pl.ds(group + 1 - 2 * core, 1), :]
        other = jnp.where(second, other[:, n - size :], other[:, :size])
        chip_bias[index, :, :size] = mask_of(own, other, shift)
    stat_ref[...] = jnp.zeros_like(stat_ref)
    lane = iota((block, LANES), 1)

    @pl.loop(0, PART_ATT)
    def _(head):
        keys, values = head_lanes(head)
        for index in range(count):
            at, start, _ = reach(second, count - 1 - index, count, block)
            size = (index + 1) * block
            here, there = pl.ds(at, block), pl.ds(start, size)
            query = query_ref[here, keys]
            score = dot(query, kv_ref[:, keys], ((1,), (1,))) + bias[here, :]
            chip = dot(query, chip_ref[there, keys], ((1,), (1,))) + chip_bias[index, :, :size]
            peak = jnp.maximum(jnp.max(score, axis=1, keepdims=True), jnp.max(chip, axis=1, keepdims=True))
            score = jnp.exp2((score - peak) * FACTOR)
            chip = jnp.exp2((chip - peak) * FACTOR)
            total = jnp.sum(score, axis=1, keepdims=True) + jnp.sum(chip, axis=1, keepdims=True)
            out_ref[here, keys] = dot(score.astype(BF16), kv_ref[:, values]) + dot(chip.astype(BF16), chip_ref[there, values])
            stat = jnp.where(lane == 2 * head, peak, stat_ref[here, :])
            stat_ref[here, :] = jnp.where(lane == 2 * head + 1, total, stat)


def far_kernel(block, place_ref, query_ref, ids_ref, near_ref, stat_ref, kv_ref, out_ref, bias):
    n = query_ref.shape[0]
    count = n // block
    core, group = place_ref[2], place_ref[3]
    last = ids_ref.shape[0] - 1
    first = core == 0
    beyond = group - 1 + 2 * core
    exists = (beyond >= 0) & (beyond <= last)
    ids = ids_ref[pl.ds(group, 1), :]
    for index in range(count):
        _, _, shift = reach(first, index, count, block)
        size = n - index * block
        own = block_ids(ids, index, count, block, core == 1)
        other = ids_ref[pl.ds(jnp.clip(beyond, 0, last), 1), :]
        other = jnp.where(first, other[:, n - size :], other[:, :size])
        bias[index, :, :size] = mask_of(own, jnp.where(exists, other, -1), shift)
    lane = iota((block, LANES), 1)

    @pl.loop(0, PART_ATT)
    def _(head):
        keys, values = head_lanes(head)
        for index in range(count):
            at, start, _ = reach(first, index, count, block)
            size = n - index * block
            here, there = pl.ds(at, block), pl.ds(start, size)
            score = dot(query_ref[here, keys], kv_ref[there, keys], ((1,), (1,))) + bias[index, :, :size]
            stat = stat_ref[here, :]
            old_peak = jnp.sum(jnp.where(lane == 2 * head, stat, 0.0), axis=1, keepdims=True)
            old_total = jnp.sum(jnp.where(lane == 2 * head + 1, stat, 0.0), axis=1, keepdims=True)
            peak = jnp.maximum(jnp.max(score, axis=1, keepdims=True), old_peak)
            keep = jnp.exp2((old_peak - peak) * FACTOR)
            score = jnp.exp2((score - peak) * FACTOR)
            total = old_total * keep + jnp.sum(score, axis=1, keepdims=True)
            mixed = near_ref[here, keys] * keep + dot(score.astype(BF16), kv_ref[there, values])
            out_ref[here, keys] = mixed / total


def apply_kernel(first_goal, first_rows, place_ref, weight_ref, query_ref, attended_ref, *refs):
    hidden = weight_ref.shape[2]
    out_refs, (fresh, scales, rows_buf) = refs[-3 - PARTS : -3], refs[-3:]
    count = (len(refs) - 3 - PARTS) // 2
    mine_refs, other_refs = refs[:count], refs[count : 2 * count]
    core = place_ref[2]
    for head in range(PART_FAST):
        _, offset = window_of(head)
        for index in range(3):
            lanes = slice(index * hidden, (index + 1) * hidden)
            anchor = jnp.full((1, hidden), EPS, F32)
            length = jnp.full((1, hidden), EPS, F32)
            for step in range(count):
                piece = mine_refs[step].shape[0]
                at = pl.multiple_of(place_ref[first_rows + step], 16)
                base = weight_ref[index, pl.ds(at + head * HEAD_DIM, piece), :].astype(F32)
                grad = jnp.where(core == head, mine_refs[step][:, lanes], other_refs[step][:, lanes]).astype(F32)
                update = base + grad
                anchor += jnp.sum(base * base, axis=0, keepdims=True)
                length += jnp.sum(update * update, axis=0, keepdims=True)
                fresh[head, index, pl.ds(at + offset, piece), :] = update.astype(BF16)
            scales[head * 3 + index, :] = (jnp.sqrt(anchor) / jnp.sqrt(length))[0]
            if offset:
                fresh[head, index, :offset, :] = jnp.zeros((offset, hidden), BF16)
            if offset + HEAD_DIM < SPAN:
                fresh[head, index, offset + HEAD_DIM :, :] = jnp.zeros((SPAN - offset - HEAD_DIM, hidden), BF16)
    parts = []
    for head in range(PART_FAST):
        begin, _ = window_of(head)
        query = query_ref[:, begin : begin + SPAN]
        scale = [scales[head * 3 + index : head * 3 + index + 1, :] for index in range(3)]
        gate = dot(query, fresh[head, 0]) * scale[0]
        upward = dot(query, fresh[head, 1]) * (scale[1] * scale[2])
        product = (gate * jax.nn.sigmoid(gate) * upward).astype(BF16)
        parts.append((begin, dot(product, fresh[head, 2], ((1,), (1,)))))
    for lane in range(0, PART_WIDTH, LANES):
        inside = [value[:, lane - begin : lane - begin + LANES] for begin, value in parts if begin <= lane < begin + SPAN]
        rows_buf[:, lane : lane + LANES] = functools.reduce(jnp.add, inside, attended_ref[:, lane : lane + LANES]).astype(BF16)
    block = out_refs[0].shape[0]
    for index, ref in enumerate(out_refs):
        begin = pl.multiple_of(place_ref[first_goal + index] * block, block)
        ref[...] = rows_buf[pl.ds(begin, block), :]


def norm_kernel(place_ref, *refs):
    part_refs, gain_ref, out_ref, buf = refs[:PARTS], refs[PARTS], refs[PARTS + 1], refs[PARTS + 2]
    square = jnp.zeros((out_ref.shape[0], 1), F32)
    for index, ref in enumerate(part_refs):
        rows = ref[...]
        buf[place_ref[4 + index]] = rows
        wide = rows.astype(F32)
        square += jnp.sum(wide * wide, axis=1, keepdims=True)
    factor = lax.rsqrt(square / WIDTH + EPS)
    for part in range(PARTS):
        lanes = slice(part * PART_WIDTH, (part + 1) * PART_WIDTH)
        out_ref[:, lanes] = (buf[part].astype(F32) * factor * gain_ref[:, lanes]).astype(BF16)


def gather_layout(bits, piece, relay):
    layout = [(0, 0, piece)]
    for bit in reversed(range(bits)):
        for mask, begin, size in list(layout):
            cuts = [(begin, size)]
            if mask == 0 and bit == bits - 1 and bits > 1:
                cuts = [(0, relay), (relay, piece - relay)]
            layout += [(mask ^ 1 << bit, first, count) for first, count in cuts]
    return layout


def shards(queries, key_rows, value_rows, learn_rates, frame_order, window_ids, fast_init, norm_gain):
    tok_dev = queries.shape[0]
    hidden = fast_init.shape[0]
    sections = lax.axis_size("tok")
    plane_size = PARTS * PART_FAST
    planes = sections // plane_size
    group_rows = tok_dev * PARTS
    groups = planes * PART_FAST
    slots = tok_dev // groups
    half = WINDOW // 2
    assert PART_FAST == 2 and half == group_rows and group_rows & (group_rows - 1) == 0
    group_shift = group_rows.bit_length() - 1

    rank = lax.axis_index("tok")
    plane = rank // plane_size
    part = rank // PART_FAST % PARTS
    core = rank % PART_FAST
    row, column = part // 2, part % 2
    group = plane * PART_FAST + core

    def at(plane, row, column, core):
        return plane * plane_size + (row * 2 + column) * PART_FAST + core

    everyone = [(z, y, x, c) for z in range(planes) for y in range(2) for x in range(2) for c in range(2)]

    def permute(array, target):
        route = []
        for source in everyone:
            goal = target(*source)
            if goal is not None:
                route.append((at(*source), at(*goal)))
        return lax.ppermute(array, "tok", route)

    sources = [2 * (core ^ j // 2) + (column ^ j % 2) for j in range(PARTS)]
    bits = planes.bit_length() - 1
    piece = HEAD_DIM >> bits
    assert planes == 1 << bits and piece << bits == HEAD_DIM and piece % 16 == 0

    def owned(plane):
        return sum((plane >> bit & 1) * (HEAD_DIM >> bit + 1) for bit in range(bits))

    relay = -(-piece // 32) * 16
    layout = gather_layout(bits, piece, relay)
    starts = [owned(plane ^ mask) for mask in range(planes)]
    rows_from = [starts[mask] + begin for mask, begin, _ in layout]
    goals = [2 * (column ^ j % 2) + (row ^ j // 2) for j in range(PARTS)]
    first_start = 4 + PARTS
    first_goal = first_start + planes
    first_rows = first_goal + PARTS
    place = jnp.stack([rank, part, core, group] + sources + starts + goals + rows_from).astype(jnp.int32)

    def weight_part():
        own = lax.dynamic_slice_in_dim(fast_init, part * PART_WIDTH, PART_WIDTH, 2)
        return jnp.transpose(own, (1, 2, 0))

    weights = weight_part()

    full = lambda a: pl.BlockSpec(a.shape, lambda h: (0,) * a.ndim)
    steps = 2
    together = PARTS // steps
    orders = frame_order.reshape(sections, tok_dev)
    rates = learn_rates.T
    cut = pl.BlockSpec((tok_dev, WIDTH // steps), lambda h: (0, h))
    head_shape = jax.ShapeDtypeStruct((tok_dev, 2 * HEAD_DIM), BF16)
    packed, *heads_out = call(
        functools.partial(front_kernel, group_shift, slots),
        [jax.ShapeDtypeStruct((planes, PARTS, PART_FAST, slots, 3 * PART_WIDTH), BF16)] + [head_shape] * plane_size,
        [place, orders, rates, queries, key_rows, value_rows],
        in_specs=[full(orders), full(rates), cut, cut, cut],
        out_specs=[pl.BlockSpec((planes, together, PART_FAST, slots, 3 * PART_WIDTH), lambda h: (0, h, 0, 0, 0))]
        + [full(head_shape)] * plane_size,
        grid=(steps,),
        scratch=[VMEM((tok_dev, tok_dev), BF16)],
        smem=1, flops=2 * tok_dev * tok_dev * 3 * WIDTH,
    )
    heads_in = [heads_out[0]]
    send_order = [2, 4, 3, 5, 6, 7, 1]
    for j in range(1, plane_size):
        heads_in.append(permute(heads_out[j], lambda z, y, x, c, j=j: (z, y ^ j >> 2, x ^ j >> 1 & 1, c ^ j & 1)))

    arrived = lax.all_to_all(
        packed.reshape(sections, slots, 3 * PART_WIDTH), "tok", split_axis=0, concat_axis=0, tiled=True
    ).reshape(group_rows, 3 * PART_WIDTH)

    (choose,) = call(
        functools.partial(choose_kernel, group_shift, slots),
        [jax.ShapeDtypeStruct((group_rows, group_rows), BF16)],
        [place, orders], smem=1, flops=2 * group_rows * group_rows,
    )
    kv_seq, query_seq = call(
        place_kernel,
        [jax.ShapeDtypeStruct((group_rows, width), BF16) for width in (2 * PART_WIDTH, PART_WIDTH)],
        [choose, arrived], flops=2 * group_rows * group_rows * 3 * PART_WIDTH,
    )

    swap = lambda z, y, x, c: (z, y, x, 1 - c)

    def beyond(z, y, x, c):
        goal = z + 2 * c - 1
        return (goal, y, x, 1 - c) if 0 <= goal < planes else None

    kv_chip = permute(kv_seq, swap)
    kv_far = permute(kv_seq, beyond)

    near = plane_size // 2
    tokens = near * tok_dev
    by_arrival = [heads_in[0]] + [heads_in[j] for j in send_order]
    early_heads, late_heads = by_arrival[:near], by_arrival[near:]
    grad_scratch = [VMEM((SPAN, 3 * hidden), BF16)] + [VMEM((tokens, SPAN), BF16)] * 2
    grad_scratch += [VMEM((tokens, 2 * hidden), BF16), VMEM((tokens, hidden), BF16), VMEM((HEAD_DIM, 3 * hidden), BF16)]
    grad_flops = 12 * tokens * HEAD_DIM * hidden
    (early,) = call(
        functools.partial(grads_kernel, tokens, first_start, 1),
        [jax.ShapeDtypeStruct((HEAD_DIM, 3 * hidden), BF16)], [place, weights] + early_heads,
        scratch=grad_scratch, smem=1, flops=grad_flops,
    )
    quarters = call(
        functools.partial(grads_kernel, tokens, first_start, planes),
        [jax.ShapeDtypeStruct((piece, 3 * hidden), BF16)] * planes,
        [place, weights] + late_heads + [early],
        scratch=grad_scratch, smem=1, flops=grad_flops,
    )

    def across(bit):
        return lambda z, y, x, c: (z ^ 1 << bit, y, x, c)

    def added(first, second):
        return (first.astype(F32) + second.astype(F32)).astype(BF16)

    held = dict(enumerate(quarters))
    for bit in range(bits):
        flip = 1 << bit
        for mask in sorted([mask for mask in held if mask & flip], reverse=True):
            came = permute(held.pop(mask), across(bit))
            kept = held[mask ^ flip]
            held[mask ^ flip] = added(kept, came)
    total = held[0]
    pieces = [total]
    sent = {(0, 0, piece): total}
    for mask, begin, size in layout[1:]:
        bit = [bit for bit in range(bits) if mask >> bit & 1][0]
        source = (mask ^ 1 << bit, begin, size)
        if source not in sent:
            sent[source] = added(kept[begin : begin + size], came[begin : begin + size])
        sent[mask, begin, size] = permute(sent[source], across(bit))
        pieces.append(sent[mask, begin, size])
    pieces_other = []
    for held_piece in pieces:
        pieces_other.append(permute(held_piece, swap))

    block = min(LANES, group_rows)
    count = group_rows // block
    ids = window_ids.reshape(groups, group_rows)
    wide = jax.ShapeDtypeStruct((group_rows, PART_WIDTH), F32)
    assert 2 * PART_ATT <= LANES
    near_mixed, stats = call(
        functools.partial(near_kernel, block),
        [wide, jax.ShapeDtypeStruct((group_rows, LANES), F32)],
        [place, query_seq, ids, kv_seq, kv_chip],
        scratch=[VMEM((group_rows, group_rows), F32), VMEM((count, block, group_rows), F32)],
        smem=1, flops=6 * group_rows * group_rows * PART_WIDTH, limit=24,
    )
    (attended,) = call(
        functools.partial(far_kernel, block),
        [wide],
        [place, query_seq, ids, near_mixed, stats, kv_far],
        scratch=[VMEM((count, block, group_rows), F32)],
        smem=1, flops=3 * group_rows * group_rows * PART_WIDTH, limit=24,
    )

    blocks = call(
        functools.partial(apply_kernel, first_goal, first_rows),
        [jax.ShapeDtypeStruct((tok_dev, PART_WIDTH), BF16)] * PARTS,
        [place, weights, query_seq, attended] + pieces + pieces_other,
        scratch=[
            VMEM((PART_FAST, 3, SPAN, hidden), BF16),
            VMEM((PART_FAST * 3, hidden), F32),
            VMEM((group_rows, PART_WIDTH), BF16),
        ],
        smem=1, flops=6 * group_rows * PART_WIDTH * hidden, limit=40,
    )

    parts = []
    for j in range(PARTS):
        parts.append(permute(blocks[j], lambda z, y, x, c, j=j: (z, c, x ^ j % 2, y ^ j // 2)))

    (out,) = call(
        norm_kernel,
        [jax.ShapeDtypeStruct((tok_dev, WIDTH), BF16)],
        [place] + parts + [norm_gain.reshape(1, WIDTH)],
        scratch=[VMEM((PARTS, tok_dev, PART_WIDTH), BF16)],
        smem=1, flops=6 * tok_dev * WIDTH,
    )
    return out


def solution(mesh):
    rows = P(("groups", "tok"), None)
    return jax.shard_map(
        shards,
        mesh=mesh,
        in_specs=(rows, rows, rows, rows, P("groups"), P("groups"), P(), P()),
        out_specs=rows,
        check_vma=False,
    )
```

```python
import functools
import math

import jax
import jax.numpy as jnp
from jax import lax
from jax.experimental import pallas as pl
from jax.experimental.pallas import tpu as pltpu
from jax.sharding import PartitionSpec as P


HEADS = 8
HEAD_DIM = 320
ATT_DIM = 128
WINDOW = 1024
WIDTH = 2560
ATT_HEADS = 20
LANES = 128
EPS = 1e-06

PARTS = math.gcd(HEADS, ATT_HEADS)
PART_WIDTH = WIDTH // PARTS
PART_FAST = HEADS // PARTS
PART_ATT = ATT_HEADS // PARTS
SPAN = -(-HEAD_DIM // LANES) * LANES


VMEM_BYTES = 67043328

F32 = jnp.float32
BF16 = jnp.bfloat16
VMEM = pltpu.VMEM


def iota(shape, dim):
    return lax.broadcasted_iota(jnp.int32, shape, dim)


def dot(a, b, dims=((1,), (0,))):
    return lax.dot_general(a, b, (dims, ((), ())), preferred_element_type=F32)


def column_of(row):
    n = row.shape[1]
    square = jnp.broadcast_to(row.astype(F32), (n, n))
    diagonal = iota((n, n), 0) == iota((n, n), 1)
    return jnp.sum(jnp.where(diagonal, square, 0.0), axis=1, keepdims=True)


def call(kernel, outs, ins, scratch=(), smem=0, flops=0, grid=None, in_specs=None, out_specs=None, limit=60):
    specs = [pl.BlockSpec(memory_space=pltpu.SMEM)] * smem
    specs += in_specs or [pl.BlockSpec(memory_space=VMEM)] * (len(ins) - smem)
    moved = sum(x.size * x.dtype.itemsize for x in list(ins) + list(outs))
    extra = {} if grid is None else {"grid": grid}
    return pl.pallas_call(
        kernel,
        out_shape=list(outs),
        in_specs=specs,
        out_specs=out_specs or [pl.BlockSpec(memory_space=VMEM)] * len(outs),
        scratch_shapes=list(scratch),
        compiler_params=pltpu.CompilerParams(vmem_limit_bytes=min(limit << 20, VMEM_BYTES)),
        cost_estimate=pl.CostEstimate(flops=flops, bytes_accessed=moved, transcendentals=0),
        **extra,
    )(*ins)


def window_of(head):
    begin = min(head * HEAD_DIM // LANES * LANES, PART_WIDTH - SPAN)
    return begin, head * HEAD_DIM - begin


def front_kernel(group_shift, slots, place_ref, order_ref, rate_ref, query_ref, key_ref, value_ref, *refs):
    head_refs, out_refs, choose_buf = refs[: PARTS * PART_FAST], refs[PARTS * PART_FAST : -1], refs[-1]
    n, _ = key_ref.shape
    planes, (together, cores) = len(out_refs), out_refs[0].shape[:2]
    step, part, core = pl.program_id(0), place_ref[1], place_ref[2]

    @pl.when(step == 0)
    def _():
        pos = order_ref[pl.ds(place_ref[0], 1), :]
        group = lax.shift_right_logical(pos, group_shift)
        group_col = column_of(group).astype(jnp.int32)
        earlier = (group_col == group) & (iota((n, n), 0) < iota((n, n), 1))
        rank = jnp.sum(jnp.where(earlier, 1.0, 0.0), axis=0, keepdims=True)
        away = group ^ place_ref[3] // cores * cores
        slot = away * slots + rank.astype(jnp.int32)
        choose_buf[...] = jnp.where(iota((n, n), 0) == slot, 1.0, 0.0).astype(BF16)

    choose = choose_buf[...]
    for index, ref in enumerate((key_ref, value_ref, query_ref)):
        lanes = slice(index * PART_WIDTH, (index + 1) * PART_WIDTH)
        for local in range(together):
            rows = dot(choose, ref[:, local * PART_WIDTH : (local + 1) * PART_WIDTH]).astype(BF16)
            for plane in range(planes):
                for at in range(cores):
                    first = (plane * cores + at) * slots
                    out_refs[plane][local, at, :, lanes] = rows[first : first + slots]

    lane = iota((n, SPAN), 1)
    tail = PART_WIDTH - SPAN
    for local in range(together):
        target_part = step * together + local
        rows = []
        for head in range(PART_FAST):
            begin, offset = window_of(head)
            span = slice(local * PART_WIDTH + begin, local * PART_WIDTH + begin + SPAN)
            rate = column_of(rate_ref[pl.ds(target_part * PART_FAST + head, 1), :])
            keys = key_ref[:, span].astype(F32)
            targets = value_ref[:, span].astype(F32) * rate
            turn = SPAN - HEAD_DIM
            if offset:
                keys = pltpu.roll(keys, SPAN - offset, 1)
            if offset != turn:
                targets = pltpu.roll(targets, turn - offset, 1)
            rows.append((keys.astype(BF16), targets.astype(BF16)))
        for flip in range(PART_FAST):
            keys, targets = (jnp.where(core == flip, one, two) for one, two in zip(*rows))
            middle = jnp.where(iota((n, LANES), 1) < HEAD_DIM - tail, keys[:, tail:], targets[:, : SPAN - tail])
            for index in range(PARTS):
                @pl.when((target_part ^ part) == index)
                def _():
                    ref = head_refs[index * PART_FAST + flip]
                    ref[:, :tail] = keys[:, :tail]
                    ref[:, tail:SPAN] = middle
                    ref[:, SPAN:] = targets[:, SPAN - tail :]


def arrival_choice(group_shift, slots, orders, group, n):
    sources, rows = orders.shape
    low_shift = group_shift // 2
    mine = lax.shift_right_logical(orders, group_shift) == group
    before = jnp.where(iota((rows, rows), 0) < iota((rows, rows), 1), 1.0, 0.0).astype(BF16)
    rank = dot(jnp.where(mine, 1.0, 0.0).astype(BF16), before)
    within = orders & ((1 << group_shift) - 1)
    digits = (lax.shift_right_logical(within, low_shift).astype(F32), (within & ((1 << low_shift) - 1)).astype(F32))
    team = PARTS * PART_FAST
    stages = sources // team // 2
    row = iota((sources, n), 1)
    distance = row // (n // stages) * 2 + row // slots % 2
    source = (group // PART_FAST ^ distance) * team + row // (2 * slots) % team
    spread = jnp.where(source == iota((sources, n), 0), 1.0, 0.0).astype(BF16)
    keep = iota((slots, n), 1) % slots == iota((slots, n), 0)
    column = iota((sources, slots), 1)
    pos = jnp.zeros((1, n), F32)
    for digit, weight in zip(digits, (float(1 << low_shift), 1.0)):
        table = jnp.zeros((sources, slots), F32)
        for k in range(slots):
            one = jnp.sum(jnp.where(mine & (rank == float(k)), digit, 0.0), axis=1, keepdims=True)
            table = jnp.where(column == k, one, table)
        wide = dot(table.astype(BF16), spread, ((0,), (0,)))
        pos += weight * jnp.sum(jnp.where(keep, wide, 0.0), axis=0, keepdims=True)
    return jnp.where(iota((n, n), 0) == pos.astype(jnp.int32), 1.0, 0.0).astype(BF16)


def choose_kernel(group_shift, slots, place_ref, order_ref, choose_ref):
    choose_ref[...] = arrival_choice(group_shift, slots, order_ref[...], place_ref[3], choose_ref.shape[0])


def place_kernel(choose_ref, *refs):
    in_refs, (kv_ref, q_ref) = refs[:-2], refs[-2:]
    size = in_refs[0].shape[0]
    for ref, lanes in ((kv_ref, slice(0, 2 * PART_WIDTH)), (q_ref, slice(2 * PART_WIDTH, 3 * PART_WIDTH))):
        parts = [dot(choose_ref[:, i * size : (i + 1) * size], part[:, lanes]) for i, part in enumerate(in_refs)]
        ref[...] = functools.reduce(jnp.add, parts).astype(BF16)


def grads_kernel(chunk, first_start, outs, place_ref, weight_ref, *refs):
    last = outs > 1
    weight_buf, key_buf, target_buf, delta_buf, pr_buf, sums = refs[-6:]
    out_refs, in_refs = refs[-6 - outs : -6], refs[: -6 - outs]
    kv_refs, early_ref = (in_refs[:-1], in_refs[-1]) if last else (in_refs, None)
    block = kv_refs[0].shape[0]
    n = key_buf.shape[0]
    hidden = weight_ref.shape[2]
    first = pl.multiple_of(place_ref[2] * HEAD_DIM, 16)
    spare = SPAN - HEAD_DIM
    for index in range(3):
        lanes = slice(index * hidden, (index + 1) * hidden)
        begin, blank = (0, HEAD_DIM) if index < 2 else (spare, 0)
        weight_buf[begin : begin + HEAD_DIM, lanes] = weight_ref[index, pl.ds(first, HEAD_DIM), :]
        weight_buf[blank : blank + spare, lanes] = jnp.zeros((spare, hidden), BF16)
    for index, ref in enumerate(kv_refs):
        here = pl.ds(index * block, block)
        key_buf[here, :] = ref[:, :SPAN]
        target_buf[here, :] = ref[:, PART_WIDTH - SPAN :]
    for at in range(0, n, chunk):
        here = pl.ds(at, chunk)
        both = dot(key_buf[here, :], weight_buf[:, : 2 * hidden])
        gate, upward = both[:, :hidden], both[:, hidden:]
        backward = dot(target_buf[here, :], weight_buf[:, 2 * hidden :])
        sigmoid = jax.nn.sigmoid(gate)
        active = gate * sigmoid
        pr_buf[here, :] = (active * upward).astype(BF16)
        delta_buf[here, hidden:] = (backward * active).astype(BF16)
        delta_buf[here, :hidden] = (backward * upward * sigmoid * (1.0 + gate * (1.0 - sigmoid))).astype(BF16)
    for left, right, begin, row in ((key_buf, delta_buf, 0, 0), (target_buf, pr_buf, 2 * hidden, spare)):
        lanes = slice(begin, begin + right.shape[1])
        total = dot(left[...], right[...], ((0,), (0,)))[row : row + HEAD_DIM]
        if last:
            sums[:, lanes] = (total + early_ref[:, lanes].astype(F32)).astype(BF16)
        else:
            out_refs[0][:, lanes] = total.astype(BF16)
    if last:
        for index, ref in enumerate(out_refs):
            begin = pl.multiple_of(place_ref[first_start + index], 16)
            ref[...] = sums[pl.ds(begin, ref.shape[0]), :]


FACTOR = ATT_DIM ** (-0.5) * math.log2(math.e)


def reach(before, index, count, block):
    at = pl.multiple_of(jnp.where(before, index, count - 1 - index) * block, block)
    return at, pl.multiple_of(jnp.where(before, at, 0), block), jnp.where(before, -count * block, count * block - at)


def block_ids(ids, index, count, block, turned):
    turn = count - 1 - index
    row = jnp.where(turned, ids[:, turn * block : (turn + 1) * block], ids[:, index * block : (index + 1) * block])
    return column_of(row).astype(jnp.int32)


def mask_of(own, ids, shift):
    gap = iota((own.shape[0], ids.shape[1]), 1) - iota((own.shape[0], ids.shape[1]), 0) + shift
    return jnp.where((gap < WINDOW // 2) & (gap > -(WINDOW // 2)) & (own == ids), 0.0, -1e30)


def head_lanes(head):
    return pl.ds(pl.multiple_of(head * ATT_DIM, ATT_DIM), ATT_DIM), pl.ds(pl.multiple_of(PART_WIDTH + head * ATT_DIM, ATT_DIM), ATT_DIM)


def near_kernel(block, place_ref, query_ref, ids_ref, kv_ref, chip_ref, out_ref, stat_ref, bias, chip_bias):
    n = query_ref.shape[0]
    count = n // block
    core, group = place_ref[2], place_ref[3]
    second = core == 1
    ids = ids_ref[pl.ds(group, 1), :]
    for index in range(count):
        at = index * block
        bias[at : at + block, :] = mask_of(column_of(ids[:, at : at + block]).astype(jnp.int32), ids, -at)
    for index in range(count):
        _, _, shift = reach(second, count - 1 - index, count, block)
        size = (index + 1) * block
        own = block_ids(ids, index, count, block, second)
        other = ids_ref[pl.ds(group + 1 - 2 * core, 1), :]
        other = jnp.where(second, other[:, n - size :], other[:, :size])
        chip_bias[index, :, :size] = mask_of(own, other, shift)
    stat_ref[...] = jnp.zeros_like(stat_ref)
    lane = iota((block, LANES), 1)

    @pl.loop(0, PART_ATT)
    def _(head):
        keys, values = head_lanes(head)
        for index in range(count):
            at, start, _ = reach(second, count - 1 - index, count, block)
            size = (index + 1) * block
            here, there = pl.ds(at, block), pl.ds(start, size)
            query = query_ref[here, keys]
            score = dot(query, kv_ref[:, keys], ((1,), (1,))) + bias[here, :]
            chip = dot(query, chip_ref[there, keys], ((1,), (1,))) + chip_bias[index, :, :size]
            peak = jnp.maximum(jnp.max(score, axis=1, keepdims=True), jnp.max(chip, axis=1, keepdims=True))
            score = jnp.exp2((score - peak) * FACTOR)
            chip = jnp.exp2((chip - peak) * FACTOR)
            total = jnp.sum(score, axis=1, keepdims=True) + jnp.sum(chip, axis=1, keepdims=True)
            out_ref[here, keys] = dot(score.astype(BF16), kv_ref[:, values]) + dot(chip.astype(BF16), chip_ref[there, values])
            stat = jnp.where(lane == 2 * head, peak, stat_ref[here, :])
            stat_ref[here, :] = jnp.where(lane == 2 * head + 1, total, stat)


def far_kernel(block, place_ref, query_ref, ids_ref, near_ref, stat_ref, kv_ref, out_ref, bias):
    n = query_ref.shape[0]
    count = n // block
    core, group = place_ref[2], place_ref[3]
    last = ids_ref.shape[0] - 1
    first = core == 0
    beyond = group - 1 + 2 * core
    exists = (beyond >= 0) & (beyond <= last)
    ids = ids_ref[pl.ds(group, 1), :]
    for index in range(count):
        _, _, shift = reach(first, index, count, block)
        size = n - index * block
        own = block_ids(ids, index, count, block, core == 1)
        other = ids_ref[pl.ds(jnp.clip(beyond, 0, last), 1), :]
        other = jnp.where(first, other[:, n - size :], other[:, :size])
        bias[index, :, :size] = mask_of(own, jnp.where(exists, other, -1), shift)
    lane = iota((block, LANES), 1)

    @pl.loop(0, PART_ATT)
    def _(head):
        keys, values = head_lanes(head)
        for index in range(count):
            at, start, _ = reach(first, index, count, block)
            size = n - index * block
            here, there = pl.ds(at, block), pl.ds(start, size)
            score = dot(query_ref[here, keys], kv_ref[there, keys], ((1,), (1,))) + bias[index, :, :size]
            stat = stat_ref[here, :]
            old_peak = jnp.sum(jnp.where(lane == 2 * head, stat, 0.0), axis=1, keepdims=True)
            old_total = jnp.sum(jnp.where(lane == 2 * head + 1, stat, 0.0), axis=1, keepdims=True)
            peak = jnp.maximum(jnp.max(score, axis=1, keepdims=True), old_peak)
            keep = jnp.exp2((old_peak - peak) * FACTOR)
            score = jnp.exp2((score - peak) * FACTOR)
            total = old_total * keep + jnp.sum(score, axis=1, keepdims=True)
            mixed = near_ref[here, keys] * keep + dot(score.astype(BF16), kv_ref[there, values])
            out_ref[here, keys] = mixed / total


def apply_kernel(first_goal, first_rows, place_ref, weight_ref, query_ref, attended_ref, *refs):
    hidden = weight_ref.shape[2]
    out_refs, (fresh, scales, rows_buf) = refs[-3 - PARTS : -3], refs[-3:]
    count = (len(refs) - 3 - PARTS) // 2
    mine_refs, other_refs = refs[:count], refs[count : 2 * count]
    core = place_ref[2]
    for head in range(PART_FAST):
        _, offset = window_of(head)
        for index in range(3):
            lanes = slice(index * hidden, (index + 1) * hidden)
            anchor = jnp.full((1, hidden), EPS, F32)
            length = jnp.full((1, hidden), EPS, F32)
            for step in range(count):
                piece = mine_refs[step].shape[0]
                at = pl.multiple_of(place_ref[first_rows + step], 16)
                base = weight_ref[index, pl.ds(at + head * HEAD_DIM, piece), :].astype(F32)
                grad = jnp.where(core == head, mine_refs[step][:, lanes], other_refs[step][:, lanes]).astype(F32)
                update = base + grad
                anchor += jnp.sum(base * base, axis=0, keepdims=True)
                length += jnp.sum(update * update, axis=0, keepdims=True)
                fresh[head, index, pl.ds(at + offset, piece), :] = update.astype(BF16)
            scales[head * 3 + index, :] = (jnp.sqrt(anchor) / jnp.sqrt(length))[0]
            if offset:
                fresh[head, index, :offset, :] = jnp.zeros((offset, hidden), BF16)
            if offset + HEAD_DIM < SPAN:
                fresh[head, index, offset + HEAD_DIM :, :] = jnp.zeros((SPAN - offset - HEAD_DIM, hidden), BF16)
    parts = []
    for head in range(PART_FAST):
        begin, _ = window_of(head)
        query = query_ref[:, begin : begin + SPAN]
        scale = [scales[head * 3 + index : head * 3 + index + 1, :] for index in range(3)]
        gate = dot(query, fresh[head, 0]) * scale[0]
        upward = dot(query, fresh[head, 1]) * (scale[1] * scale[2])
        product = (gate * jax.nn.sigmoid(gate) * upward).astype(BF16)
        parts.append((begin, dot(product, fresh[head, 2], ((1,), (1,)))))
    for lane in range(0, PART_WIDTH, LANES):
        inside = [value[:, lane - begin : lane - begin + LANES] for begin, value in parts if begin <= lane < begin + SPAN]
        rows_buf[:, lane : lane + LANES] = functools.reduce(jnp.add, inside, attended_ref[:, lane : lane + LANES]).astype(BF16)
    block = out_refs[0].shape[0]
    for index, ref in enumerate(out_refs):
        begin = pl.multiple_of(place_ref[first_goal + index] * block, block)
        ref[...] = rows_buf[pl.ds(begin, block), :]


def norm_kernel(place_ref, *refs):
    part_refs, gain_ref, out_ref, buf = refs[:PARTS], refs[PARTS], refs[PARTS + 1], refs[PARTS + 2]
    square = jnp.zeros((out_ref.shape[0], 1), F32)
    for index, ref in enumerate(part_refs):
        rows = ref[...]
        buf[place_ref[4 + index]] = rows
        wide = rows.astype(F32)
        square += jnp.sum(wide * wide, axis=1, keepdims=True)
    factor = lax.rsqrt(square / WIDTH + EPS)
    for part in range(PARTS):
        lanes = slice(part * PART_WIDTH, (part + 1) * PART_WIDTH)
        out_ref[:, lanes] = (buf[part].astype(F32) * factor * gain_ref[:, lanes]).astype(BF16)


def gather_layout(bits, piece, relay):
    layout = [(0, 0, piece)]
    for bit in reversed(range(bits)):
        for mask, begin, size in list(layout):
            cuts = [(begin, size)]
            if mask == 0 and bit == bits - 1 and bits > 1:
                cuts = [(0, relay), (relay, piece - relay)]
            layout += [(mask ^ 1 << bit, first, count) for first, count in cuts]
    return layout


def shards(queries, key_rows, value_rows, learn_rates, frame_order, window_ids, fast_init, norm_gain):
    tok_dev = queries.shape[0]
    hidden = fast_init.shape[0]
    sections = lax.axis_size("tok")
    plane_size = PARTS * PART_FAST
    planes = sections // plane_size
    group_rows = tok_dev * PARTS
    groups = planes * PART_FAST
    slots = tok_dev // groups
    half = WINDOW // 2
    assert PART_FAST == 2 and half == group_rows and group_rows & (group_rows - 1) == 0
    group_shift = group_rows.bit_length() - 1

    rank = lax.axis_index("tok")
    plane = rank // plane_size
    part = rank // PART_FAST % PARTS
    core = rank % PART_FAST
    row, column = part // 2, part % 2
    group = plane * PART_FAST + core

    def at(plane, row, column, core):
        return plane * plane_size + (row * 2 + column) * PART_FAST + core

    everyone = [(z, y, x, c) for z in range(planes) for y in range(2) for x in range(2) for c in range(2)]

    def permute(array, target):
        route = []
        for source in everyone:
            goal = target(*source)
            if goal is not None:
                route.append((at(*source), at(*goal)))
        return lax.ppermute(array, "tok", route)

    sources = [2 * (core ^ j // 2) + (column ^ j % 2) for j in range(PARTS)]
    bits = planes.bit_length() - 1
    piece = HEAD_DIM >> bits
    assert planes == 1 << bits and piece << bits == HEAD_DIM and piece % 16 == 0

    def owned(plane):
        return sum((plane >> bit & 1) * (HEAD_DIM >> bit + 1) for bit in range(bits))

    relay = -(-piece // 32) * 16
    layout = gather_layout(bits, piece, relay)
    starts = [owned(plane ^ mask) for mask in range(planes)]
    rows_from = [starts[mask] + begin for mask, begin, _ in layout]
    goals = [2 * (column ^ j % 2) + (row ^ j // 2) for j in range(PARTS)]
    first_start = 4 + PARTS
    first_goal = first_start + planes
    first_rows = first_goal + PARTS
    place = jnp.stack([rank, part, core, group] + sources + starts + goals + rows_from).astype(jnp.int32)

    def weight_part():
        own = lax.dynamic_slice_in_dim(fast_init, part * PART_WIDTH, PART_WIDTH, 2)
        return jnp.transpose(own, (1, 2, 0))

    weights = weight_part()

    full = lambda a: pl.BlockSpec(a.shape, lambda h: (0,) * a.ndim)
    steps = 2
    together = PARTS // steps
    orders = frame_order.reshape(sections, tok_dev)
    rates = learn_rates.T
    cut = pl.BlockSpec((tok_dev, WIDTH // steps), lambda h: (0, h))
    head_shape = jax.ShapeDtypeStruct((tok_dev, 2 * HEAD_DIM), BF16)
    outs = call(
        functools.partial(front_kernel, group_shift, slots),
        [head_shape] * plane_size + [jax.ShapeDtypeStruct((PARTS, PART_FAST, slots, 3 * PART_WIDTH), BF16)] * planes,
        [place, orders, rates, queries, key_rows, value_rows],
        in_specs=[full(orders), full(rates), cut, cut, cut],
        out_specs=[full(head_shape)] * plane_size
        + [pl.BlockSpec((together, PART_FAST, slots, 3 * PART_WIDTH), lambda h: (h, 0, 0, 0))] * planes,
        grid=(steps,),
        scratch=[VMEM((tok_dev, tok_dev), BF16)],
        smem=1, flops=2 * tok_dev * tok_dev * 3 * WIDTH,
    )
    heads_out, packed = outs[:plane_size], [rows.reshape(plane_size, slots, 3 * PART_WIDTH) for rows in outs[plane_size:]]
    heads_in = [heads_out[0]]
    send_order = [2, 4, 3, 5, 6, 7, 1]
    for j in range(1, plane_size):
        heads_in.append(permute(heads_out[j], lambda z, y, x, c, j=j: (z, y ^ j >> 2, x ^ j >> 1 & 1, c ^ j & 1)))

    teams = [[z * plane_size + i for i in range(plane_size)] for z in range(planes)]
    arrived = []
    for stage in range(planes // 2):
        both = []
        for distance in (2 * stage, 2 * stage + 1):
            rows = packed[distance]
            if distance:
                rows = permute(rows, lambda z, y, x, c, m=distance: (z ^ m, y, x, c))
            both.append(rows)
        both = jnp.concatenate(both, axis=1)
        both = lax.all_to_all(both, "tok", split_axis=0, concat_axis=0, axis_index_groups=teams, tiled=True)
        arrived.append(both.reshape(plane_size * 2 * slots, 3 * PART_WIDTH))

    (choose,) = call(
        functools.partial(choose_kernel, group_shift, slots),
        [jax.ShapeDtypeStruct((group_rows, group_rows), BF16)],
        [place, orders], smem=1, flops=2 * group_rows * group_rows,
    )
    kv_seq, query_seq = call(
        place_kernel,
        [jax.ShapeDtypeStruct((group_rows, width), BF16) for width in (2 * PART_WIDTH, PART_WIDTH)],
        [choose] + arrived, flops=2 * group_rows * group_rows * 3 * PART_WIDTH,
    )

    swap = lambda z, y, x, c: (z, y, x, 1 - c)

    def beyond(z, y, x, c):
        goal = z + 2 * c - 1
        return (goal, y, x, 1 - c) if 0 <= goal < planes else None

    kv_chip = permute(kv_seq, swap)
    kv_far = permute(kv_seq, beyond)

    near = plane_size // 2
    tokens = near * tok_dev
    by_arrival = [heads_in[0]] + [heads_in[j] for j in send_order]
    early_heads, late_heads = by_arrival[:near], by_arrival[near:]
    grad_scratch = [VMEM((SPAN, 3 * hidden), BF16)] + [VMEM((tokens, SPAN), BF16)] * 2
    grad_scratch += [VMEM((tokens, 2 * hidden), BF16), VMEM((tokens, hidden), BF16), VMEM((HEAD_DIM, 3 * hidden), BF16)]
    grad_flops = 12 * tokens * HEAD_DIM * hidden
    (early,) = call(
        functools.partial(grads_kernel, tokens, first_start, 1),
        [jax.ShapeDtypeStruct((HEAD_DIM, 3 * hidden), BF16)], [place, weights] + early_heads,
        scratch=grad_scratch, smem=1, flops=grad_flops,
    )
    quarters = call(
        functools.partial(grads_kernel, tokens, first_start, planes),
        [jax.ShapeDtypeStruct((piece, 3 * hidden), BF16)] * planes,
        [place, weights] + late_heads + [early],
        scratch=grad_scratch, smem=1, flops=grad_flops,
    )

    def across(bit):
        return lambda z, y, x, c: (z ^ 1 << bit, y, x, c)

    def added(first, second):
        return (first.astype(F32) + second.astype(F32)).astype(BF16)

    held = dict(enumerate(quarters))
    for bit in range(bits):
        flip = 1 << bit
        for mask in sorted([mask for mask in held if mask & flip], reverse=True):
            came = permute(held.pop(mask), across(bit))
            kept = held[mask ^ flip]
            held[mask ^ flip] = added(kept, came)
    total = held[0]
    pieces = [total]
    sent = {(0, 0, piece): total}
    for mask, begin, size in layout[1:]:
        bit = [bit for bit in range(bits) if mask >> bit & 1][0]
        source = (mask ^ 1 << bit, begin, size)
        if source not in sent:
            sent[source] = added(kept[begin : begin + size], came[begin : begin + size])
        sent[mask, begin, size] = permute(sent[source], across(bit))
        pieces.append(sent[mask, begin, size])
    pieces_other = []
    for held_piece in pieces:
        pieces_other.append(permute(held_piece, swap))

    block = min(LANES, group_rows)
    count = group_rows // block
    ids = window_ids.reshape(groups, group_rows)
    wide = jax.ShapeDtypeStruct((group_rows, PART_WIDTH), F32)
    assert 2 * PART_ATT <= LANES
    near_mixed, stats = call(
        functools.partial(near_kernel, block),
        [wide, jax.ShapeDtypeStruct((group_rows, LANES), F32)],
        [place, query_seq, ids, kv_seq, kv_chip],
        scratch=[VMEM((group_rows, group_rows), F32), VMEM((count, block, group_rows), F32)],
        smem=1, flops=6 * group_rows * group_rows * PART_WIDTH, limit=24,
    )
    (attended,) = call(
        functools.partial(far_kernel, block),
        [wide],
        [place, query_seq, ids, near_mixed, stats, kv_far],
        scratch=[VMEM((count, block, group_rows), F32)],
        smem=1, flops=3 * group_rows * group_rows * PART_WIDTH, limit=24,
    )

    blocks = call(
        functools.partial(apply_kernel, first_goal, first_rows),
        [jax.ShapeDtypeStruct((tok_dev, PART_WIDTH), BF16)] * PARTS,
        [place, weights, query_seq, attended] + pieces + pieces_other,
        scratch=[
            VMEM((PART_FAST, 3, SPAN, hidden), BF16),
            VMEM((PART_FAST * 3, hidden), F32),
            VMEM((group_rows, PART_WIDTH), BF16),
        ],
        smem=1, flops=6 * group_rows * PART_WIDTH * hidden, limit=40,
    )

    parts = []
    for j in range(PARTS):
        parts.append(permute(blocks[j], lambda z, y, x, c, j=j: (z, c, x ^ j % 2, y ^ j // 2)))

    (out,) = call(
        norm_kernel,
        [jax.ShapeDtypeStruct((tok_dev, WIDTH), BF16)],
        [place] + parts + [norm_gain.reshape(1, WIDTH)],
        scratch=[VMEM((PARTS, tok_dev, PART_WIDTH), BF16)],
        smem=1, flops=6 * tok_dev * WIDTH,
    )
    return out


def solution(mesh):
    rows = P(("groups", "tok"), None)
    return jax.shard_map(
        shards,
        mesh=mesh,
        in_specs=(rows, rows, rows, rows, P("groups"), P("groups"), P(), P()),
        out_specs=rows,
        check_vma=False,
    )
```

```python
import functools
import math

import jax
import jax.numpy as jnp
from jax import lax
from jax.experimental import pallas as pl
from jax.experimental.pallas import tpu as pltpu
from jax.sharding import PartitionSpec as P


HEADS = 8
HEAD_DIM = 320
ATT_DIM = 128
WINDOW = 1024
WIDTH = 2560
ATT_HEADS = 20
LANES = 128
EPS = 1e-06

PARTS = math.gcd(HEADS, ATT_HEADS)
PART_WIDTH = WIDTH // PARTS
PART_FAST = HEADS // PARTS
PART_ATT = ATT_HEADS // PARTS
SPAN = -(-HEAD_DIM // LANES) * LANES


VMEM_BYTES = 67043328

F32 = jnp.float32
BF16 = jnp.bfloat16
VMEM = pltpu.VMEM


def iota(shape, dim):
    return lax.broadcasted_iota(jnp.int32, shape, dim)


def dot(a, b, dims=((1,), (0,))):
    return lax.dot_general(a, b, (dims, ((), ())), preferred_element_type=F32)


def column_of(row):
    n = row.shape[1]
    square = jnp.broadcast_to(row.astype(F32), (n, n))
    diagonal = iota((n, n), 0) == iota((n, n), 1)
    return jnp.sum(jnp.where(diagonal, square, 0.0), axis=1, keepdims=True)


def call(kernel, outs, ins, scratch=(), smem=0, flops=0, grid=None, in_specs=None, out_specs=None, limit=60):
    specs = [pl.BlockSpec(memory_space=pltpu.SMEM)] * smem
    specs += in_specs or [pl.BlockSpec(memory_space=VMEM)] * (len(ins) - smem)
    moved = sum(x.size * x.dtype.itemsize for x in list(ins) + list(outs))
    extra = {} if grid is None else {"grid": grid}
    return pl.pallas_call(
        kernel,
        out_shape=list(outs),
        in_specs=specs,
        out_specs=out_specs or [pl.BlockSpec(memory_space=VMEM)] * len(outs),
        scratch_shapes=list(scratch),
        compiler_params=pltpu.CompilerParams(vmem_limit_bytes=min(limit << 20, VMEM_BYTES)),
        cost_estimate=pl.CostEstimate(flops=flops, bytes_accessed=moved, transcendentals=0),
        **extra,
    )(*ins)


def window_of(head):
    begin = min(head * HEAD_DIM // LANES * LANES, PART_WIDTH - SPAN)
    return begin, head * HEAD_DIM - begin


def front_kernel(group_shift, slots, place_ref, order_ref, rate_ref, query_ref, key_ref, value_ref, *refs):
    head_refs, out_refs, choose_buf = refs[: PARTS * PART_FAST], refs[PARTS * PART_FAST : -1], refs[-1]
    n, _ = key_ref.shape
    planes, (together, cores) = len(out_refs), out_refs[0].shape[:2]
    step, part, core = pl.program_id(0), place_ref[1], place_ref[2]

    @pl.when(step == 0)
    def _():
        pos = order_ref[pl.ds(place_ref[0], 1), :]
        group = lax.shift_right_logical(pos, group_shift)
        group_col = column_of(group).astype(jnp.int32)
        earlier = (group_col == group) & (iota((n, n), 0) < iota((n, n), 1))
        rank = jnp.sum(jnp.where(earlier, 1.0, 0.0), axis=0, keepdims=True)
        away = group ^ place_ref[3] // cores * cores
        slot = away * slots + rank.astype(jnp.int32)
        choose_buf[...] = jnp.where(iota((n, n), 0) == slot, 1.0, 0.0).astype(BF16)

    choose = choose_buf[...]
    for index, ref in enumerate((key_ref, value_ref, query_ref)):
        lanes = slice(index * PART_WIDTH, (index + 1) * PART_WIDTH)
        for local in range(together):
            rows = dot(choose, ref[:, local * PART_WIDTH : (local + 1) * PART_WIDTH]).astype(BF16)
            for plane in range(planes):
                for at in range(cores):
                    first = (plane * cores + at) * slots
                    out_refs[plane][local, at, :, lanes] = rows[first : first + slots]

    lane = iota((n, SPAN), 1)
    tail = PART_WIDTH - SPAN
    for local in range(together):
        target_part = step * together + local
        rows = []
        for head in range(PART_FAST):
            begin, offset = window_of(head)
            span = slice(local * PART_WIDTH + begin, local * PART_WIDTH + begin + SPAN)
            rate = column_of(rate_ref[pl.ds(target_part * PART_FAST + head, 1), :])
            keys = key_ref[:, span].astype(F32)
            targets = value_ref[:, span].astype(F32) * rate
            turn = SPAN - HEAD_DIM
            if offset:
                keys = pltpu.roll(keys, SPAN - offset, 1)
            if offset != turn:
                targets = pltpu.roll(targets, turn - offset, 1)
            rows.append((keys.astype(BF16), targets.astype(BF16)))
        for flip in range(PART_FAST):
            keys, targets = (jnp.where(core == flip, one, two) for one, two in zip(*rows))
            middle = jnp.where(iota((n, LANES), 1) < HEAD_DIM - tail, keys[:, tail:], targets[:, : SPAN - tail])
            for index in range(PARTS):
                @pl.when((target_part ^ part) == index)
                def _():
                    ref = head_refs[index * PART_FAST + flip]
                    ref[:, :tail] = keys[:, :tail]
                    ref[:, tail:SPAN] = middle
                    ref[:, SPAN:] = targets[:, SPAN - tail :]


def arrival_choice(group_shift, slots, orders, group, n):
    sources, rows = orders.shape
    low_shift = group_shift // 2
    mine = lax.shift_right_logical(orders, group_shift) == group
    before = jnp.where(iota((rows, rows), 0) < iota((rows, rows), 1), 1.0, 0.0).astype(BF16)
    rank = dot(jnp.where(mine, 1.0, 0.0).astype(BF16), before)
    within = orders & ((1 << group_shift) - 1)
    digits = (lax.shift_right_logical(within, low_shift).astype(F32), (within & ((1 << low_shift) - 1)).astype(F32))
    team = PARTS * PART_FAST
    stages = sources // team // 2
    row = iota((sources, n), 1)
    distance = row // (n // stages) * 2 + row // slots % 2
    source = (group // PART_FAST ^ distance) * team + row // (2 * slots) % team
    spread = jnp.where(source == iota((sources, n), 0), 1.0, 0.0).astype(BF16)
    keep = iota((slots, n), 1) % slots == iota((slots, n), 0)
    column = iota((sources, slots), 1)
    pos = jnp.zeros((1, n), F32)
    for digit, weight in zip(digits, (float(1 << low_shift), 1.0)):
        table = jnp.zeros((sources, slots), F32)
        for k in range(slots):
            one = jnp.sum(jnp.where(mine & (rank == float(k)), digit, 0.0), axis=1, keepdims=True)
            table = jnp.where(column == k, one, table)
        wide = dot(table.astype(BF16), spread, ((0,), (0,)))
        pos += weight * jnp.sum(jnp.where(keep, wide, 0.0), axis=0, keepdims=True)
    return jnp.where(iota((n, n), 0) == pos.astype(jnp.int32), 1.0, 0.0).astype(BF16)


def choose_kernel(group_shift, slots, place_ref, order_ref, choose_ref):
    choose_ref[...] = arrival_choice(group_shift, slots, order_ref[...], place_ref[3], choose_ref.shape[0])


def place_kernel(choose_ref, *refs):
    in_refs, (kv_ref, q_ref) = refs[:-2], refs[-2:]
    size = in_refs[0].shape[0]
    for ref, lanes in ((kv_ref, slice(0, 2 * PART_WIDTH)), (q_ref, slice(2 * PART_WIDTH, 3 * PART_WIDTH))):
        parts = [dot(choose_ref[:, i * size : (i + 1) * size], part[:, lanes]) for i, part in enumerate(in_refs)]
        ref[...] = functools.reduce(jnp.add, parts).astype(BF16)


def grads_kernel(chunk, first_start, outs, place_ref, weight_ref, *refs):
    last = outs > 1
    weight_buf, key_buf, target_buf, delta_buf, pr_buf, sums = refs[-6:]
    out_refs, in_refs = refs[-6 - outs : -6], refs[: -6 - outs]
    kv_refs, early_ref = (in_refs[:-1], in_refs[-1]) if last else (in_refs, None)
    block = kv_refs[0].shape[0]
    n = key_buf.shape[0]
    hidden = weight_ref.shape[2]
    first = pl.multiple_of(place_ref[2] * HEAD_DIM, 16)
    spare = SPAN - HEAD_DIM
    for index in range(3):
        lanes = slice(index * hidden, (index + 1) * hidden)
        begin, blank = (0, HEAD_DIM) if index < 2 else (spare, 0)
        weight_buf[begin : begin + HEAD_DIM, lanes] = weight_ref[index, pl.ds(first, HEAD_DIM), :]
        weight_buf[blank : blank + spare, lanes] = jnp.zeros((spare, hidden), BF16)
    for index, ref in enumerate(kv_refs):
        here = pl.ds(index * block, block)
        key_buf[here, :] = ref[:, :SPAN]
        target_buf[here, :] = ref[:, PART_WIDTH - SPAN :]
    for at in range(0, n, chunk):
        here = pl.ds(at, chunk)
        both = dot(key_buf[here, :], weight_buf[:, : 2 * hidden])
        gate, upward = both[:, :hidden], both[:, hidden:]
        backward = dot(target_buf[here, :], weight_buf[:, 2 * hidden :])
        sigmoid = jax.nn.sigmoid(gate)
        active = gate * sigmoid
        pr_buf[here, :] = (active * upward).astype(BF16)
        delta_buf[here, hidden:] = (backward * active).astype(BF16)
        delta_buf[here, :hidden] = (backward * upward * sigmoid * (1.0 + gate * (1.0 - sigmoid))).astype(BF16)
    for left, right, begin, row in ((key_buf, delta_buf, 0, 0), (target_buf, pr_buf, 2 * hidden, spare)):
        lanes = slice(begin, begin + right.shape[1])
        total = dot(left[...], right[...], ((0,), (0,)))[row : row + HEAD_DIM]
        if last:
            sums[:, lanes] = (total + early_ref[:, lanes].astype(F32)).astype(BF16)
        else:
            out_refs[0][:, lanes] = total.astype(BF16)
    if last:
        for index, ref in enumerate(out_refs):
            begin = pl.multiple_of(place_ref[first_start + index], 16)
            ref[...] = sums[pl.ds(begin, ref.shape[0]), :]


FACTOR = ATT_DIM ** (-0.5) * math.log2(math.e)


def reach(before, index, count, block):
    at = pl.multiple_of(jnp.where(before, index, count - 1 - index) * block, block)
    return at, pl.multiple_of(jnp.where(before, at, 0), block), jnp.where(before, -count * block, count * block - at)


def block_ids(ids, index, count, block, turned):
    turn = count - 1 - index
    row = jnp.where(turned, ids[:, turn * block : (turn + 1) * block], ids[:, index * block : (index + 1) * block])
    return column_of(row).astype(jnp.int32)


def mask_of(own, ids, shift):
    gap = iota((own.shape[0], ids.shape[1]), 1) - iota((own.shape[0], ids.shape[1]), 0) + shift
    return jnp.where((gap < WINDOW // 2) & (gap > -(WINDOW // 2)) & (own == ids), 0.0, -1e30)


def head_lanes(head):
    return pl.ds(pl.multiple_of(head * ATT_DIM, ATT_DIM), ATT_DIM), pl.ds(pl.multiple_of(PART_WIDTH + head * ATT_DIM, ATT_DIM), ATT_DIM)


def near_kernel(block, place_ref, query_ref, ids_ref, kv_ref, chip_ref, out_ref, stat_ref, bias, chip_bias):
    n = query_ref.shape[0]
    count = n // block
    core, group = place_ref[2], place_ref[3]
    second = core == 1
    ids = ids_ref[pl.ds(group, 1), :]
    for index in range(count):
        at = index * block
        bias[at : at + block, :] = mask_of(column_of(ids[:, at : at + block]).astype(jnp.int32), ids, -at)
    for index in range(count):
        _, _, shift = reach(second, count - 1 - index, count, block)
        size = (index + 1) * block
        own = block_ids(ids, index, count, block, second)
        other = ids_ref[pl.ds(group + 1 - 2 * core, 1), :]
        other = jnp.where(second, other[:, n - size :], other[:, :size])
        chip_bias[index, :, :size] = mask_of(own, other, shift)
    stat_ref[...] = jnp.zeros_like(stat_ref)
    lane = iota((block, LANES), 1)

    @pl.loop(0, PART_ATT)
    def _(head):
        keys, values = head_lanes(head)
        for index in range(count):
            at, start, _ = reach(second, count - 1 - index, count, block)
            size = (index + 1) * block
            here, there = pl.ds(at, block), pl.ds(start, size)
            query = query_ref[here, keys]
            score = dot(query, kv_ref[:, keys], ((1,), (1,))) + bias[here, :]
            chip = dot(query, chip_ref[there, keys], ((1,), (1,))) + chip_bias[index, :, :size]
            peak = jnp.maximum(jnp.max(score, axis=1, keepdims=True), jnp.max(chip, axis=1, keepdims=True))
            score = jnp.exp2((score - peak) * FACTOR)
            chip = jnp.exp2((chip - peak) * FACTOR)
            total = jnp.sum(score, axis=1, keepdims=True) + jnp.sum(chip, axis=1, keepdims=True)
            out_ref[here, keys] = dot(score.astype(BF16), kv_ref[:, values]) + dot(chip.astype(BF16), chip_ref[there, values])
            stat = jnp.where(lane == 2 * head, peak, stat_ref[here, :])
            stat_ref[here, :] = jnp.where(lane == 2 * head + 1, total, stat)


def far_kernel(block, first_goal, place_ref, query_ref, ids_ref, near_ref, stat_ref, fast_ref, kv_ref, *refs):
    out_refs, (bias, rows_buf) = refs[:-2], refs[-2:]
    n = query_ref.shape[0]
    count = n // block
    core, group = place_ref[2], place_ref[3]
    last = ids_ref.shape[0] - 1
    first = core == 0
    beyond = group - 1 + 2 * core
    exists = (beyond >= 0) & (beyond <= last)
    ids = ids_ref[pl.ds(group, 1), :]
    for index in range(count):
        _, _, shift = reach(first, index, count, block)
        size = n - index * block
        own = block_ids(ids, index, count, block, core == 1)
        other = ids_ref[pl.ds(jnp.clip(beyond, 0, last), 1), :]
        other = jnp.where(first, other[:, n - size :], other[:, :size])
        bias[index, :, :size] = mask_of(own, jnp.where(exists, other, -1), shift)
    lane = iota((block, LANES), 1)

    @pl.loop(0, PART_ATT)
    def _(head):
        keys, values = head_lanes(head)
        for index in range(count):
            at, start, _ = reach(first, index, count, block)
            size = n - index * block
            here, there = pl.ds(at, block), pl.ds(start, size)
            score = dot(query_ref[here, keys], kv_ref[there, keys], ((1,), (1,))) + bias[index, :, :size]
            stat = stat_ref[here, :]
            old_peak = jnp.sum(jnp.where(lane == 2 * head, stat, 0.0), axis=1, keepdims=True)
            old_total = jnp.sum(jnp.where(lane == 2 * head + 1, stat, 0.0), axis=1, keepdims=True)
            peak = jnp.maximum(jnp.max(score, axis=1, keepdims=True), old_peak)
            keep = jnp.exp2((old_peak - peak) * FACTOR)
            score = jnp.exp2((score - peak) * FACTOR)
            total = old_total * keep + jnp.sum(score, axis=1, keepdims=True)
            mixed = near_ref[here, keys] * keep + dot(score.astype(BF16), kv_ref[there, values])
            rows_buf[here, keys] = (mixed / total + fast_ref[here, keys]).astype(BF16)

    rows = out_refs[0].shape[0]
    for index, ref in enumerate(out_refs):
        begin = pl.multiple_of(place_ref[first_goal + index] * rows, rows)
        ref[...] = rows_buf[pl.ds(begin, rows), :]


def apply_kernel(first_rows, place_ref, weight_ref, query_ref, *refs):
    hidden = weight_ref.shape[2]
    out_ref, fresh, scales = refs[-3:]
    count = (len(refs) - 3) // 2
    mine_refs, other_refs = refs[:count], refs[count : 2 * count]
    core = place_ref[2]
    for head in range(PART_FAST):
        _, offset = window_of(head)
        for index in range(3):
            lanes = slice(index * hidden, (index + 1) * hidden)
            anchor = jnp.full((1, hidden), EPS, F32)
            length = jnp.full((1, hidden), EPS, F32)
            for step in range(count):
                piece = mine_refs[step].shape[0]
                at = pl.multiple_of(place_ref[first_rows + step], 16)
                base = weight_ref[index, pl.ds(at + head * HEAD_DIM, piece), :].astype(F32)
                grad = jnp.where(core == head, mine_refs[step][:, lanes], other_refs[step][:, lanes]).astype(F32)
                update = base + grad
                anchor += jnp.sum(base * base, axis=0, keepdims=True)
                length += jnp.sum(update * update, axis=0, keepdims=True)
                fresh[head, index, pl.ds(at + offset, piece), :] = update.astype(BF16)
            scales[head * 3 + index, :] = (jnp.sqrt(anchor) / jnp.sqrt(length))[0]
            if offset:
                fresh[head, index, :offset, :] = jnp.zeros((offset, hidden), BF16)
            if offset + HEAD_DIM < SPAN:
                fresh[head, index, offset + HEAD_DIM :, :] = jnp.zeros((SPAN - offset - HEAD_DIM, hidden), BF16)
    parts = []
    for head in range(PART_FAST):
        begin, _ = window_of(head)
        query = query_ref[:, begin : begin + SPAN]
        scale = [scales[head * 3 + index : head * 3 + index + 1, :] for index in range(3)]
        gate = dot(query, fresh[head, 0]) * scale[0]
        upward = dot(query, fresh[head, 1]) * (scale[1] * scale[2])
        product = (gate * jax.nn.sigmoid(gate) * upward).astype(BF16)
        parts.append((begin, dot(product, fresh[head, 2], ((1,), (1,)))))
    for lane in range(0, PART_WIDTH, LANES):
        inside = [value[:, lane - begin : lane - begin + LANES] for begin, value in parts if begin <= lane < begin + SPAN]
        out_ref[:, lane : lane + LANES] = functools.reduce(jnp.add, inside)


def norm_kernel(place_ref, *refs):
    part_refs, gain_ref, out_ref, buf = refs[:PARTS], refs[PARTS], refs[PARTS + 1], refs[PARTS + 2]
    square = jnp.zeros((out_ref.shape[0], 1), F32)
    for index, ref in enumerate(part_refs):
        rows = ref[...]
        buf[place_ref[4 + index]] = rows
        wide = rows.astype(F32)
        square += jnp.sum(wide * wide, axis=1, keepdims=True)
    factor = lax.rsqrt(square / WIDTH + EPS)
    for part in range(PARTS):
        lanes = slice(part * PART_WIDTH, (part + 1) * PART_WIDTH)
        out_ref[:, lanes] = (buf[part].astype(F32) * factor * gain_ref[:, lanes]).astype(BF16)


def gather_layout(bits, piece, relay):
    layout = [(0, 0, piece)]
    for bit in reversed(range(bits)):
        for mask, begin, size in list(layout):
            cuts = [(begin, size)]
            if mask == 0 and bit == bits - 1 and bits > 1:
                cuts = [(0, relay), (relay, piece - relay)]
            layout += [(mask ^ 1 << bit, first, count) for first, count in cuts]
    return layout


def shards(queries, key_rows, value_rows, learn_rates, frame_order, window_ids, fast_init, norm_gain):
    tok_dev = queries.shape[0]
    hidden = fast_init.shape[0]
    sections = lax.axis_size("tok")
    plane_size = PARTS * PART_FAST
    planes = sections // plane_size
    group_rows = tok_dev * PARTS
    groups = planes * PART_FAST
    slots = tok_dev // groups
    half = WINDOW // 2
    assert PART_FAST == 2 and half == group_rows and group_rows & (group_rows - 1) == 0
    group_shift = group_rows.bit_length() - 1

    rank = lax.axis_index("tok")
    plane = rank // plane_size
    part = rank // PART_FAST % PARTS
    core = rank % PART_FAST
    row, column = part // 2, part % 2
    group = plane * PART_FAST + core

    def at(plane, row, column, core):
        return plane * plane_size + (row * 2 + column) * PART_FAST + core

    everyone = [(z, y, x, c) for z in range(planes) for y in range(2) for x in range(2) for c in range(2)]

    def permute(array, target):
        route = []
        for source in everyone:
            goal = target(*source)
            if goal is not None:
                route.append((at(*source), at(*goal)))
        return lax.ppermute(array, "tok", route)

    sources = [2 * (core ^ j // 2) + (column ^ j % 2) for j in range(PARTS)]
    bits = planes.bit_length() - 1
    piece = HEAD_DIM >> bits
    assert planes == 1 << bits and piece << bits == HEAD_DIM and piece % 16 == 0

    def owned(plane):
        return sum((plane >> bit & 1) * (HEAD_DIM >> bit + 1) for bit in range(bits))

    relay = -(-piece // 32) * 16
    layout = gather_layout(bits, piece, relay)
    starts = [owned(plane ^ mask) for mask in range(planes)]
    rows_from = [starts[mask] + begin for mask, begin, _ in layout]
    goals = [2 * (column ^ j % 2) + (row ^ j // 2) for j in range(PARTS)]
    first_start = 4 + PARTS
    first_goal = first_start + planes
    first_rows = first_goal + PARTS
    place = jnp.stack([rank, part, core, group] + sources + starts + goals + rows_from).astype(jnp.int32)

    def weight_part():
        own = lax.dynamic_slice_in_dim(fast_init, part * PART_WIDTH, PART_WIDTH, 2)
        return jnp.transpose(own, (1, 2, 0))

    weights = weight_part()

    full = lambda a: pl.BlockSpec(a.shape, lambda h: (0,) * a.ndim)
    steps = 2
    together = PARTS // steps
    orders = frame_order.reshape(sections, tok_dev)
    rates = learn_rates.T
    cut = pl.BlockSpec((tok_dev, WIDTH // steps), lambda h: (0, h))
    head_shape = jax.ShapeDtypeStruct((tok_dev, 2 * HEAD_DIM), BF16)
    outs = call(
        functools.partial(front_kernel, group_shift, slots),
        [head_shape] * plane_size + [jax.ShapeDtypeStruct((PARTS, PART_FAST, slots, 3 * PART_WIDTH), BF16)] * planes,
        [place, orders, rates, queries, key_rows, value_rows],
        in_specs=[full(orders), full(rates), cut, cut, cut],
        out_specs=[full(head_shape)] * plane_size
        + [pl.BlockSpec((together, PART_FAST, slots, 3 * PART_WIDTH), lambda h: (h, 0, 0, 0))] * planes,
        grid=(steps,),
        scratch=[VMEM((tok_dev, tok_dev), BF16)],
        smem=1, flops=2 * tok_dev * tok_dev * 3 * WIDTH,
    )
    heads_out, packed = outs[:plane_size], [rows.reshape(plane_size, slots, 3 * PART_WIDTH) for rows in outs[plane_size:]]
    heads_in = [heads_out[0]]
    send_order = [2, 4, 3, 5, 6, 7, 1]
    for j in range(1, plane_size):
        heads_in.append(permute(heads_out[j], lambda z, y, x, c, j=j: (z, y ^ j >> 2, x ^ j >> 1 & 1, c ^ j & 1)))

    teams = [[z * plane_size + i for i in range(plane_size)] for z in range(planes)]
    arrived = []
    for stage in range(planes // 2):
        both = []
        for distance in (2 * stage, 2 * stage + 1):
            rows = packed[distance]
            if distance:
                rows = permute(rows, lambda z, y, x, c, m=distance: (z ^ m, y, x, c))
            both.append(rows)
        both = jnp.concatenate(both, axis=1)
        both = lax.all_to_all(both, "tok", split_axis=0, concat_axis=0, axis_index_groups=teams, tiled=True)
        arrived.append(both.reshape(plane_size * 2 * slots, 3 * PART_WIDTH))

    (choose,) = call(
        functools.partial(choose_kernel, group_shift, slots),
        [jax.ShapeDtypeStruct((group_rows, group_rows), BF16)],
        [place, orders], smem=1, flops=2 * group_rows * group_rows,
    )
    kv_seq, query_seq = call(
        place_kernel,
        [jax.ShapeDtypeStruct((group_rows, width), BF16) for width in (2 * PART_WIDTH, PART_WIDTH)],
        [choose] + arrived, flops=2 * group_rows * group_rows * 3 * PART_WIDTH,
    )

    swap = lambda z, y, x, c: (z, y, x, 1 - c)

    def beyond(z, y, x, c):
        goal = z + 2 * c - 1
        return (goal, y, x, 1 - c) if 0 <= goal < planes else None

    kv_chip = permute(kv_seq, swap)
    kv_far = permute(kv_seq, beyond)

    near = plane_size // 2
    tokens = near * tok_dev
    by_arrival = [heads_in[0]] + [heads_in[j] for j in send_order]
    early_heads, late_heads = by_arrival[:near], by_arrival[near:]
    grad_scratch = [VMEM((SPAN, 3 * hidden), BF16)] + [VMEM((tokens, SPAN), BF16)] * 2
    grad_scratch += [VMEM((tokens, 2 * hidden), BF16), VMEM((tokens, hidden), BF16), VMEM((HEAD_DIM, 3 * hidden), BF16)]
    grad_flops = 12 * tokens * HEAD_DIM * hidden
    (early,) = call(
        functools.partial(grads_kernel, tokens, first_start, 1),
        [jax.ShapeDtypeStruct((HEAD_DIM, 3 * hidden), BF16)], [place, weights] + early_heads,
        scratch=grad_scratch, smem=1, flops=grad_flops,
    )
    quarters = call(
        functools.partial(grads_kernel, tokens, first_start, planes),
        [jax.ShapeDtypeStruct((piece, 3 * hidden), BF16)] * planes,
        [place, weights] + late_heads + [early],
        scratch=grad_scratch, smem=1, flops=grad_flops,
    )

    def across(bit):
        return lambda z, y, x, c: (z ^ 1 << bit, y, x, c)

    def added(first, second):
        return (first.astype(F32) + second.astype(F32)).astype(BF16)

    held = dict(enumerate(quarters))
    for bit in range(bits):
        flip = 1 << bit
        for mask in sorted([mask for mask in held if mask & flip], reverse=True):
            came = permute(held.pop(mask), across(bit))
            kept = held[mask ^ flip]
            held[mask ^ flip] = added(kept, came)
    total = held[0]
    pieces = [total]
    sent = {(0, 0, piece): total}
    for mask, begin, size in layout[1:]:
        bit = [bit for bit in range(bits) if mask >> bit & 1][0]
        source = (mask ^ 1 << bit, begin, size)
        if source not in sent:
            sent[source] = added(kept[begin : begin + size], came[begin : begin + size])
        sent[mask, begin, size] = permute(sent[source], across(bit))
        pieces.append(sent[mask, begin, size])
    pieces_other = []
    for held_piece in pieces:
        pieces_other.append(permute(held_piece, swap))

    block = min(LANES, group_rows)
    count = group_rows // block
    ids = window_ids.reshape(groups, group_rows)
    wide = jax.ShapeDtypeStruct((group_rows, PART_WIDTH), F32)
    assert 2 * PART_ATT <= LANES
    near_mixed, stats = call(
        functools.partial(near_kernel, block),
        [wide, jax.ShapeDtypeStruct((group_rows, LANES), F32)],
        [place, query_seq, ids, kv_seq, kv_chip],
        scratch=[VMEM((group_rows, group_rows), F32), VMEM((count, block, group_rows), F32)],
        smem=1, flops=6 * group_rows * group_rows * PART_WIDTH, limit=24,
    )
    (fast_out,) = call(
        functools.partial(apply_kernel, first_rows),
        [wide],
        [place, weights, query_seq] + pieces + pieces_other,
        scratch=[VMEM((PART_FAST, 3, SPAN, hidden), BF16), VMEM((PART_FAST * 3, hidden), F32)],
        smem=1, flops=6 * group_rows * PART_WIDTH * hidden, limit=40,
    )
    blocks = call(
        functools.partial(far_kernel, block, first_goal),
        [jax.ShapeDtypeStruct((tok_dev, PART_WIDTH), BF16)] * PARTS,
        [place, query_seq, ids, near_mixed, stats, fast_out, kv_far],
        scratch=[VMEM((count, block, group_rows), F32), VMEM((group_rows, PART_WIDTH), BF16)],
        smem=1, flops=3 * group_rows * group_rows * PART_WIDTH, limit=24,
    )

    parts = []
    for j in range(PARTS):
        parts.append(permute(blocks[j], lambda z, y, x, c, j=j: (z, c, x ^ j % 2, y ^ j // 2)))

    (out,) = call(
        norm_kernel,
        [jax.ShapeDtypeStruct((tok_dev, WIDTH), BF16)],
        [place] + parts + [norm_gain.reshape(1, WIDTH)],
        scratch=[VMEM((PARTS, tok_dev, PART_WIDTH), BF16)],
        smem=1, flops=6 * tok_dev * WIDTH,
    )
    return out


def solution(mesh):
    rows = P(("groups", "tok"), None)
    return jax.shard_map(
        shards,
        mesh=mesh,
        in_specs=(rows, rows, rows, rows, P("groups"), P("groups"), P(), P()),
        out_specs=rows,
        check_vma=False,
    )
```

```python
import functools
import math

import jax
import jax.numpy as jnp
from jax import lax
from jax.experimental import pallas as pl
from jax.experimental.pallas import tpu as pltpu
from jax.sharding import PartitionSpec as P


HEADS = 8
HEAD_DIM = 320
ATT_DIM = 128
WINDOW = 1024
WIDTH = 2560
ATT_HEADS = 20
LANES = 128
EPS = 1e-06

PARTS = math.gcd(HEADS, ATT_HEADS)
PART_WIDTH = WIDTH // PARTS
PART_FAST = HEADS // PARTS
PART_ATT = ATT_HEADS // PARTS
SPAN = -(-HEAD_DIM // LANES) * LANES


VMEM_BYTES = 67043328

F32 = jnp.float32
BF16 = jnp.bfloat16
VMEM = pltpu.VMEM


def iota(shape, dim):
    return lax.broadcasted_iota(jnp.int32, shape, dim)


def dot(a, b, dims=((1,), (0,))):
    return lax.dot_general(a, b, (dims, ((), ())), preferred_element_type=F32)


def column_of(row):
    n = row.shape[1]
    square = jnp.broadcast_to(row.astype(F32), (n, n))
    diagonal = iota((n, n), 0) == iota((n, n), 1)
    return jnp.sum(jnp.where(diagonal, square, 0.0), axis=1, keepdims=True)


def call(kernel, outs, ins, scratch=(), smem=0, flops=0, grid=None, in_specs=None, out_specs=None, limit=60):
    specs = [pl.BlockSpec(memory_space=pltpu.SMEM)] * smem
    specs += in_specs or [pl.BlockSpec(memory_space=VMEM)] * (len(ins) - smem)
    moved = sum(x.size * x.dtype.itemsize for x in list(ins) + list(outs))
    extra = {} if grid is None else {"grid": grid}
    return pl.pallas_call(
        kernel,
        out_shape=list(outs),
        in_specs=specs,
        out_specs=out_specs or [pl.BlockSpec(memory_space=VMEM)] * len(outs),
        scratch_shapes=list(scratch),
        compiler_params=pltpu.CompilerParams(vmem_limit_bytes=min(limit << 20, VMEM_BYTES)),
        cost_estimate=pl.CostEstimate(flops=flops, bytes_accessed=moved, transcendentals=0),
        **extra,
    )(*ins)


def window_of(head):
    begin = min(head * HEAD_DIM // LANES * LANES, PART_WIDTH - SPAN)
    return begin, head * HEAD_DIM - begin


def front_kernel(group_shift, slots, place_ref, order_ref, rate_ref, query_ref, key_ref, value_ref, *refs):
    out_ref, head_refs, choose_buf = refs[0], refs[1:-1], refs[-1]
    n, _ = key_ref.shape
    planes, together, cores = out_ref.shape[:3]
    step, part, core = pl.program_id(0), place_ref[1], place_ref[2]

    @pl.when(step == 0)
    def _():
        pos = order_ref[pl.ds(place_ref[0], 1), :]
        group = lax.shift_right_logical(pos, group_shift)
        group_col = column_of(group).astype(jnp.int32)
        earlier = (group_col == group) & (iota((n, n), 0) < iota((n, n), 1))
        rank = jnp.sum(jnp.where(earlier, 1.0, 0.0), axis=0, keepdims=True)
        slot = group * slots + rank.astype(jnp.int32)
        choose_buf[...] = jnp.where(iota((n, n), 0) == slot, 1.0, 0.0).astype(BF16)

    choose = choose_buf[...]
    for index, ref in enumerate((key_ref, value_ref, query_ref)):
        lanes = slice(index * PART_WIDTH, (index + 1) * PART_WIDTH)
        for local in range(together):
            rows = dot(choose, ref[:, local * PART_WIDTH : (local + 1) * PART_WIDTH]).astype(BF16)
            for plane in range(planes):
                for at in range(cores):
                    first = (plane * cores + at) * slots
                    out_ref[plane, local, at, :, lanes] = rows[first : first + slots]

    lane = iota((n, SPAN), 1)
    tail = PART_WIDTH - SPAN
    for local in range(together):
        target_part = step * together + local
        rows = []
        for head in range(PART_FAST):
            begin, offset = window_of(head)
            span = slice(local * PART_WIDTH + begin, local * PART_WIDTH + begin + SPAN)
            rate = column_of(rate_ref[pl.ds(target_part * PART_FAST + head, 1), :])
            keys = key_ref[:, span].astype(F32)
            targets = value_ref[:, span].astype(F32) * rate
            turn = SPAN - HEAD_DIM
            if offset:
                keys = pltpu.roll(keys, SPAN - offset, 1)
            if offset != turn:
                targets = pltpu.roll(targets, turn - offset, 1)
            rows.append((keys.astype(BF16), targets.astype(BF16)))
        for flip in range(PART_FAST):
            keys, targets = (jnp.where(core == flip, one, two) for one, two in zip(*rows))
            middle = jnp.where(iota((n, LANES), 1) < HEAD_DIM - tail, keys[:, tail:], targets[:, : SPAN - tail])
            for index in range(PARTS):
                @pl.when((target_part ^ part) == index)
                def _():
                    ref = head_refs[index * PART_FAST + flip]
                    ref[:, :tail] = keys[:, :tail]
                    ref[:, tail:SPAN] = middle
                    ref[:, SPAN:] = targets[:, SPAN - tail :]


def arrival_choice(group_shift, slots, orders, group, n):
    sources, rows = orders.shape
    low_shift = group_shift // 2
    mine = lax.shift_right_logical(orders, group_shift) == group
    before = jnp.where(iota((rows, rows), 0) < iota((rows, rows), 1), 1.0, 0.0).astype(BF16)
    rank = dot(jnp.where(mine, 1.0, 0.0).astype(BF16), before)
    within = orders & ((1 << group_shift) - 1)
    digits = (lax.shift_right_logical(within, low_shift).astype(F32), (within & ((1 << low_shift) - 1)).astype(F32))
    spread = jnp.where(iota((sources, n), 1) // slots == iota((sources, n), 0), 1.0, 0.0).astype(BF16)
    keep = iota((slots, n), 1) % slots == iota((slots, n), 0)
    column = iota((sources, slots), 1)
    pos = jnp.zeros((1, n), F32)
    for digit, weight in zip(digits, (float(1 << low_shift), 1.0)):
        table = jnp.zeros((sources, slots), F32)
        for k in range(slots):
            one = jnp.sum(jnp.where(mine & (rank == float(k)), digit, 0.0), axis=1, keepdims=True)
            table = jnp.where(column == k, one, table)
        wide = dot(table.astype(BF16), spread, ((0,), (0,)))
        pos += weight * jnp.sum(jnp.where(keep, wide, 0.0), axis=0, keepdims=True)
    return jnp.where(iota((n, n), 0) == pos.astype(jnp.int32), 1.0, 0.0).astype(BF16)


def choose_kernel(group_shift, slots, place_ref, order_ref, choose_ref):
    choose_ref[...] = arrival_choice(group_shift, slots, order_ref[...], place_ref[3], choose_ref.shape[0])


def place_kernel(choose_ref, in_ref, kv_ref, q_ref):
    choose = choose_ref[...]
    kv_ref[...] = dot(choose, in_ref[:, : 2 * PART_WIDTH]).astype(BF16)
    q_ref[...] = dot(choose, in_ref[:, 2 * PART_WIDTH :]).astype(BF16)


def grads_kernel(chunk, first_start, outs, place_ref, weight_ref, *refs):
    last = outs > 1
    weight_buf, key_buf, target_buf, delta_buf, pr_buf, sums = refs[-6:]
    out_refs, in_refs = refs[-6 - outs : -6], refs[: -6 - outs]
    kv_refs, early_ref = (in_refs[:-1], in_refs[-1]) if last else (in_refs, None)
    block = kv_refs[0].shape[0]
    n = key_buf.shape[0]
    hidden = weight_ref.shape[2]
    first = pl.multiple_of(place_ref[2] * HEAD_DIM, 16)
    spare = SPAN - HEAD_DIM
    for index in range(3):
        lanes = slice(index * hidden, (index + 1) * hidden)
        begin, blank = (0, HEAD_DIM) if index < 2 else (spare, 0)
        weight_buf[begin : begin + HEAD_DIM, lanes] = weight_ref[index, pl.ds(first, HEAD_DIM), :]
        weight_buf[blank : blank + spare, lanes] = jnp.zeros((spare, hidden), BF16)
    for index, ref in enumerate(kv_refs):
        here = pl.ds(index * block, block)
        key_buf[here, :] = ref[:, :SPAN]
        target_buf[here, :] = ref[:, PART_WIDTH - SPAN :]
    for at in range(0, n, chunk):
        here = pl.ds(at, chunk)
        both = dot(key_buf[here, :], weight_buf[:, : 2 * hidden])
        gate, upward = both[:, :hidden], both[:, hidden:]
        backward = dot(target_buf[here, :], weight_buf[:, 2 * hidden :])
        sigmoid = jax.nn.sigmoid(gate)
        active = gate * sigmoid
        pr_buf[here, :] = (active * upward).astype(BF16)
        delta_buf[here, hidden:] = (backward * active).astype(BF16)
        delta_buf[here, :hidden] = (backward * upward * sigmoid * (1.0 + gate * (1.0 - sigmoid))).astype(BF16)
    for left, right, begin, row in ((key_buf, delta_buf, 0, 0), (target_buf, pr_buf, 2 * hidden, spare)):
        lanes = slice(begin, begin + right.shape[1])
        total = dot(left[...], right[...], ((0,), (0,)))[row : row + HEAD_DIM]
        if last:
            sums[:, lanes] = (total + early_ref[:, lanes].astype(F32)).astype(BF16)
        else:
            out_refs[0][:, lanes] = total.astype(BF16)
    if last:
        for index, ref in enumerate(out_refs):
            begin = pl.multiple_of(place_ref[first_start + index], 16)
            ref[...] = sums[pl.ds(begin, ref.shape[0]), :]


FACTOR = ATT_DIM ** (-0.5) * math.log2(math.e)


def reach(before, index, count, block):
    at = pl.multiple_of(jnp.where(before, index, count - 1 - index) * block, block)
    return at, pl.multiple_of(jnp.where(before, at, 0), block), jnp.where(before, -count * block, count * block - at)


def block_ids(ids, index, count, block, turned):
    turn = count - 1 - index
    row = jnp.where(turned, ids[:, turn * block : (turn + 1) * block], ids[:, index * block : (index + 1) * block])
    return column_of(row).astype(jnp.int32)


def mask_of(own, ids, shift):
    gap = iota((own.shape[0], ids.shape[1]), 1) - iota((own.shape[0], ids.shape[1]), 0) + shift
    return jnp.where((gap < WINDOW // 2) & (gap > -(WINDOW // 2)) & (own == ids), 0.0, -1e30)


def head_lanes(head):
    return pl.ds(pl.multiple_of(head * ATT_DIM, ATT_DIM), ATT_DIM), pl.ds(pl.multiple_of(PART_WIDTH + head * ATT_DIM, ATT_DIM), ATT_DIM)


def near_kernel(block, place_ref, query_ref, ids_ref, kv_ref, chip_ref, out_ref, stat_ref, bias, chip_bias):
    n = query_ref.shape[0]
    count = n // block
    core, group = place_ref[2], place_ref[3]
    second = core == 1
    ids = ids_ref[pl.ds(group, 1), :]
    for index in range(count):
        at = index * block
        bias[at : at + block, :] = mask_of(column_of(ids[:, at : at + block]).astype(jnp.int32), ids, -at)
    for index in range(count):
        _, _, shift = reach(second, count - 1 - index, count, block)
        size = (index + 1) * block
        own = block_ids(ids, index, count, block, second)
        other = ids_ref[pl.ds(group + 1 - 2 * core, 1), :]
        other = jnp.where(second, other[:, n - size :], other[:, :size])
        chip_bias[index, :, :size] = mask_of(own, other, shift)
    stat_ref[...] = jnp.zeros_like(stat_ref)
    lane = iota((block, LANES), 1)

    @pl.loop(0, PART_ATT)
    def _(head):
        keys, values = head_lanes(head)
        for index in range(count):
            at, start, _ = reach(second, count - 1 - index, count, block)
            size = (index + 1) * block
            here, there = pl.ds(at, block), pl.ds(start, size)
            query = query_ref[here, keys]
            score = dot(query, kv_ref[:, keys], ((1,), (1,))) + bias[here, :]
            chip = dot(query, chip_ref[there, keys], ((1,), (1,))) + chip_bias[index, :, :size]
            peak = jnp.maximum(jnp.max(score, axis=1, keepdims=True), jnp.max(chip, axis=1, keepdims=True))
            score = jnp.exp2((score - peak) * FACTOR)
            chip = jnp.exp2((chip - peak) * FACTOR)
            total = jnp.sum(score, axis=1, keepdims=True) + jnp.sum(chip, axis=1, keepdims=True)
            out_ref[here, keys] = dot(score.astype(BF16), kv_ref[:, values]) + dot(chip.astype(BF16), chip_ref[there, values])
            stat = jnp.where(lane == 2 * head, peak, stat_ref[here, :])
            stat_ref[here, :] = jnp.where(lane == 2 * head + 1, total, stat)


def far_kernel(block, first_goal, place_ref, query_ref, ids_ref, near_ref, stat_ref, fast_ref, kv_ref, *refs):
    out_refs, (bias, rows_buf) = refs[:-2], refs[-2:]
    n = query_ref.shape[0]
    count = n // block
    core, group = place_ref[2], place_ref[3]
    last = ids_ref.shape[0] - 1
    first = core == 0
    beyond = group - 1 + 2 * core
    exists = (beyond >= 0) & (beyond <= last)
    ids = ids_ref[pl.ds(group, 1), :]
    for index in range(count):
        _, _, shift = reach(first, index, count, block)
        size = n - index * block
        own = block_ids(ids, index, count, block, core == 1)
        other = ids_ref[pl.ds(jnp.clip(beyond, 0, last), 1), :]
        other = jnp.where(first, other[:, n - size :], other[:, :size])
        bias[index, :, :size] = mask_of(own, jnp.where(exists, other, -1), shift)
    lane = iota((block, LANES), 1)

    @pl.loop(0, PART_ATT)
    def _(head):
        keys, values = head_lanes(head)
        for index in range(count):
            at, start, _ = reach(first, index, count, block)
            size = n - index * block
            here, there = pl.ds(at, block), pl.ds(start, size)
            score = dot(query_ref[here, keys], kv_ref[there, keys], ((1,), (1,))) + bias[index, :, :size]
            stat = stat_ref[here, :]
            old_peak = jnp.sum(jnp.where(lane == 2 * head, stat, 0.0), axis=1, keepdims=True)
            old_total = jnp.sum(jnp.where(lane == 2 * head + 1, stat, 0.0), axis=1, keepdims=True)
            peak = jnp.maximum(jnp.max(score, axis=1, keepdims=True), old_peak)
            keep = jnp.exp2((old_peak - peak) * FACTOR)
            score = jnp.exp2((score - peak) * FACTOR)
            total = old_total * keep + jnp.sum(score, axis=1, keepdims=True)
            mixed = near_ref[here, keys] * keep + dot(score.astype(BF16), kv_ref[there, values])
            rows_buf[here, keys] = (mixed / total + fast_ref[here, keys]).astype(BF16)

    rows = out_refs[0].shape[0]
    for index, ref in enumerate(out_refs):
        begin = pl.multiple_of(place_ref[first_goal + index] * rows, rows)
        ref[...] = rows_buf[pl.ds(begin, rows), :]


def apply_kernel(first_rows, place_ref, weight_ref, query_ref, *refs):
    hidden = weight_ref.shape[2]
    out_ref, fresh, scales = refs[-3:]
    count = (len(refs) - 3) // 2
    mine_refs, other_refs = refs[:count], refs[count : 2 * count]
    core = place_ref[2]
    for head in range(PART_FAST):
        _, offset = window_of(head)
        for index in range(3):
            lanes = slice(index * hidden, (index + 1) * hidden)
            anchor = jnp.full((1, hidden), EPS, F32)
            length = jnp.full((1, hidden), EPS, F32)
            for step in range(count):
                piece = mine_refs[step].shape[0]
                at = pl.multiple_of(place_ref[first_rows + step], 16)
                base = weight_ref[index, pl.ds(at + head * HEAD_DIM, piece), :].astype(F32)
                grad = jnp.where(core == head, mine_refs[step][:, lanes], other_refs[step][:, lanes]).astype(F32)
                update = base + grad
                anchor += jnp.sum(base * base, axis=0, keepdims=True)
                length += jnp.sum(update * update, axis=0, keepdims=True)
                fresh[head, index, pl.ds(at + offset, piece), :] = update.astype(BF16)
            scales[head * 3 + index, :] = (jnp.sqrt(anchor) / jnp.sqrt(length))[0]
            if offset:
                fresh[head, index, :offset, :] = jnp.zeros((offset, hidden), BF16)
            if offset + HEAD_DIM < SPAN:
                fresh[head, index, offset + HEAD_DIM :, :] = jnp.zeros((SPAN - offset - HEAD_DIM, hidden), BF16)
    parts = []
    for head in range(PART_FAST):
        begin, _ = window_of(head)
        query = query_ref[:, begin : begin + SPAN]
        scale = [scales[head * 3 + index : head * 3 + index + 1, :] for index in range(3)]
        gate = dot(query, fresh[head, 0]) * scale[0]
        upward = dot(query, fresh[head, 1]) * (scale[1] * scale[2])
        product = (gate * jax.nn.sigmoid(gate) * upward).astype(BF16)
        parts.append((begin, dot(product, fresh[head, 2], ((1,), (1,)))))
    for lane in range(0, PART_WIDTH, LANES):
        inside = [value[:, lane - begin : lane - begin + LANES] for begin, value in parts if begin <= lane < begin + SPAN]
        out_ref[:, lane : lane + LANES] = functools.reduce(jnp.add, inside)


def norm_kernel(place_ref, *refs):
    part_refs, gain_ref, out_ref, buf = refs[:PARTS], refs[PARTS], refs[PARTS + 1], refs[PARTS + 2]
    square = jnp.zeros((out_ref.shape[0], 1), F32)
    for index, ref in enumerate(part_refs):
        rows = ref[...]
        buf[place_ref[4 + index]] = rows
        wide = rows.astype(F32)
        square += jnp.sum(wide * wide, axis=1, keepdims=True)
    factor = lax.rsqrt(square / WIDTH + EPS)
    for part in range(PARTS):
        lanes = slice(part * PART_WIDTH, (part + 1) * PART_WIDTH)
        out_ref[:, lanes] = (buf[part].astype(F32) * factor * gain_ref[:, lanes]).astype(BF16)


def gather_layout(bits, piece, relay):
    layout = [(0, 0, piece)]
    for bit in reversed(range(bits)):
        for mask, begin, size in list(layout):
            cuts = [(begin, size)]
            if mask == 0 and bit == bits - 1 and bits > 1:
                cuts = [(0, relay), (relay, piece - relay)]
            layout += [(mask ^ 1 << bit, first, count) for first, count in cuts]
    return layout


def shards(queries, key_rows, value_rows, learn_rates, frame_order, window_ids, fast_init, norm_gain):
    tok_dev = queries.shape[0]
    hidden = fast_init.shape[0]
    sections = lax.axis_size("tok")
    plane_size = PARTS * PART_FAST
    planes = sections // plane_size
    group_rows = tok_dev * PARTS
    groups = planes * PART_FAST
    slots = tok_dev // groups
    half = WINDOW // 2
    assert PART_FAST == 2 and half == group_rows and group_rows & (group_rows - 1) == 0
    group_shift = group_rows.bit_length() - 1

    rank = lax.axis_index("tok")
    plane = rank // plane_size
    part = rank // PART_FAST % PARTS
    core = rank % PART_FAST
    row, column = part // 2, part % 2
    group = plane * PART_FAST + core

    def at(plane, row, column, core):
        return plane * plane_size + (row * 2 + column) * PART_FAST + core

    everyone = [(z, y, x, c) for z in range(planes) for y in range(2) for x in range(2) for c in range(2)]

    def permute(array, target):
        route = []
        for source in everyone:
            goal = target(*source)
            if goal is not None:
                route.append((at(*source), at(*goal)))
        return lax.ppermute(array, "tok", route)

    sources = [2 * (core ^ j // 2) + (column ^ j % 2) for j in range(PARTS)]
    bits = planes.bit_length() - 1
    piece = HEAD_DIM >> bits
    assert planes == 1 << bits and piece << bits == HEAD_DIM and piece % 16 == 0

    def owned(plane):
        return sum((plane >> bit & 1) * (HEAD_DIM >> bit + 1) for bit in range(bits))

    relay = -(-piece // 32) * 16
    layout = gather_layout(bits, piece, relay)
    starts = [owned(plane ^ mask) for mask in range(planes)]
    rows_from = [starts[mask] + begin for mask, begin, _ in layout]
    goals = [2 * (column ^ j % 2) + (row ^ j // 2) for j in range(PARTS)]
    first_start = 4 + PARTS
    first_goal = first_start + planes
    first_rows = first_goal + PARTS
    place = jnp.stack([rank, part, core, group] + sources + starts + goals + rows_from).astype(jnp.int32)

    def weight_part():
        own = lax.dynamic_slice_in_dim(fast_init, part * PART_WIDTH, PART_WIDTH, 2)
        return jnp.transpose(own, (1, 2, 0))

    weights = weight_part()

    full = lambda a: pl.BlockSpec(a.shape, lambda h: (0,) * a.ndim)
    steps = 2
    together = PARTS // steps
    orders = frame_order.reshape(sections, tok_dev)
    rates = learn_rates.T
    cut = pl.BlockSpec((tok_dev, WIDTH // steps), lambda h: (0, h))
    head_shape = jax.ShapeDtypeStruct((tok_dev, 2 * HEAD_DIM), BF16)
    packed, *heads_out = call(
        functools.partial(front_kernel, group_shift, slots),
        [jax.ShapeDtypeStruct((planes, PARTS, PART_FAST, slots, 3 * PART_WIDTH), BF16)] + [head_shape] * plane_size,
        [place, orders, rates, queries, key_rows, value_rows],
        in_specs=[full(orders), full(rates), cut, cut, cut],
        out_specs=[pl.BlockSpec((planes, together, PART_FAST, slots, 3 * PART_WIDTH), lambda h: (0, h, 0, 0, 0))]
        + [full(head_shape)] * plane_size,
        grid=(steps,),
        scratch=[VMEM((tok_dev, tok_dev), BF16)],
        smem=1, flops=2 * tok_dev * tok_dev * 3 * WIDTH,
    )
    heads_in = [heads_out[0]]
    send_order = [2, 4, 3, 5, 6, 7, 1]
    for j in range(1, plane_size):
        heads_in.append(permute(heads_out[j], lambda z, y, x, c, j=j: (z, y ^ j >> 2, x ^ j >> 1 & 1, c ^ j & 1)))

    arrived = lax.all_to_all(
        packed.reshape(sections, slots, 3 * PART_WIDTH), "tok", split_axis=0, concat_axis=0, tiled=True
    ).reshape(group_rows, 3 * PART_WIDTH)

    (choose,) = call(
        functools.partial(choose_kernel, group_shift, slots),
        [jax.ShapeDtypeStruct((group_rows, group_rows), BF16)],
        [place, orders], smem=1, flops=2 * group_rows * group_rows,
    )
    kv_seq, query_seq = call(
        place_kernel,
        [jax.ShapeDtypeStruct((group_rows, width), BF16) for width in (2 * PART_WIDTH, PART_WIDTH)],
        [choose, arrived], flops=2 * group_rows * group_rows * 3 * PART_WIDTH,
    )

    swap = lambda z, y, x, c: (z, y, x, 1 - c)

    def beyond(z, y, x, c):
        goal = z + 2 * c - 1
        return (goal, y, x, 1 - c) if 0 <= goal < planes else None

    kv_chip = permute(kv_seq, swap)
    kv_far = permute(kv_seq, beyond)

    near = plane_size // 2
    tokens = near * tok_dev
    by_arrival = [heads_in[0]] + [heads_in[j] for j in send_order]
    early_heads, late_heads = by_arrival[:near], by_arrival[near:]
    grad_scratch = [VMEM((SPAN, 3 * hidden), BF16)] + [VMEM((tokens, SPAN), BF16)] * 2
    grad_scratch += [VMEM((tokens, 2 * hidden), BF16), VMEM((tokens, hidden), BF16), VMEM((HEAD_DIM, 3 * hidden), BF16)]
    grad_flops = 12 * tokens * HEAD_DIM * hidden
    (early,) = call(
        functools.partial(grads_kernel, tokens, first_start, 1),
        [jax.ShapeDtypeStruct((HEAD_DIM, 3 * hidden), BF16)], [place, weights] + early_heads,
        scratch=grad_scratch, smem=1, flops=grad_flops,
    )
    quarters = call(
        functools.partial(grads_kernel, tokens, first_start, planes),
        [jax.ShapeDtypeStruct((piece, 3 * hidden), BF16)] * planes,
        [place, weights] + late_heads + [early],
        scratch=grad_scratch, smem=1, flops=grad_flops,
    )

    def across(bit):
        return lambda z, y, x, c: (z ^ 1 << bit, y, x, c)

    def added(first, second):
        return (first.astype(F32) + second.astype(F32)).astype(BF16)

    held = dict(enumerate(quarters))
    for bit in range(bits):
        flip = 1 << bit
        for mask in sorted([mask for mask in held if mask & flip], reverse=True):
            came = permute(held.pop(mask), across(bit))
            kept = held[mask ^ flip]
            held[mask ^ flip] = added(kept, came)
    total = held[0]
    pieces = [total]
    sent = {(0, 0, piece): total}
    for mask, begin, size in layout[1:]:
        bit = [bit for bit in range(bits) if mask >> bit & 1][0]
        source = (mask ^ 1 << bit, begin, size)
        if source not in sent:
            sent[source] = added(kept[begin : begin + size], came[begin : begin + size])
        sent[mask, begin, size] = permute(sent[source], across(bit))
        pieces.append(sent[mask, begin, size])
    pieces_other = []
    for held_piece in pieces:
        pieces_other.append(permute(held_piece, swap))

    block = min(LANES, group_rows)
    count = group_rows // block
    ids = window_ids.reshape(groups, group_rows)
    wide = jax.ShapeDtypeStruct((group_rows, PART_WIDTH), F32)
    assert 2 * PART_ATT <= LANES
    near_mixed, stats = call(
        functools.partial(near_kernel, block),
        [wide, jax.ShapeDtypeStruct((group_rows, LANES), F32)],
        [place, query_seq, ids, kv_seq, kv_chip],
        scratch=[VMEM((group_rows, group_rows), F32), VMEM((count, block, group_rows), F32)],
        smem=1, flops=6 * group_rows * group_rows * PART_WIDTH, limit=24,
    )
    (fast_out,) = call(
        functools.partial(apply_kernel, first_rows),
        [wide],
        [place, weights, query_seq] + pieces + pieces_other,
        scratch=[VMEM((PART_FAST, 3, SPAN, hidden), BF16), VMEM((PART_FAST * 3, hidden), F32)],
        smem=1, flops=6 * group_rows * PART_WIDTH * hidden, limit=40,
    )
    blocks = call(
        functools.partial(far_kernel, block, first_goal),
        [jax.ShapeDtypeStruct((tok_dev, PART_WIDTH), BF16)] * PARTS,
        [place, query_seq, ids, near_mixed, stats, fast_out, kv_far],
        scratch=[VMEM((count, block, group_rows), F32), VMEM((group_rows, PART_WIDTH), BF16)],
        smem=1, flops=3 * group_rows * group_rows * PART_WIDTH, limit=24,
    )

    parts = []
    for j in range(PARTS):
        parts.append(permute(blocks[j], lambda z, y, x, c, j=j: (z, c, x ^ j % 2, y ^ j // 2)))

    (out,) = call(
        norm_kernel,
        [jax.ShapeDtypeStruct((tok_dev, WIDTH), BF16)],
        [place] + parts + [norm_gain.reshape(1, WIDTH)],
        scratch=[VMEM((PARTS, tok_dev, PART_WIDTH), BF16)],
        smem=1, flops=6 * tok_dev * WIDTH,
    )
    return out


def solution(mesh):
    rows = P(("groups", "tok"), None)
    return jax.shard_map(
        shards,
        mesh=mesh,
        in_specs=(rows, rows, rows, rows, P("groups"), P("groups"), P(), P()),
        out_specs=rows,
        check_vma=False,
    )
```
